32 devices in a mesh: fsdp: 4 (over z), ctx: 2 (over x), tp: 4 (over y, core).
Axes of the slice: x: 2, y: 2, z: 4, core: 2. Of those that a mesh axis runs over, the one named last changes fastest.
Arguments:
- tokens: bfloat16 [4, 2048, 2048], P('fsdp', 'ctx'), may hold values from -6 to 6
- segments: int32 [4, 2048], P('fsdp'), may hold values from 0 to 7, never falling along the last dimension, each value on 1 to 1024 neighbouring positions
- cotangent: bfloat16 [4, 2048, 2048], P('fsdp', 'ctx'), may hold values from -6 to 6
- gain_mix: float32 [2048], replicated, may hold values from 0.5 to 1.5
- w_branch: bfloat16 [2048, 2560], P('fsdp', 'tp'), may hold values from -0.125 to 0.125
- w_input: bfloat16 [2048, 2560], P('fsdp', 'tp'), may hold values from -0.125 to 0.125
- conv_weight: float32 [4, 2560], P(None, 'tp'), may hold values from -3 to 3
- conv_bias: float32 [2560], P('tp'), may hold values from -1.75 to 1.75
- gate_a: bfloat16 [16, 160, 160], P('tp'), may hold values from -0.5 to 0.5
- bias_a: float32 [2560], P('tp'), may hold values from -3 to 3
- gate_x: bfloat16 [16, 160, 160], P('tp'), may hold values from -0.5 to 0.5
- bias_x: float32 [2560], P('tp'), may hold values from -3 to 3
- decay_param: float32 [2560], P('tp'), may hold values from 4 to 8
- w_out: bfloat16 [2560, 2048], P('tp', 'fsdp'), may hold values from -0.3125 to 0.3125
- gain_mlp: float32 [2048], replicated, may hold values from 0.5 to 1.5
- w_gate: bfloat16 [2048, 6144], P('fsdp', 'tp'), may hold values from -0.125 to 0.125
- w_up: bfloat16 [2048, 6144], P('fsdp', 'tp'), may hold values from -0.125 to 0.125
- w_down: bfloat16 [6144, 2048], P('tp', 'fsdp'), may hold values from -0.15625 to 0.15625
Outputs:
- output: bfloat16 [4, 2048, 2048], P('fsdp', 'ctx')
- grad_tokens: bfloat16 [4, 2048, 2048], P('fsdp', 'ctx')
- grad_gain_mix: float32 [2048], replicated
- grad_w_branch: float32 [2048, 2560], P('fsdp', 'tp')
- grad_w_input: float32 [2048, 2560], P('fsdp', 'tp')
- grad_conv_weight: float32 [4, 2560], P(None, 'tp')
- grad_conv_bias: float32 [2560], P('tp')
- grad_gate_a: float32 [16, 160, 160], P('tp')
- grad_bias_a: float32 [2560], P('tp')
- grad_gate_x: float32 [16, 160, 160], P('tp')
- grad_bias_x: float32 [2560], P('tp')
- grad_decay_param: float32 [2560], P('tp')
- grad_w_out: float32 [2560, 2048], P('tp', 'fsdp')
- grad_gain_mlp: float32 [2048], replicated
- grad_w_gate: float32 [2048, 6144], P('fsdp', 'tp')
- grad_w_up: float32 [2048, 6144], P('fsdp', 'tp')
- grad_w_down: float32 [6144, 2048], P('tp', 'fsdp')
The draws below stay inside these ranges and needn't reach their ends.
Inputs may be any that keep to these rules, and one draw needn't show every extreme that they name: `segments`: within a sequence the document numbers never fall; every document has 1 to 1024 positions and one has exactly 1024.
All inputs are finite; a program needn't handle non-finite values.
Results may differ from the reference program's by a relative error of at most 0.012.
Values may be sent and summed in bfloat16 or wider, within the bound.
A program may use at most 256 MiB of HBM per device.

```python
import math
import jax
import jax.numpy as jnp
import numpy as np
from jax import lax

D = 2048
R = 2560
FF = 6144
BW = 160
KW = 4
HEADS = 16
SEQS = 4
LENGTH = 2048
DOCS = 8
DOC_MOST = 1024


def block_levels(stream_key, extent, shards, least, largest):
    def one(axis_at, parts):
        draws = jax.random.uniform(jax.random.fold_in(jax.random.fold_in(stream_key, 6), axis_at), (parts,), jnp.float32, least / len(shards), largest / len(shards))
        return jnp.repeat(jnp.exp(draws), extent[axis_at] // parts).reshape((-1,) + (1,) * (len(extent) - axis_at - 1))

    factor_of = one(*shards[0])
    for cut in shards[1:]:
        factor_of = factor_of * one(*cut)
    return factor_of


def length_profile(number_of, total, most, slope):
    portions = [(1 << 20) // math.isqrt(rank ** slope) + 1 for rank in range(2, number_of + 1)]
    rest, counts = total - most - (number_of - 1), [1] * (number_of - 1)
    while rest > 0:
        candidates = [i for i in range(number_of - 1) if counts[i] < most]
        mass, remaining = sum([portions[i] for i in candidates]), rest
        for i in candidates:
            extra = min(most - counts[i], max(1, remaining * portions[i] // mass), rest)
            counts[i] = counts[i] + extra
            rest = rest - extra
    return np.array([most] + counts)


def uneven(rng, amount, total, most, skew):
    if amount == 2:
        one = jax.random.randint(rng, (), max(1, total - most), min(most, total - 1) + 1)
        return jnp.stack([one, total - one])
    sizes = jnp.asarray(length_profile(amount, total, most, skew), jnp.int32)
    pairs = (amount - 1) // 2
    giver, taker = sizes[1:1 + 2 * pairs:2], sizes[2:2 + 2 * pairs:2]
    room = jnp.minimum(giver - 1, most - taker)
    moved = jax.random.randint(jax.random.fold_in(rng, 1), (pairs,), 0, 1 << 20) % (room + 1)
    sizes = sizes.at[1:1 + 2 * pairs:2].set(giver - moved).at[2:2 + 2 * pairs:2].set(taker + moved)
    return sizes[jax.random.permutation(jax.random.fold_in(rng, 2), amount)]


def noise(rng, extent, deviation, most, pieces=(), kind=jnp.bfloat16):
    drawn = jax.random.normal(rng, extent, jnp.float32) * deviation
    if len(pieces) > 0:
        drawn = block_levels(rng, extent, pieces, -0.22, 0.18) * drawn
    return jnp.clip(drawn, min=-most, max=most).astype(kind)


def setup_inputs(seed: int = 0) -> dict:
    key_of = jax.random.split(jax.random.key(seed), 19)
    return {
        "tokens": noise(key_of[0], (SEQS, LENGTH, D), 1.0, 6.0, ((0, 4), (1, 2))),
        "segments": jax.vmap(lambda own: jnp.searchsorted(jnp.cumsum(uneven(own, DOCS, LENGTH, DOC_MOST, 2)), jnp.arange(LENGTH), side="right"))(jax.random.split(key_of[1], SEQS)).reshape((SEQS, LENGTH)).astype(jnp.int32),
        "cotangent": noise(key_of[2], (SEQS, LENGTH, D), 1.0, 6.0, ((0, 4), (1, 2))),
        "gain_mix": jnp.clip(1.0 + 0.1 * jax.random.normal(key_of[3], (D,), jnp.float32), 0.5, 1.5),
        "w_branch": noise(key_of[4], (D, R), D ** -0.5, 0.125, ((0, 4), (1, 4))),
        "w_input": noise(key_of[5], (D, R), D ** -0.5, 0.125, ((0, 4), (1, 4))),
        "conv_weight": noise(key_of[6], (KW, R), 0.5, 3.0, ((1, 4),), jnp.float32),
        "conv_bias": noise(key_of[7], (R,), 0.3, 1.75, ((0, 4),), jnp.float32),
        "gate_a": noise(key_of[8], (HEADS, BW, BW), BW ** -0.5, 0.5, ((0, 4),)),
        "bias_a": noise(key_of[9], (R,), 0.5, 3.0, ((0, 4),), jnp.float32),
        "gate_x": noise(key_of[10], (HEADS, BW, BW), BW ** -0.5, 0.5, ((0, 4),)),
        "bias_x": noise(key_of[11], (R,), 0.5, 3.0, ((0, 4),), jnp.float32),
        "decay_param": jnp.clip(4.0 + 4.0 * jax.random.uniform(key_of[12], (R,), jnp.float32) ** block_levels(key_of[12], (R,), ((0, 4),), -0.2, 0.2), 4.0, 8.0),
        "w_out": noise(key_of[13], (R, D), (R // 8) ** -0.5, 0.3125, ((0, 4), (1, 4))),
        "gain_mlp": jnp.clip(1.0 + 0.1 * jax.random.normal(key_of[14], (D,), jnp.float32), 0.5, 1.5),
        "w_gate": noise(key_of[15], (D, FF), D ** -0.5, 0.125, ((0, 4), (1, 4))),
        "w_up": noise(key_of[16], (D, FF), D ** -0.5, 0.125, ((0, 4), (1, 4))),
        "w_down": noise(key_of[17], (FF, D), (FF // 4) ** -0.5, 0.15625, ((0, 4), (1, 4))),
    }


EPSILON = 1e-06
RATE_SCALE = 8.0
HIGHEST = lax.Precision.HIGHEST

@jax.custom_vjp
def low(v):
    return lax.optimization_barrier(v.astype(jnp.bfloat16)).astype(jnp.float32)

@jax.custom_vjp
def low_back(v):
    return v

def low_keep(v):
    return (low(v), None)

def low_pass(kept, grad):
    return (grad,)

def back_keep(v):
    return (v, None)

def back_low(kept, grad):
    return (low(grad),)
low.defvjp(low_keep, low_pass)
low_back.defvjp(back_keep, back_low)

def matmul(left, right):
    return jnp.dot(left, right, precision=HIGHEST)

def blocked(values, blocks):
    row_count = values.shape[0]
    heads_in = values.reshape(row_count, HEADS, BW)
    return jnp.einsum('thi,hij->thj', heads_in, blocks, precision=HIGHEST).reshape(row_count, R)

def gelu_tanh(values):
    return jax.nn.gelu(values, approximate=True)

def rms_scale(values):
    return lax.rsqrt(lax.optimization_barrier(jnp.mean(values * values, axis=-1, keepdims=True)) + EPSILON)

def layer(inputs, seg_row, weights_all):
    gain_mix, w_branch, w_input, conv_weight, conv_bias, gate_a, bias_a, gate_x, bias_x, decay_param, w_out, gain_mlp, w_gate, w_up, w_down = weights_all
    row_count = inputs.shape[0]
    normed = low(inputs * rms_scale(inputs) * gain_mix)
    branch_pre = low_back(matmul(normed, w_branch))
    branch = gelu_tanh(branch_pre)
    conv_in = low(low_back(matmul(normed, w_input)))
    conv_sum = jnp.zeros_like(conv_in) + conv_bias
    doc_start = jnp.zeros((row_count,), dtype=bool)
    for offset in range(KW):
        if offset == 0:
            shifted, shifted_seg = (conv_in, seg_row)
        else:
            shifted = jnp.concatenate([jnp.zeros((offset, R), jnp.float32), conv_in[:row_count - offset]], axis=0)
            shifted_seg = jnp.concatenate([jnp.full((offset,), -1, jnp.int32), seg_row[:row_count - offset]], axis=0)
        same_doc = shifted_seg == seg_row
        if offset == 1:
            doc_start = jnp.logical_not(same_doc)
        conv_sum = conv_sum + conv_weight[offset] * jnp.where(same_doc[:, None], shifted, 0.0)
    conv_out = low(conv_sum)
    pre_a = low_back(blocked(conv_out, gate_a) + bias_a)
    pre_x = low_back(blocked(conv_out, gate_x) + bias_x)
    recur_gate = jax.nn.sigmoid(pre_a)
    input_gate = jax.nn.sigmoid(pre_x)
    log_decay = -RATE_SCALE * jax.nn.softplus(-decay_param) * recur_gate
    starts = doc_start[:, None]
    multiplier = jnp.where(starts, 1.0, jnp.sqrt(-jnp.expm1(2.0 * log_decay)))
    carry_factor = jnp.where(starts, 0.0, jnp.exp(log_decay))
    driven = input_gate * conv_out * multiplier

    def advance(carried, inputs_t):
        factor, driven_t = inputs_t
        carried = factor * carried + driven_t
        return (carried, carried)
    last_state, states = lax.scan(jax.checkpoint(advance), jnp.zeros((R,), jnp.float32), (carry_factor, driven))
    mixed_out = low(states * branch)
    residual = inputs + low_back(matmul(mixed_out, w_out))
    normed_mlp = low(residual * rms_scale(residual) * gain_mlp)
    gate_pre = low_back(matmul(normed_mlp, w_gate))
    up_pre = low_back(matmul(normed_mlp, w_up))
    hidden = low(gelu_tanh(gate_pre) * up_pre)
    return residual + low_back(matmul(hidden, w_down))

def reference(tokens, segments, cotangent, gain_mix, w_branch, w_input, conv_weight, conv_bias, gate_a, bias_a, gate_x, bias_x, decay_param, w_out, gain_mlp, w_gate, w_up, w_down):
    weights_all = tuple((value.astype(jnp.float32) for value in (gain_mix, w_branch, w_input, conv_weight, conv_bias, gate_a, bias_a, gate_x, bias_x, decay_param, w_out, gain_mlp, w_gate, w_up, w_down)))

    def one_sequence(totals, sequence_item):
        seq_tokens, seq_segments, seq_cot = sequence_item

        def forward(inputs, weights_in):
            return layer(inputs, seq_segments, weights_in)
        result, pull_back = jax.vjp(forward, seq_tokens.astype(jnp.float32), weights_all)
        grad_in, grad_weights = pull_back(seq_cot.astype(jnp.float32))
        totals = jax.tree.map(jnp.add, totals, grad_weights)
        return (totals, (result.astype(jnp.bfloat16), grad_in.astype(jnp.bfloat16)))
    zero_grads = jax.tree.map(jnp.zeros_like, weights_all)
    grad_totals, (output, grad_tokens) = lax.scan(one_sequence, zero_grads, (tokens, segments, cotangent))
    grad_gain_mix, grad_w_branch, grad_w_input, grad_conv_weight, grad_conv_bias, grad_gate_a, grad_bias_a, grad_gate_x, grad_bias_x, grad_decay_param, grad_w_out, grad_gain_mlp, grad_w_gate, grad_w_up, grad_w_down = grad_totals
    return (output, grad_tokens, grad_gain_mix, grad_w_branch, grad_w_input, grad_conv_weight, grad_conv_bias, grad_gate_a, grad_bias_a, grad_gate_x, grad_bias_x, grad_decay_param, grad_w_out, grad_gain_mlp, grad_w_gate, grad_w_up, grad_w_down)
```

```python
import functools

import jax
import jax.numpy as jnp
import numpy as np
from jax import lax
from jax.experimental import pallas as pl
from jax.experimental.pallas import tpu as pltpu
from jax.sharding import PartitionSpec as P

EPSILON = 1e-06
RATE_SCALE = 8.0
GELU_C = 0.7978845608028654
GELU_K = 0.044715
GROUP = ("ctx", "tp")
F32, BF16 = jnp.float32, jnp.bfloat16


def matmul(left, right):
    return jnp.dot(left, right, preferred_element_type=F32)


def left_inner(left, right):
    return lax.dot_general(left, right, (((0,), (0,)), ((), ())), preferred_element_type=F32)


def right_inner(left, right):
    return lax.dot_general(left, right, (((1,), (1,)), ((), ())), preferred_element_type=F32)


def gelu_parts(v):
    t = jnp.tanh(GELU_C * (v + GELU_K * (v * v * v)))
    half = 0.5 * (1.0 + t)
    slope = half + 0.5 * v * (1.0 - t * t) * (GELU_C * (1.0 + 3.0 * GELU_K * v * v))
    return v * half, slope


def gelu(v):
    return 0.5 * v * (1.0 + jnp.tanh(GELU_C * (v + GELU_K * (v * v * v))))


def one_minus_exp(u):
    series = 1.0 - u * (1.0 / 8.0)
    for n in (7.0, 6.0, 5.0, 4.0, 3.0, 2.0):
        series = 1.0 - u * (1.0 / n) * series
    return jnp.where(u < 0.5, u * series, 1.0 - jnp.exp(-u))


def rms_rows(values):
    return lax.rsqrt(jnp.mean(values * values, axis=-1, keepdims=True) + EPSILON)


def norm_back(grad_norm, scaled, scale_row, gain):
    grad_scaled = grad_norm * gain
    return scale_row * (
        grad_scaled - scaled * jnp.mean(grad_scaled * scaled, axis=-1, keepdims=True)
    )


def step_mask(kind, g):
    core = g % 2
    if kind == "core":
        return 1
    return 2 if (kind == "near") == (core == 0) else 4


def exchange(block, kind):
    pairs = [(g, g ^ step_mask(kind, g)) for g in range(8)]
    return lax.ppermute(block, GROUP, pairs)


def flip(block, mask):
    return lax.ppermute(block, GROUP, [(g, g ^ mask) for g in range(8)])


def place_table():
    table = np.zeros((8, 8), np.int32)
    for g in range(8):
        for spot in range(8):
            at = g ^ (spot >> 2)
            block = at
            if spot & 1:
                block ^= step_mask("near", at)
            if spot & 2:
                block ^= step_mask("far", at)
            table[g, block] = spot
    return table


def gather_rows(rows):
    for kind in ("near", "far", "core"):
        rows = jnp.concatenate([rows, exchange(rows, kind)], axis=0)
    return rows


def reduce_rows(left, right, product):
    half = left.shape[0] // 2
    sent = product(left[half:], right).astype(BF16)
    kept = product(left[:half], right)
    got = exchange(sent, "core")
    kept, got = lax.optimization_barrier((kept, got))
    total = kept + got.astype(F32)
    for kind in ("far", "near"):
        half = half // 2
        got = exchange(total[half:].astype(BF16), kind)
        total = total[:half] + got.astype(F32)
    return total


def whole_rows(rows):
    count = rows.shape[0]
    rows = jnp.concatenate([rows, flip(rows, 2)], axis=0)
    rows = jnp.concatenate([rows, flip(rows, 1)], axis=0)
    place = lax.axis_index("tp")
    blocks = []
    for b in range(4):
        away = jnp.bitwise_xor(place, b)
        spot = (away % 2) * 2 + away // 2
        blocks.append(lax.dynamic_slice_in_dim(rows, spot * count, count, 0))
    return jnp.concatenate(blocks, axis=0)


def sum_fsdp(x):
    size = lax.axis_size("fsdp")
    bit = 1
    while bit < size:
        x = x + lax.ppermute(x, "fsdp", [(i, i ^ bit) for i in range(size)])
        bit *= 2
    return x


def scan_rows(a_ref, b_ref, carry, reverse):
    rows, width = b_ref.shape
    groups = rows // 8
    a = a_ref[...].reshape(groups, 8, width)
    b = b_ref[...].reshape(groups, 8, width)
    at = lax.broadcasted_iota(jnp.int32, (groups, 8, width), 1)
    for shift in (1, 2, 4):
        ok = (at < 8 - shift) if reverse else (at >= shift)
        turn = 8 - shift if reverse else shift
        b_before = jnp.where(ok, pltpu.roll(b, turn, 1), 0.0)
        a_before = jnp.where(ok, pltpu.roll(a, turn, 1), 1.0)
        b = a * b_before + b
        a = a * a_before
    a_ref[...] = a.reshape(rows, width)
    b_ref[...] = b.reshape(rows, width)
    for k in range(groups):
        k = groups - 1 - k if reverse else k
        part = pl.ds(8 * k, 8)
        now = b_ref[part, :] + a_ref[part, :] * carry
        b_ref[part, :] = now
        carry = now[0:1, :] if reverse else now[7:8, :]
    return carry


def mixer_kernel(
    place, pre, masks, params, gate_a, gate_x, mixed, states, recur_out, input_out, conv_out, ext, a_buf, b_buf, carry
):
    rows, width = states.shape

    @pl.when(pl.program_id(0) == 0)
    def _():
        ext[...] = jnp.zeros_like(ext)
        carry[...] = jnp.zeros_like(carry)

    ext[0:8, :] = ext[rows : rows + 8, :]
    ext[8:, :] = pre[:, width:].astype(BF16).astype(F32)
    conv = params[4:5, :] + params[0:1, :] * ext[8:, :]
    for k in range(1, 4):
        conv = conv + params[k : k + 1, :] * (masks[:, k - 1 : k] * ext[pl.ds(8 - k, rows), :])
    conv_low = conv.astype(BF16)
    conv_out[...] = conv_low
    conv = conv_low.astype(F32)
    recur = jax.nn.sigmoid(matmul(conv_low, gate_a[...]) + params[5:6, :])
    opened = jax.nn.sigmoid(matmul(conv_low, gate_x[...]) + params[6:7, :])
    recur_out[...] = recur
    input_out[...] = opened
    log_decay = params[7:8, :] * recur
    same = masks[:, 0:1]
    root = jnp.sqrt(one_minus_exp(-2.0 * log_decay))
    a_buf[...] = same * jnp.exp(log_decay)
    b_buf[...] = opened * conv * jnp.where(same > 0.5, root, 1.0)
    carry[0:1, :] = scan_rows(a_buf, b_buf, carry[0:1, :], False)
    state = b_buf[...]
    states[...] = state
    mixed[...] = (state * gelu(pre[:, :width])).astype(BF16)


def mixer_back_kernel(
    place, grad_mixed, pre, pre_tail, states, states_tail, recur_in, input_in, conv_in, masks, params, gate_a, gate_x,
    grads, sums, sum_a, sum_x, ext, grad_ext, a_buf, b_buf, carry,
):
    rows, width = states.shape
    step = pl.program_id(0)
    first = step == pl.num_programs(0) - 1

    @pl.when(step == 0)
    def _():
        grad_ext[...] = jnp.zeros_like(grad_ext)
        carry[...] = jnp.zeros_like(carry)
        sums[...] = jnp.zeros_like(sums)
        sum_a[...] = jnp.zeros_like(sum_a)
        sum_x[...] = jnp.zeros_like(sum_x)

    inside = jnp.where(first, 0.0, 1.0)
    branch, slope = gelu_parts(pre[:, :width])
    above = grad_mixed[...]
    state = states[...]
    grads[:, :width] = (above * state * slope).astype(BF16)
    recur, opened = recur_in[...], input_in[...]
    conv_low = conv_in[...]
    conv = conv_low.astype(F32)
    same = masks[:, 0:1]
    rate = params[7:8, :]
    log_decay = rate * recur
    decay = jnp.exp(log_decay)
    root = jnp.sqrt(one_minus_exp(-2.0 * log_decay))
    mult = jnp.where(same > 0.5, root, 1.0)
    a_buf[0:rows, :] = same * decay
    head = a_buf[0:1, :]
    a_buf[rows : rows + 8, :] = jnp.broadcast_to(carry[1:2, :], (8, width))
    factor = a_buf[pl.ds(1, rows), :]
    a_buf[0:rows, :] = factor
    b_buf[...] = above * branch
    new_carry = scan_rows(a_buf.at[pl.ds(0, rows), :], b_buf, carry[0:1, :], True)
    carry[0:1, :] = new_carry
    carry[1:2, :] = head
    total = b_buf[...]
    ext[0:8, :] = inside * states_tail[...]
    ext[8:, :] = state
    before = ext[pl.ds(7, rows), :]
    grad_open = total * opened
    grad_log = jnp.where(
        same > 0.5, total * before * decay - grad_open * conv * decay * decay / root, 0.0
    )

    def fold(x):
        return jnp.sum(x.reshape(rows // 8, 8, width), axis=0)

    sums[0:8, :] += fold(grad_log * recur)
    low_a = (grad_log * rate * recur * (1.0 - recur)).astype(BF16)
    low_x = (total * conv * mult * opened * (1.0 - opened)).astype(BF16)
    sums[8:16, :] += fold(low_a.astype(F32))
    sums[16:24, :] += fold(low_x.astype(F32))
    sum_a[...] += left_inner(conv_low, low_a)
    sum_x[...] += left_inner(conv_low, low_x)
    grad_conv = grad_open * mult + (
        right_inner(low_a, gate_a[...]) + right_inner(low_x, gate_x[...])
    )
    sums[24:32, :] += fold(grad_conv)
    ext[0:8, :] = inside * pre_tail[:, width:].astype(BF16).astype(F32)
    ext[8:, :] = pre[:, width:].astype(BF16).astype(F32)
    grad_ext[rows : rows + 8, :] = grad_ext[0:8, :]
    grad_ext[0:rows, :] = grad_conv
    grad_in = params[0:1, :] * grad_conv
    sums[32:40, :] += fold(grad_conv * ext[8:, :])
    for k in range(1, 4):
        earlier = masks[:, k - 1 : k] * ext[pl.ds(8 - k, rows), :]
        sums[32 + 8 * k : 40 + 8 * k, :] += fold(grad_conv * earlier)
        grad_in = grad_in + params[k : k + 1, :] * (
            masks[:, k + 2 : k + 3] * grad_ext[pl.ds(k, rows), :]
        )
    grads[:, width:] = grad_in.astype(BF16)


def mixer(pre, masks, params, gate_a, gate_x, place, rows):
    count, width = pre.shape[0], pre.shape[1] // 2
    steps = count // rows
    spot = lambda i, place: (place[i], 0)
    inorder = lambda i, place: (i, 0)
    fixed = lambda i, place: (0, 0)
    wide = pl.BlockSpec((rows, 2 * width), spot)
    one = pl.BlockSpec((rows, width), spot)
    gate = pl.BlockSpec((width, width), fixed)
    return pl.pallas_call(
        mixer_kernel,
        grid_spec=pltpu.PrefetchScalarGridSpec(
            num_scalar_prefetch=1,
            grid=(steps,),
            in_specs=[wide, pl.BlockSpec((rows, 8), inorder), pl.BlockSpec((8, width), fixed), gate, gate],
            out_specs=[one] * 5,
            scratch_shapes=[
                pltpu.VMEM((rows + 8, width), F32),
                pltpu.VMEM((rows, width), F32),
                pltpu.VMEM((rows, width), F32),
                pltpu.VMEM((8, width), F32),
            ],
        ),
        out_shape=[
            jax.ShapeDtypeStruct((count, width), kind) for kind in (BF16, F32, F32, F32, BF16)
        ],
        cost_estimate=pl.CostEstimate(
            flops=count * width * (4 * width + 120), bytes_accessed=count * width * 24, transcendentals=count * width * 6
        ),
        name="mixer",
    )(place, pre, masks, params, gate_a, gate_x)


def mixer_back(grad_mixed, pre, states, recur, opened, conv, masks, params, gate_a, gate_x, place, rows):
    count, width = states.shape
    steps = count // rows
    last = steps - 1
    spot = lambda i, place: (place[last - i], 0)
    inorder = lambda i, place: (last - i, 0)
    fixed = lambda i, place: (0, 0)

    def tail(i, place):
        return (place[jnp.maximum(last - i - 1, 0)] * (rows // 8) + rows // 8 - 1, 0)

    wide = pl.BlockSpec((rows, 2 * width), spot)
    one = pl.BlockSpec((rows, width), spot)
    gate = pl.BlockSpec((width, width), fixed)
    return pl.pallas_call(
        mixer_back_kernel,
        grid_spec=pltpu.PrefetchScalarGridSpec(
            num_scalar_prefetch=1,
            grid=(steps,),
            in_specs=[
                one, wide, pl.BlockSpec((8, 2 * width), tail), one, pl.BlockSpec((8, width), tail), one, one, one,
                pl.BlockSpec((rows, 8), inorder), pl.BlockSpec((8, width), fixed), gate, gate,
            ],
            out_specs=[wide, pl.BlockSpec((64, width), fixed), gate, gate],
            scratch_shapes=[
                pltpu.VMEM((rows + 8, width), F32),
                pltpu.VMEM((rows + 8, width), F32),
                pltpu.VMEM((rows + 8, width), F32),
                pltpu.VMEM((rows, width), F32),
                pltpu.VMEM((8, width), F32),
            ],
        ),
        out_shape=[
            jax.ShapeDtypeStruct((count, 2 * width), BF16),
            jax.ShapeDtypeStruct((64, width), F32),
            jax.ShapeDtypeStruct((width, width), F32),
            jax.ShapeDtypeStruct((width, width), F32),
        ],
        cost_estimate=pl.CostEstimate(
            flops=count * width * (8 * width + 200), bytes_accessed=count * width * 34, transcendentals=count * width * 4
        ),
        name="mixer_back",
    )(place, grad_mixed, pre, pre, states, states, recur, opened, conv, masks, params, gate_a, gate_x)


def on_diagonal(blocks):
    heads, size = blocks.shape[0], blocks.shape[1]
    out = jnp.zeros((heads * size, heads * size), blocks.dtype)
    for h in range(heads):
        out = lax.dynamic_update_slice(out, blocks[h], (h * size, h * size))
    return out


def shards(
    tokens, segments, cotangent, gain_mix, w_branch, w_input, conv_weight, conv_bias, gate_a, bias_a, gate_x, bias_x,
    decay_param, w_out, gain_mlp, w_gate, w_up, w_down,
):
    half_at = lax.axis_index("ctx")
    place_tp = lax.axis_index("tp")

    def mine(x, axis):
        size = x.shape[axis] // 2
        return lax.dynamic_slice_in_dim(x, half_at * size, size, axis)

    _, tok_count, model_width = tokens.shape
    rows = tok_count // 4
    length = 2 * tok_count
    own_in = jnp.concatenate([mine(w_branch, 1), mine(w_input, 1)], axis=1)
    full_in = lax.all_gather(own_in, "fsdp", axis=0, tiled=True)
    full_out = lax.all_gather(mine(w_out, 0), "fsdp", axis=1, tiled=True)
    own_gu = jnp.concatenate([mine(w_gate, 1), mine(w_up, 1)], axis=1)
    full_gu = lax.all_gather(own_gu, "fsdp", axis=0, tiled=True)
    full_down = lax.all_gather(mine(w_down, 0), "fsdp", axis=1, tiled=True)

    width = own_in.shape[1] // 2
    units = own_gu.shape[1] // 2
    place = jnp.asarray(place_table())[half_at * 4 + place_tp]

    rate = -RATE_SCALE * jax.nn.softplus(-decay_param)
    params = jnp.concatenate(
        [
            mine(conv_weight, 1),
            jnp.stack([mine(v, 0) for v in (conv_bias, bias_a, bias_x, rate)]),
        ],
        axis=0,
    )
    heads_a, heads_x = mine(gate_a, 0), mine(gate_x, 0)
    head_count, head_width = heads_a.shape[0], heads_a.shape[1]
    diag_a, diag_x = on_diagonal(heads_a), on_diagonal(heads_x)
    seg = segments[0]
    around = jnp.pad(seg, (3, 3), constant_values=-1)
    marks = [around[3 - k : 3 - k + length] == seg for k in (1, 2, 3)]
    marks += [around[3 + k : 3 + k + length] == seg for k in (1, 2, 3)]
    marks += [jnp.zeros_like(marks[0])] * 2
    masks = jnp.stack(marks, axis=1).astype(F32)

    own = lax.dynamic_slice_in_dim(tokens[0], place_tp * rows, rows, 0)
    inputs = own.astype(F32)
    scale_mix = rms_rows(inputs)
    scaled_mix = inputs * scale_mix
    normed = gather_rows((scaled_mix * gain_mix).astype(BF16))
    own_cot = lax.dynamic_slice_in_dim(cotangent[0], place_tp * rows, rows, 0)
    cot = gather_rows(own_cot)

    pre = matmul(normed, full_in)
    mixed, states, recur, opened, conv = mixer(pre, masks, params, diag_a, diag_x, place, rows)
    resid = inputs + reduce_rows(mixed, full_out, matmul)
    scale_mlp = rms_rows(resid)
    scaled_mlp = resid * scale_mlp
    normed_mlp = gather_rows((scaled_mlp * gain_mlp).astype(BF16))

    both = matmul(normed_mlp, full_gu)
    gate_pre, up_pre = both[:, :units], both[:, units:]
    gate_act, gate_slope = gelu_parts(gate_pre)
    hidden = (gate_act * up_pre).astype(BF16)
    grad_w_down = left_inner(hidden, cot).astype(BF16)
    output = (resid + reduce_rows(hidden, full_down, matmul)).astype(BF16)

    grad_hidden = right_inner(cot, full_down)
    grad_both = jnp.concatenate(
        [
            (grad_hidden * up_pre * gate_slope).astype(BF16),
            (grad_hidden * gate_act).astype(BF16),
        ],
        axis=1,
    )
    grad_norm_mlp = reduce_rows(grad_both, full_gu, right_inner)
    grad_w_gu = left_inner(normed_mlp, grad_both).astype(BF16)
    grad_resid = own_cot.astype(F32) + norm_back(grad_norm_mlp, scaled_mlp, scale_mlp, gain_mlp)
    gain_mlp_part = jnp.sum(grad_norm_mlp * scaled_mlp, axis=0)
    grad_proj = gather_rows(grad_resid.astype(BF16))

    grad_w_out = left_inner(mixed, grad_proj).astype(BF16)
    grad_mixed = right_inner(grad_proj, full_out)
    grads_in, sums, sum_a, sum_x = mixer_back(
        grad_mixed, pre, states, recur, opened, conv, masks, params, diag_a, diag_x, place, rows
    )
    grad_w_in = left_inner(normed, grads_in).astype(BF16)
    grad_norm_mix = reduce_rows(grads_in, full_in, right_inner)
    gain_mix_part = jnp.sum(grad_norm_mix * scaled_mix, axis=0)
    grad_tokens = (grad_resid + norm_back(grad_norm_mix, scaled_mix, scale_mix, gain_mix)).astype(BF16)

    def owned(x, axis):
        return lax.psum_scatter(x, "fsdp", scatter_dimension=axis, tiled=True)

    def both_halves(x, axis):
        other = flip(x, 4)
        low = jnp.where(half_at == 0, x, other)
        high = jnp.where(half_at == 0, other, x)
        return jnp.concatenate([low, high], axis=axis).astype(F32)

    own_down = both_halves(owned(grad_w_down, 1), 0)
    sum_gu = owned(grad_w_gu, 0)
    own_gate = both_halves(sum_gu[:, :units], 1)
    own_up = both_halves(sum_gu[:, units:], 1)
    own_out = both_halves(owned(grad_w_out, 1), 0)
    sum_in = owned(grad_w_in, 0)
    own_branch = both_halves(sum_in[:, :width], 1)
    own_input = both_halves(sum_in[:, width:], 1)

    lines = jnp.sum(sums.reshape(8, 8, width), axis=1)
    squares = [
        part[h * head_width : (h + 1) * head_width, h * head_width : (h + 1) * head_width]
        for part in (sum_a, sum_x)
        for h in range(head_count)
    ]
    lines = both_halves(sum_fsdp(lines), 1)
    squares = sum_fsdp(jnp.stack(squares).reshape(2, head_count, head_width, head_width))
    squares = both_halves(squares, 1)
    gains = jnp.stack([gain_mix_part, gain_mlp_part])
    for mask in (1, 2, 4):
        gains = gains + flip(gains, mask)
    gains = sum_fsdp(gains)
    return (
        whole_rows(output)[None],
        whole_rows(grad_tokens)[None],
        gains[0],
        own_branch,
        own_input,
        lines[4:8],
        lines[3],
        squares[0],
        lines[1],
        squares[1],
        lines[2],
        RATE_SCALE * jax.nn.sigmoid(-decay_param) * lines[0],
        own_out,
        gains[1],
        own_gate,
        own_up,
        own_down,
    )


def solution(mesh):
    in_specs = (
        P("fsdp", "ctx", None),
        P("fsdp", None),
        P("fsdp", "ctx", None),
        P(),
        P("fsdp", "tp"),
        P("fsdp", "tp"),
        P(None, "tp"),
        P("tp"),
        P("tp", None, None),
        P("tp"),
        P("tp", None, None),
        P("tp"),
        P("tp"),
        P("tp", "fsdp"),
        P(),
        P("fsdp", "tp"),
        P("fsdp", "tp"),
        P("tp", "fsdp"),
    )
    out_specs = (
        P("fsdp", "ctx", None),
        P("fsdp", "ctx", None),
        P(),
        P("fsdp", "tp"),
        P("fsdp", "tp"),
        P(None, "tp"),
        P("tp"),
        P("tp", None, None),
        P("tp"),
        P("tp", None, None),
        P("tp"),
        P("tp"),
        P("tp", "fsdp"),
        P(),
        P("fsdp", "tp"),
        P("fsdp", "tp"),
        P("tp", "fsdp"),
    )
    return jax.shard_map(shards, mesh=mesh, in_specs=in_specs, out_specs=out_specs, check_vma=False)
```

```python
import functools

import jax
import jax.numpy as jnp
import numpy as np
from jax import lax
from jax.experimental import pallas as pl
from jax.experimental.pallas import tpu as pltpu
from jax.sharding import PartitionSpec as P

EPSILON = 1e-06
RATE_SCALE = 8.0
GELU_C = 0.7978845608028654
GELU_K = 0.044715
GROUP = ("ctx", "tp")
F32, BF16 = jnp.float32, jnp.bfloat16


def matmul(left, right):
    return jnp.dot(left, right, preferred_element_type=F32)


def left_inner(left, right):
    return lax.dot_general(left, right, (((0,), (0,)), ((), ())), preferred_element_type=F32)


def right_inner(left, right):
    return lax.dot_general(left, right, (((1,), (1,)), ((), ())), preferred_element_type=F32)


def gelu_parts(v):
    t = jnp.tanh(GELU_C * (v + GELU_K * (v * v * v)))
    half = 0.5 * (1.0 + t)
    slope = half + 0.5 * v * (1.0 - t * t) * (GELU_C * (1.0 + 3.0 * GELU_K * v * v))
    return v * half, slope


def gelu(v):
    return 0.5 * v * (1.0 + jnp.tanh(GELU_C * (v + GELU_K * (v * v * v))))


def one_minus_exp(u):
    series = 1.0 - u * (1.0 / 8.0)
    for n in (7.0, 6.0, 5.0, 4.0, 3.0, 2.0):
        series = 1.0 - u * (1.0 / n) * series
    return jnp.where(u < 0.5, u * series, 1.0 - jnp.exp(-u))


def rms_rows(values):
    return lax.rsqrt(jnp.mean(values * values, axis=-1, keepdims=True) + EPSILON)


def norm_back(grad_norm, scaled, scale_row, gain):
    grad_scaled = grad_norm * gain
    return scale_row * (
        grad_scaled - scaled * jnp.mean(grad_scaled * scaled, axis=-1, keepdims=True)
    )


def step_mask(kind, g):
    core = g % 2
    if kind == "core":
        return 1
    return 2 if (kind == "near") == (core == 0) else 4


def exchange(block, kind):
    pairs = [(g, g ^ step_mask(kind, g)) for g in range(8)]
    return lax.ppermute(block, GROUP, pairs)


def flip(block, mask):
    return lax.ppermute(block, GROUP, [(g, g ^ mask) for g in range(8)])


def place_table():
    table = np.zeros((8, 8), np.int32)
    for g in range(8):
        for spot in range(8):
            at = g ^ (spot >> 2)
            block = at
            if spot & 1:
                block ^= step_mask("near", at)
            if spot & 2:
                block ^= step_mask("far", at)
            table[g, block] = spot
    return table


def reduce_rows(left, right, product):
    half = left.shape[0] // 2
    sent = product(left[half:], right).astype(BF16)
    kept = product(left[:half], right)
    got = exchange(sent, "core")
    kept, got = lax.optimization_barrier((kept, got))
    total = kept + got.astype(F32)
    for kind in ("far", "near"):
        half = half // 2
        got = exchange(total[half:].astype(BF16), kind)
        total = total[:half] + got.astype(F32)
    return total


def partners():
    fsdp, ctx, tp = lax.axis_index("fsdp"), lax.axis_index("ctx"), lax.axis_index("tp")
    core, line = tp % 2, tp // 2
    across = (fsdp, 1 - ctx, tp)
    along = (fsdp, ctx, (1 - line) * 2 + core)
    same = (fsdp, ctx, line * 2 + 1 - core)
    near = (fsdp, ctx + core * (1 - 2 * ctx), (line + (1 - core) * (1 - 2 * line)) * 2 + core)
    far = (fsdp, ctx + (1 - core) * (1 - 2 * ctx), (line + core * (1 - 2 * line)) * 2 + core)
    return core, line, tp, across, along, same, near, far


def meet(*devices):
    barrier = pltpu.get_barrier_semaphore()
    for device in devices:
        pl.semaphore_signal(barrier, inc=1, device_id=device, device_id_type=pl.DeviceIdType.MESH)
    pl.semaphore_wait(barrier, len(devices))


def remote(src, dst, send_sem, recv_sem, device):
    return pltpu.make_async_remote_copy(
        src_ref=src, dst_ref=dst, send_sem=send_sem, recv_sem=recv_sem, device_id=device,
        device_id_type=pl.DeviceIdType.MESH,
    )


def by_rows(count, step, body):
    def turn(i, _):
        body(pl.multiple_of(i * step, step))
        return 0

    lax.fori_loop(0, count // step, turn, 0)


def head_kernel(tokens, cot, gain, normed_out, cot_out, x_buf, n_buf, c_buf, load, store, send, recv):
    rows = x_buf.shape[0] // 4
    core, line, tp, across, along, same, _, _ = partners()
    load_x = pltpu.make_async_copy(tokens, x_buf, load.at[0])
    load_c = pltpu.make_async_copy(cot, c_buf, load.at[1])
    load_x.start()
    load_c.start()
    meet(across, along, same)

    def block(j):
        return pl.ds(pl.multiple_of(j * rows, rows), rows)

    def normalize(j):
        def body(r):
            at = pl.ds(pl.multiple_of(j * rows + r, 32), 32)
            x = x_buf[at, :].astype(F32)
            n_buf[at, :] = (x * rms_rows(x) * gain[...]).astype(BF16)

        by_rows(rows, 32, body)

    load_x.wait()
    normalize(tp)
    outs = (normed_out, cot_out)
    bufs = (n_buf, c_buf)
    first = [
        remote(bufs[i].at[block(tp)], outs[i].at[2 - core], send.at[i], recv.at[i], across) for i in range(2)
    ]
    first[0].start()
    load_c.wait()
    first[1].start()
    for j in range(1, 4):
        normalize((tp + j) % 4)
    kept = []
    for k, (dy, dc) in enumerate(((0, 0), (1, 0), (0, 1), (1, 1))):
        there = line + dy * (1 - 2 * line)
        which = core + dc * (1 - 2 * core)
        effect = which
        spot = 4 * dc + dy * (1 + effect)
        for i in range(2):
            copy = pltpu.make_async_copy(bufs[i].at[block(there * 2 + which)], outs[i].at[spot], store.at[2 * k + i])
            copy.start()
            kept.append(copy)
    later = []
    for i in range(2):
        first[i].wait_recv()
        second = remote(outs[i].at[2 - core], outs[i].at[3], send.at[2 + i], recv.at[2 + i], along)
        second.start()
        third = remote(outs[i].at[2 - core], outs[i].at[6 - core], send.at[4 + i], recv.at[4 + i], same)
        third.start()
        later.append((second, third))
    last = []
    for i in range(2):
        later[i][0].wait_recv()
        fourth = remote(outs[i].at[3], outs[i].at[7], send.at[6 + i], recv.at[6 + i], same)
        fourth.start()
        last.append(fourth)
    for i in range(2):
        later[i][1].wait_recv()
        last[i].wait_recv()
        first[i].wait_send()
        later[i][0].wait_send()
        later[i][1].wait_send()
        last[i].wait_send()
    for copy in kept:
        copy.wait()


def head(tokens, cot, gain, collective_id):
    count, width = tokens.shape
    rows = count // 4
    out = jax.ShapeDtypeStruct((8, rows, width), BF16)
    anywhere = pl.BlockSpec(memory_space=pl.ANY)
    return pl.pallas_call(
        head_kernel,
        in_specs=[anywhere, anywhere, pl.BlockSpec(memory_space=pltpu.VMEM)],
        out_specs=[anywhere, anywhere],
        out_shape=[out, out],
        scratch_shapes=[pltpu.VMEM((count, width), BF16)] * 3
        + [
            pltpu.SemaphoreType.DMA((2,)),
            pltpu.SemaphoreType.DMA((8,)),
            pltpu.SemaphoreType.DMA((8,)),
            pltpu.SemaphoreType.DMA((8,)),
        ],
        compiler_params=pltpu.CompilerParams(
            collective_id=collective_id, has_side_effects=True, vmem_limit_bytes=60 << 20
        ),
        cost_estimate=pl.CostEstimate(flops=5 << 33, bytes_accessed=64 << 20, transcendentals=0),
        name="head",
    )(tokens, cot, gain)


def plane_sum_kernel(
    epilogue, wide, left, right, base, source, gain, *refs
):
    if epilogue == "norm":
        out, kept_out, refs = refs[0], refs[1], refs[2:]
    elif wide:
        out, kept_out, gain_out, refs = refs[0], refs[1], refs[2], refs[3:]
    else:
        rows_in, pair, single, out, gain_out, rows_out, pair_a, pair_b, single_out = refs[:9]
        refs = refs[9:]
    to_core, from_core, acc, to_far, from_far, to_near, from_near, own, store, send, recv, gsend, grecv = refs
    rows, width = own.shape
    core, line, tp, across, along, same, near, far = partners()
    meet(same, near, far)
    tile = width // 4

    def products(row, ref, at):
        def turn(i, _):
            cols = pl.ds(pl.multiple_of(i * tile, tile), tile)
            part = right_inner(left[pl.ds(row, 2 * rows), :], right[cols, :])
            ref[pl.ds(at, 2 * rows), cols] = part.astype(ref.dtype)
            return 0

        lax.fori_loop(0, 4, turn, 0)

    def both(a):
        return pl.ds(a * rows, 2 * rows)

    core_copy = [
        remote(to_core.at[both(2 * h)], from_core.at[both(2 * h)], send.at[h], recv.at[h], same) for h in range(2)
    ]
    far_copy = [remote(to_far.at[h], from_far.at[h], send.at[2 + h], recv.at[2 + h], far) for h in range(2)]
    near_copy = remote(to_near, from_near, send.at[4], recv.at[4], near)

    local = []
    if not wide:
        came = (1 - line) * 2 + core
        local.append(pltpu.make_async_copy(rows_in, rows_out.at[tp], store.at[1]))
        rows_copy = [
            remote(rows_in, rows_out.at[tp], gsend.at[3], grecv.at[3], along),
            remote(rows_in, rows_out.at[tp], gsend.at[4], grecv.at[4], same),
            remote(rows_out.at[came], rows_out.at[came], gsend.at[5], grecv.at[5], same),
        ]
        half_at = lax.axis_index("ctx")
        units, deep = pair.shape[1] // 2, single.shape[0]
        cols = pl.ds(pl.multiple_of(half_at * units, 128), units)
        lines = pl.ds(pl.multiple_of(half_at * deep, 16), deep)
        swap = (
            (pair.at[:, pl.ds(0, units)], pair_a.at[:, cols]),
            (pair.at[:, pl.ds(units, units)], pair_b.at[:, cols]),
            (single, single_out.at[lines, :]),
        )
        half_copy = [
            remote(src, dst, gsend.at[6 + i], grecv.at[6 + i], across) for i, (src, dst) in enumerate(swap)
        ]
        local += [pltpu.make_async_copy(src, dst, store.at[2 + i]) for i, (src, dst) in enumerate(swap)]
        rows_copy[0].start()
        rows_copy[1].start()
        for copy in local:
            copy.start()

    products(6 * rows, to_core, 2 * rows)
    core_copy[1].start()
    products(2 * rows, acc, 2 * rows)
    core_copy[1].wait_recv()
    for h in (1, 0):
        def body(r, h=h):
            at = pl.ds(pl.multiple_of((2 + h) * rows + r, 32), 32)
            to_far[h, pl.ds(r, 32), :] = (acc[at, :] + from_core[at, :].astype(F32)).astype(BF16)

        by_rows(rows, 32, body)
        far_copy[h].start()
    products(4 * rows, to_core, 0)
    core_copy[0].start()
    products(0, acc, 0)
    core_copy[0].wait_recv()
    far_copy[1].wait_recv()

    def send_near(r):
        at = pl.ds(pl.multiple_of(rows + r, 32), 32)
        total = acc[at, :] + from_core[at, :].astype(F32) + from_far[1, pl.ds(r, 32), :].astype(F32)
        to_near[pl.ds(r, 32), :] = total.astype(BF16)

    by_rows(rows, 32, send_near)
    near_copy.start()
    far_copy[0].wait_recv()
    if not wide:
        for copy in half_copy:
            copy.start()
        rows_copy[0].wait_recv()
        rows_copy[2].start()

    def settle(r):
        at = pl.ds(r, 32)
        acc[at, :] = acc[at, :] + from_core[at, :].astype(F32) + from_far[0, at, :].astype(F32)

    by_rows(rows, 32, settle)
    if epilogue != "norm":
        gain_out[...] = jnp.zeros_like(gain_out)
    near_copy.wait_recv()

    def finish(r):
        at = pl.ds(r, 32)
        total = acc[at, :] + from_near[at, :].astype(F32)
        if epilogue == "norm":
            resid = base[at, :].astype(F32) + total
            kept_out[at, :] = resid
            own[at, :] = (resid * rms_rows(resid) * gain[...]).astype(BF16)
        else:
            x = source[at, :].astype(F32)
            scale = rms_rows(x)
            scaled = x * scale
            grad = base[at, :].astype(F32) + norm_back(total, scaled, scale, gain[...])
            gain_out[...] += jnp.sum((total * scaled).reshape(4, 8, width), axis=0)
            if wide:
                kept_out[at, :] = grad
            own[at, :] = grad.astype(BF16)

    by_rows(rows, 32, finish)
    if wide:
        mine = pltpu.make_async_copy(own, out.at[0], store.at[0])
        mine.start()
        copies = [
            remote(own, out.at[1], gsend.at[1], grecv.at[1], near),
            remote(own, out.at[2], gsend.at[2], grecv.at[2], far),
            remote(own, out.at[4], gsend.at[4], grecv.at[4], same),
            remote(out.at[1], out.at[3], gsend.at[3], grecv.at[3], far),
            remote(out.at[1], out.at[5], gsend.at[5], grecv.at[5], same),
            remote(out.at[2], out.at[6], gsend.at[6], grecv.at[6], same),
            remote(out.at[3], out.at[7], gsend.at[7], grecv.at[7], same),
        ]
        for k in range(3):
            copies[k].start()
        copies[0].wait_recv()
        copies[3].start()
        copies[4].start()
        copies[1].wait_recv()
        copies[5].start()
        copies[3].wait_recv()
        copies[6].start()
        for k in (2, 4, 5, 6):
            copies[k].wait_recv()
    else:
        mine = pltpu.make_async_copy(own, out.at[tp], store.at[0])
        mine.start()
        copies = [
            remote(own, out.at[tp], gsend.at[0], grecv.at[0], along),
            remote(own, out.at[tp], gsend.at[1], grecv.at[1], same),
        ]
        copies[0].start()
        copies[1].start()
        copies[0].wait_recv()
        copies.append(remote(out.at[came], out.at[came], gsend.at[2], grecv.at[2], same))
        copies[2].start()
        copies[1].wait_recv()
        copies[2].wait_recv()
        for copy in rows_copy[1:] + half_copy:
            copy.wait_recv()
        copies += rows_copy + half_copy
    for copy in copies + core_copy + far_copy + [near_copy]:
        copy.wait_send()
    for copy in local + [mine]:
        copy.wait()


def plane_sum(epilogue, wide, left, right, base, source, gain, collective_id, cost, extra_in=()):
    count, width = left.shape[0], right.shape[0]
    rows = count // 8
    vmem = pl.BlockSpec(memory_space=pltpu.VMEM)
    anywhere = pl.BlockSpec(memory_space=pl.ANY)
    whole = jax.ShapeDtypeStruct((rows, width), F32)
    gains = jax.ShapeDtypeStruct((8, width), F32)
    extra = [whole] if epilogue == "norm" else [whole, gains] if wide else [gains]
    carried = []
    if not wide:
        _, pair, single = extra_in
        carried = [(4, rows, width), pair.shape, pair.shape, (2 * single.shape[0], single.shape[1])]
        carried = [jax.ShapeDtypeStruct(shape, BF16) for shape in carried]
    return pl.pallas_call(
        functools.partial(plane_sum_kernel, epilogue, wide),
        in_specs=[vmem] * (5 + len(extra_in)),
        out_specs=[anywhere] + [vmem] * len(extra) + [anywhere] * len(carried),
        out_shape=[jax.ShapeDtypeStruct((8 if wide else 4, rows, width), BF16)] + extra + carried,
        scratch_shapes=[
            pltpu.VMEM((4 * rows, width), BF16),
            pltpu.VMEM((4 * rows, width), BF16),
            pltpu.VMEM((4 * rows, width), F32),
            pltpu.VMEM((2, rows, width), BF16),
            pltpu.VMEM((2, rows, width), BF16),
            pltpu.VMEM((rows, width), BF16),
            pltpu.VMEM((rows, width), BF16),
            pltpu.VMEM((rows, width), BF16),
            pltpu.SemaphoreType.DMA((5,)),
            pltpu.SemaphoreType.DMA((5,)),
            pltpu.SemaphoreType.DMA((5,)),
            pltpu.SemaphoreType.DMA((9,)),
            pltpu.SemaphoreType.DMA((9,)),
        ],
        compiler_params=pltpu.CompilerParams(
            collective_id=collective_id, has_side_effects=True, vmem_limit_bytes=62 << 20
        ),
        cost_estimate=pl.CostEstimate(flops=cost, bytes_accessed=count * width, transcendentals=0),
        name="plane_sum",
    )(left, right, base, source, gain, *extra_in)


tied = lax.optimization_barrier


def sum_fsdp(x):
    size = lax.axis_size("fsdp")
    bit = 1
    while bit < size:
        x = x + lax.ppermute(x, "fsdp", [(i, i ^ bit) for i in range(size)])
        bit *= 2
    return x


def gather_fsdp(x):
    size, at = lax.axis_size("fsdp"), lax.axis_index("fsdp")
    bit = 1
    while bit < size:
        other = lax.ppermute(x, "fsdp", [(i, i ^ bit) for i in range(size)])
        later = (at // bit) % 2 == 1
        x = jnp.concatenate([jnp.where(later, other, x), jnp.where(later, x, other)], axis=0)
        bit *= 2
    return x


def scan_rows(a_ref, b_ref, carry, reverse):
    rows, width = b_ref.shape
    groups = rows // 8
    a = a_ref[...].reshape(groups, 8, width)
    b = b_ref[...].reshape(groups, 8, width)
    at = lax.broadcasted_iota(jnp.int32, (groups, 8, width), 1)
    for shift in (1, 2, 4):
        ok = (at < 8 - shift) if reverse else (at >= shift)
        turn = 8 - shift if reverse else shift
        b_before = jnp.where(ok, pltpu.roll(b, turn, 1), 0.0)
        a_before = jnp.where(ok, pltpu.roll(a, turn, 1), 1.0)
        b = a * b_before + b
        a = a * a_before
    a_ref[...] = a.reshape(rows, width)
    b_ref[...] = b.reshape(rows, width)
    for k in range(groups):
        k = groups - 1 - k if reverse else k
        part = pl.ds(8 * k, 8)
        now = b_ref[part, :] + a_ref[part, :] * carry
        b_ref[part, :] = now
        carry = now[0:1, :] if reverse else now[7:8, :]
    return carry


def mixer_kernel(
    place, pre, masks, params, gate_a, gate_x, mixed, states, recur_out, input_out, conv_out, ext, a_buf, b_buf, carry
):
    rows, width = states.shape

    @pl.when(pl.program_id(0) == 0)
    def _():
        ext[...] = jnp.zeros_like(ext)
        carry[...] = jnp.zeros_like(carry)

    ext[0:8, :] = ext[rows : rows + 8, :]
    ext[8:, :] = pre[:, width:].astype(BF16).astype(F32)
    conv = params[4:5, :] + params[0:1, :] * ext[8:, :]
    for k in range(1, 4):
        conv = conv + params[k : k + 1, :] * (masks[:, k - 1 : k] * ext[pl.ds(8 - k, rows), :])
    conv_low = conv.astype(BF16)
    conv_out[...] = conv_low
    conv = conv_low.astype(F32)
    recur = jax.nn.sigmoid(matmul(conv_low, gate_a[...]) + params[5:6, :])
    opened = jax.nn.sigmoid(matmul(conv_low, gate_x[...]) + params[6:7, :])
    recur_out[...] = recur
    input_out[...] = opened
    log_decay = params[7:8, :] * recur
    same = masks[:, 0:1]
    root = jnp.sqrt(one_minus_exp(-2.0 * log_decay))
    a_buf[...] = same * jnp.exp(log_decay)
    b_buf[...] = opened * conv * jnp.where(same > 0.5, root, 1.0)
    carry[0:1, :] = scan_rows(a_buf, b_buf, carry[0:1, :], False)
    state = b_buf[...]
    states[...] = state
    mixed[...] = (state * gelu(pre[:, :width])).astype(BF16)


def mixer_back_kernel(
    place, grad_mixed, pre, pre_tail, states, states_tail, recur_in, input_in, conv_in, masks, params, gate_a, gate_x,
    grads, sums, sum_a, sum_x, ext, grad_ext, a_buf, b_buf, carry,
):
    rows, width = states.shape
    step = pl.program_id(0)
    first = step == pl.num_programs(0) - 1

    @pl.when(step == 0)
    def _():
        grad_ext[...] = jnp.zeros_like(grad_ext)
        carry[...] = jnp.zeros_like(carry)
        sums[...] = jnp.zeros_like(sums)
        sum_a[...] = jnp.zeros_like(sum_a)
        sum_x[...] = jnp.zeros_like(sum_x)

    inside = jnp.where(first, 0.0, 1.0)
    branch, slope = gelu_parts(pre[:, :width])
    above = grad_mixed[...]
    state = states[...]
    grads[:, :width] = (above * state * slope).astype(BF16)
    recur, opened = recur_in[...], input_in[...]
    conv_low = conv_in[...]
    conv = conv_low.astype(F32)
    same = masks[:, 0:1]
    rate = params[7:8, :]
    log_decay = rate * recur
    decay = jnp.exp(log_decay)
    root = jnp.sqrt(one_minus_exp(-2.0 * log_decay))
    mult = jnp.where(same > 0.5, root, 1.0)
    a_buf[0:rows, :] = same * decay
    head = a_buf[0:1, :]
    a_buf[rows : rows + 8, :] = jnp.broadcast_to(carry[1:2, :], (8, width))
    factor = a_buf[pl.ds(1, rows), :]
    a_buf[0:rows, :] = factor
    b_buf[...] = above * branch
    new_carry = scan_rows(a_buf.at[pl.ds(0, rows), :], b_buf, carry[0:1, :], True)
    carry[0:1, :] = new_carry
    carry[1:2, :] = head
    total = b_buf[...]
    ext[0:8, :] = inside * states_tail[...]
    ext[8:, :] = state
    before = ext[pl.ds(7, rows), :]
    grad_open = total * opened
    grad_log = jnp.where(
        same > 0.5, total * before * decay - grad_open * conv * decay * decay / root, 0.0
    )

    def fold(x):
        return jnp.sum(x.reshape(rows // 8, 8, width), axis=0)

    sums[0:8, :] += fold(grad_log * recur)
    low_a = (grad_log * rate * recur * (1.0 - recur)).astype(BF16)
    low_x = (total * conv * mult * opened * (1.0 - opened)).astype(BF16)
    sums[8:16, :] += fold(low_a.astype(F32))
    sums[16:24, :] += fold(low_x.astype(F32))
    sum_a[...] += left_inner(conv_low, low_a)
    sum_x[...] += left_inner(conv_low, low_x)
    grad_conv = grad_open * mult + (
        right_inner(low_a, gate_a[...]) + right_inner(low_x, gate_x[...])
    )
    sums[24:32, :] += fold(grad_conv)
    ext[0:8, :] = inside * pre_tail[:, width:].astype(BF16).astype(F32)
    ext[8:, :] = pre[:, width:].astype(BF16).astype(F32)
    grad_ext[rows : rows + 8, :] = grad_ext[0:8, :]
    grad_ext[0:rows, :] = grad_conv
    grad_in = params[0:1, :] * grad_conv
    sums[32:40, :] += fold(grad_conv * ext[8:, :])
    for k in range(1, 4):
        earlier = masks[:, k - 1 : k] * ext[pl.ds(8 - k, rows), :]
        sums[32 + 8 * k : 40 + 8 * k, :] += fold(grad_conv * earlier)
        grad_in = grad_in + params[k : k + 1, :] * (
            masks[:, k + 2 : k + 3] * grad_ext[pl.ds(k, rows), :]
        )
    grads[:, width:] = grad_in.astype(BF16)


def mixer(pre, masks, params, gate_a, gate_x, place, rows):
    count, width = pre.shape[0], pre.shape[1] // 2
    steps = count // rows
    spot = lambda i, place: (place[i], 0)
    inorder = lambda i, place: (i, 0)
    fixed = lambda i, place: (0, 0)
    wide = pl.BlockSpec((rows, 2 * width), spot)
    one = pl.BlockSpec((rows, width), spot)
    gate = pl.BlockSpec((width, width), fixed)
    return pl.pallas_call(
        mixer_kernel,
        grid_spec=pltpu.PrefetchScalarGridSpec(
            num_scalar_prefetch=1,
            grid=(steps,),
            in_specs=[wide, pl.BlockSpec((rows, 8), inorder), pl.BlockSpec((8, width), fixed), gate, gate],
            out_specs=[one] * 5,
            scratch_shapes=[
                pltpu.VMEM((rows + 8, width), F32),
                pltpu.VMEM((rows, width), F32),
                pltpu.VMEM((rows, width), F32),
                pltpu.VMEM((8, width), F32),
            ],
        ),
        out_shape=[
            jax.ShapeDtypeStruct((count, width), kind) for kind in (BF16, F32, F32, F32, BF16)
        ],
        cost_estimate=pl.CostEstimate(
            flops=count * width * (4 * width + 120), bytes_accessed=count * width * 24, transcendentals=count * width * 6
        ),
        name="mixer",
    )(place, pre, masks, params, gate_a, gate_x)


def mixer_back(grad_mixed, pre, states, recur, opened, conv, masks, params, gate_a, gate_x, place, rows):
    count, width = states.shape
    steps = count // rows
    last = steps - 1
    spot = lambda i, place: (place[last - i], 0)
    inorder = lambda i, place: (last - i, 0)
    fixed = lambda i, place: (0, 0)

    def tail(i, place):
        return (place[jnp.maximum(last - i - 1, 0)] * (rows // 8) + rows // 8 - 1, 0)

    wide = pl.BlockSpec((rows, 2 * width), spot)
    one = pl.BlockSpec((rows, width), spot)
    gate = pl.BlockSpec((width, width), fixed)
    return pl.pallas_call(
        mixer_back_kernel,
        grid_spec=pltpu.PrefetchScalarGridSpec(
            num_scalar_prefetch=1,
            grid=(steps,),
            in_specs=[
                one, wide, pl.BlockSpec((8, 2 * width), tail), one, pl.BlockSpec((8, width), tail), one, one, one,
                pl.BlockSpec((rows, 8), inorder), pl.BlockSpec((8, width), fixed), gate, gate,
            ],
            out_specs=[wide, pl.BlockSpec((64, width), fixed), gate, gate],
            scratch_shapes=[
                pltpu.VMEM((rows + 8, width), F32),
                pltpu.VMEM((rows + 8, width), F32),
                pltpu.VMEM((rows + 8, width), F32),
                pltpu.VMEM((rows, width), F32),
                pltpu.VMEM((8, width), F32),
            ],
        ),
        out_shape=[
            jax.ShapeDtypeStruct((count, 2 * width), BF16),
            jax.ShapeDtypeStruct((64, width), F32),
            jax.ShapeDtypeStruct((width, width), F32),
            jax.ShapeDtypeStruct((width, width), F32),
        ],
        cost_estimate=pl.CostEstimate(
            flops=count * width * (8 * width + 200), bytes_accessed=count * width * 34, transcendentals=count * width * 4
        ),
        name="mixer_back",
    )(place, grad_mixed, pre, pre, states, states, recur, opened, conv, masks, params, gate_a, gate_x)


def on_diagonal(blocks):
    heads, size = blocks.shape[0], blocks.shape[1]
    out = jnp.zeros((heads * size, heads * size), blocks.dtype)
    for h in range(heads):
        out = lax.dynamic_update_slice(out, blocks[h], (h * size, h * size))
    return out


def shards(
    tokens, segments, cotangent, gain_mix, w_branch, w_input, conv_weight, conv_bias, gate_a, bias_a, gate_x, bias_x,
    decay_param, w_out, gain_mlp, w_gate, w_up, w_down,
):
    half_at = lax.axis_index("ctx")
    place_tp = lax.axis_index("tp")

    def mine(x, axis):
        size = x.shape[axis] // 2
        return lax.dynamic_slice_in_dim(x, half_at * size, size, axis)

    def owned(x, axis):
        return lax.psum_scatter(x, "fsdp", scatter_dimension=axis, tiled=True)

    _, tok_count, model_width = tokens.shape
    rows = tok_count // 4
    length = 2 * tok_count
    own_in = jnp.concatenate([mine(w_branch, 1), mine(w_input, 1), mine(w_out, 0).T], axis=1)
    full_mix = lax.all_gather(own_in, "fsdp", axis=0, tiled=True)
    own_gu = jnp.concatenate([mine(w_gate, 1), mine(w_up, 1)], axis=1)
    full_gu = lax.all_gather(own_gu, "fsdp", axis=0, tiled=True)
    full_down = lax.all_gather(mine(w_down, 0), "fsdp", axis=1, tiled=True)

    width = own_in.shape[1] // 3
    full_in, full_out = full_mix[:, : 2 * width], full_mix[:, 2 * width :]
    units = own_gu.shape[1] // 2
    place = jnp.asarray(place_table())[half_at * 4 + place_tp]

    rate = -RATE_SCALE * jax.nn.softplus(-decay_param)
    params = jnp.concatenate(
        [
            mine(conv_weight, 1),
            jnp.stack([mine(v, 0) for v in (conv_bias, bias_a, bias_x, rate)]),
        ],
        axis=0,
    )
    heads_a, heads_x = mine(gate_a, 0), mine(gate_x, 0)
    head_count, head_width = heads_a.shape[0], heads_a.shape[1]
    diag_a, diag_x = on_diagonal(heads_a), on_diagonal(heads_x)
    seg = segments[0]
    around = jnp.pad(seg, (3, 3), constant_values=-1)
    marks = [around[3 - k : 3 - k + length] == seg for k in (1, 2, 3)]
    marks += [around[3 + k : 3 + k + length] == seg for k in (1, 2, 3)]
    marks += [jnp.zeros_like(marks[0])] * 2
    masks = jnp.stack(marks, axis=1).astype(F32)

    own = lax.dynamic_slice_in_dim(tokens[0], place_tp * rows, rows, 0)
    own_cot = lax.dynamic_slice_in_dim(cotangent[0], place_tp * rows, rows, 0)
    gain_mix, gain_mlp = gain_mix[None], gain_mlp[None]
    normed, cot = head(tokens[0], cotangent[0], gain_mix, 1)
    normed, cot = normed.reshape(length, model_width), cot.reshape(length, model_width)

    pre = matmul(normed, full_in)
    mixed, states, recur, opened, conv = mixer(pre, masks, params, diag_a, diag_x, place, rows)
    normed_mlp, resid = plane_sum("norm", True, mixed, full_out, own, own, gain_mlp, 2, 9 << 33)
    normed_mlp = normed_mlp.reshape(length, model_width)

    both = matmul(normed_mlp, full_gu)
    gate_pre, up_pre = both[:, :units], both[:, units:]
    gate_act, gate_slope = gelu_parts(gate_pre)
    hidden = (gate_act * up_pre).astype(BF16)
    grad_w_down = left_inner(hidden, cot).astype(BF16)
    full_down, grad_w_down, hidden = tied((full_down, grad_w_down, hidden))
    own_down = owned(grad_w_down, 1)

    grad_hidden = right_inner(cot, full_down)
    grad_both = jnp.concatenate(
        [
            (grad_hidden * up_pre * gate_slope).astype(BF16),
            (grad_hidden * gate_act).astype(BF16),
        ],
        axis=1,
    )
    grad_w_gu = left_inner(normed_mlp, grad_both).astype(BF16)
    half = length // 2
    sent = matmul(hidden[half:], full_down).astype(BF16)
    grad_w_gu, sent = tied((grad_w_gu, sent))
    own_gu = owned(grad_w_gu, 0)
    got = exchange(sent, "core")
    kept = matmul(hidden[:half], full_down)
    grad_both, kept, got, grad_w_gu = tied((grad_both, kept, got, grad_w_gu))
    total = kept + got.astype(F32)
    got_far = exchange(total[half // 2 :].astype(BF16), "far")
    total = total[: half // 2]
    grad_both, total = tied((grad_both, total))
    grad_proj, grad_resid, gain_mlp_part = plane_sum(
        "back", True, grad_both, full_gu, own_cot, resid, gain_mlp, 3, 9 << 33
    )
    grad_proj = grad_proj.reshape(length, model_width)
    grad_proj, got_far, total = tied((grad_proj, got_far, total))
    total = total + got_far.astype(F32)
    got_near = exchange(total[half // 4 :].astype(BF16), "near")
    total = total[: half // 4]

    grad_w_out = left_inner(mixed, grad_proj).astype(BF16)
    grad_proj, own_down, grad_w_out = tied((grad_proj, own_down, grad_w_out))
    own_out = owned(grad_w_out, 1)
    grad_mixed = matmul(grad_proj, full_out)
    other_down = flip(own_down, 4)
    grads_in, sums, sum_a, sum_x = mixer_back(
        grad_mixed, pre, states, recur, opened, conv, masks, params, diag_a, diag_x, place, rows
    )
    grads_in, got_near, total, other_down, own_gu = tied((grads_in, got_near, total, other_down, own_gu))
    output = (resid + total + got_near.astype(F32)).astype(BF16)
    lines = jnp.sum(sums.reshape(8, 8, width), axis=1)
    head_at = lax.broadcasted_iota(jnp.int32, (head_width, width), 1) // head_width
    squares = [
        sum(
            jnp.where(head_at == h, part[h * head_width : (h + 1) * head_width], 0.0) for h in range(head_count)
        )
        for part in (sum_a, sum_x)
    ]
    fsdp_size = lax.axis_size("fsdp")
    part_rows = 16 * -(-(8 + 2 * head_width) // (16 * fsdp_size))
    spare = fsdp_size * part_rows - 8 - 2 * head_width
    small = jnp.concatenate([lines] + squares + [jnp.zeros((spare, width), F32)], axis=0).astype(BF16)
    small = small.reshape(fsdp_size, 2, part_rows // 2, width)
    small = jnp.concatenate([small[:, 0], small[:, 1]], axis=2)
    grad_w_in = left_inner(normed, grads_in).astype(BF16).reshape(fsdp_size, -1, 2 * width)
    grad_w_in = jnp.concatenate([grad_w_in, small], axis=1).reshape(-1, 2 * width)
    grads_in, grad_w_in, own_out = tied((grads_in, grad_w_in, own_out))
    own_in = owned(grad_w_in, 0)
    grad_tokens, gain_mix_part, output, own_gate, own_up, own_out = plane_sum(
        "back", False, grads_in, full_in, grad_resid, own, gain_mix, 4, 5 << 33, (output, own_gu, own_out)
    )
    gain_mix_part, gain_mlp_part = jnp.sum(gain_mix_part, axis=0), jnp.sum(gain_mlp_part, axis=0)

    def both_halves(x, other, axis):
        low = jnp.where(half_at == 0, x, other)
        high = jnp.where(half_at == 0, other, x)
        return jnp.concatenate([low, high], axis=axis).astype(F32)

    other_in = flip(own_in, 4)
    small_part = own_in[model_width // fsdp_size :]
    own_in, other_in = [x[: model_width // fsdp_size] for x in (own_in, other_in)]
    small = gather_fsdp(jnp.concatenate([small_part[:, :width], small_part[:, width:]], axis=0))
    other_small = flip(small, 4)
    own_down = both_halves(own_down, other_down, 0)
    lines = both_halves(small[:8], other_small[:8], 1)
    squares = []
    for i in range(2):
        part = both_halves(small[8 + i * head_width :][:head_width], other_small[8 + i * head_width :][:head_width], 1)
        squares.append(
            jnp.stack([part[:, h * head_width : (h + 1) * head_width] for h in range(2 * head_count)])
        )
    gains = jnp.stack([gain_mix_part, gain_mlp_part])
    for mask in (1, 2, 4):
        gains = gains + flip(gains, mask)
    gains = sum_fsdp(gains)
    own_branch = both_halves(own_in[:, :width], other_in[:, :width], 1)
    own_input = both_halves(own_in[:, width:], other_in[:, width:], 1)
    return (
        output.reshape(1, tok_count, model_width),
        grad_tokens.reshape(1, tok_count, model_width),
        gains[0],
        own_branch,
        own_input,
        lines[4:8],
        lines[3],
        squares[0],
        lines[1],
        squares[1],
        lines[2],
        RATE_SCALE * jax.nn.sigmoid(-decay_param) * lines[0],
        own_out.astype(F32),
        gains[1],
        own_gate.astype(F32),
        own_up.astype(F32),
        own_down,
    )


def solution(mesh):
    in_specs = (
        P("fsdp", "ctx", None),
        P("fsdp", None),
        P("fsdp", "ctx", None),
        P(),
        P("fsdp", "tp"),
        P("fsdp", "tp"),
        P(None, "tp"),
        P("tp"),
        P("tp", None, None),
        P("tp"),
        P("tp", None, None),
        P("tp"),
        P("tp"),
        P("tp", "fsdp"),
        P(),
        P("fsdp", "tp"),
        P("fsdp", "tp"),
        P("tp", "fsdp"),
    )
    out_specs = (
        P("fsdp", "ctx", None),
        P("fsdp", "ctx", None),
        P(),
        P("fsdp", "tp"),
        P("fsdp", "tp"),
        P(None, "tp"),
        P("tp"),
        P("tp", None, None),
        P("tp"),
        P("tp", None, None),
        P("tp"),
        P("tp"),
        P("tp", "fsdp"),
        P(),
        P("fsdp", "tp"),
        P("fsdp", "tp"),
        P("tp", "fsdp"),
    )
    return jax.shard_map(shards, mesh=mesh, in_specs=in_specs, out_specs=out_specs, check_vma=False)
```

```python
import functools

import jax
import jax.numpy as jnp
import numpy as np
from jax import lax
from jax.experimental import pallas as pl
from jax.experimental.pallas import tpu as pltpu
from jax.sharding import PartitionSpec as P

EPSILON = 1e-06
RATE_SCALE = 8.0
GELU_C = 0.7978845608028654
GELU_K = 0.044715
GROUP = ("ctx", "tp")
F32, BF16 = jnp.float32, jnp.bfloat16
tied = lax.optimization_barrier


def matmul(left, right):
    return jnp.dot(left, right, preferred_element_type=F32)


def left_inner(left, right):
    return lax.dot_general(left, right, (((0,), (0,)), ((), ())), preferred_element_type=F32)


def right_inner(left, right):
    return lax.dot_general(left, right, (((1,), (1,)), ((), ())), preferred_element_type=F32)


def gelu_parts(v):
    t = jnp.tanh(GELU_C * (v + GELU_K * (v * v * v)))
    half = 0.5 * (1.0 + t)
    slope = half + 0.5 * v * (1.0 - t * t) * (GELU_C * (1.0 + 3.0 * GELU_K * v * v))
    return v * half, slope


def gelu(v):
    return 0.5 * v * (1.0 + jnp.tanh(GELU_C * (v + GELU_K * (v * v * v))))


def one_minus_exp(u):
    series = 1.0 - u * (1.0 / 8.0)
    for n in (7.0, 6.0, 5.0, 4.0, 3.0, 2.0):
        series = 1.0 - u * (1.0 / n) * series
    return jnp.where(u < 0.5, u * series, 1.0 - jnp.exp(-u))


def rms_rows(values):
    return lax.rsqrt(jnp.mean(values * values, axis=-1, keepdims=True) + EPSILON)


def norm_back(grad_norm, scaled, scale_row, gain):
    grad_scaled = grad_norm * gain
    return scale_row * (
        grad_scaled - scaled * jnp.mean(grad_scaled * scaled, axis=-1, keepdims=True)
    )


def step_mask(kind, g):
    core = g % 2
    if kind == "core":
        return 1
    return 2 if (kind == "near") == (core == 0) else 4


def exchange(block, kind):
    pairs = [(g, g ^ step_mask(kind, g)) for g in range(8)]
    return lax.ppermute(block, GROUP, pairs)


def flip(block, mask):
    return lax.ppermute(block, GROUP, [(g, g ^ mask) for g in range(8)])


def place_table():
    table = np.zeros((8, 8), np.int32)
    for g in range(8):
        for spot in range(8):
            at = g ^ (spot >> 2)
            block = at
            if spot & 1:
                block ^= step_mask("near", at)
            if spot & 2:
                block ^= step_mask("far", at)
            table[g, block] = spot
    return table


def reduce_rows(left, right, product):
    half = left.shape[0] // 2
    sent = product(left[half:], right).astype(BF16)
    kept = product(left[:half], right)
    got = exchange(sent, "core")
    kept, got = lax.optimization_barrier((kept, got))
    total = kept + got.astype(F32)
    for kind in ("far", "near"):
        half = half // 2
        got = exchange(total[half:].astype(BF16), kind)
        total = total[:half] + got.astype(F32)
    return total


def partners():
    fsdp, ctx, tp = lax.axis_index("fsdp"), lax.axis_index("ctx"), lax.axis_index("tp")
    core, line = tp % 2, tp // 2
    across = (fsdp, 1 - ctx, tp)
    along = (fsdp, ctx, (1 - line) * 2 + core)
    same = (fsdp, ctx, line * 2 + 1 - core)
    near = (fsdp, ctx + core * (1 - 2 * ctx), (line + (1 - core) * (1 - 2 * line)) * 2 + core)
    far = (fsdp, ctx + (1 - core) * (1 - 2 * ctx), (line + core * (1 - 2 * line)) * 2 + core)
    return core, line, tp, across, along, same, near, far


def meet(*devices):
    barrier = pltpu.get_barrier_semaphore()
    for device in devices:
        pl.semaphore_signal(barrier, inc=1, device_id=device, device_id_type=pl.DeviceIdType.MESH)
    pl.semaphore_wait(barrier, len(devices))


def remote(src, dst, send_sem, recv_sem, device):
    return pltpu.make_async_remote_copy(
        src_ref=src, dst_ref=dst, send_sem=send_sem, recv_sem=recv_sem, device_id=device,
        device_id_type=pl.DeviceIdType.MESH,
    )


def by_rows(count, step, body):
    def turn(i, _):
        body(pl.multiple_of(i * step, step))
        return 0

    lax.fori_loop(0, count // step, turn, 0)


def head_kernel(tokens, cot, gain, normed_out, cot_out, x_buf, n_buf, c_buf, load, store, send, recv):
    rows = x_buf.shape[0] // 4
    core, line, tp, across, along, same, _, _ = partners()
    load_x = pltpu.make_async_copy(tokens, x_buf, load.at[0])
    load_c = pltpu.make_async_copy(cot, c_buf, load.at[1])
    load_x.start()
    load_c.start()
    meet(across, along, same)

    def block(j):
        return pl.ds(pl.multiple_of(j * rows, rows), rows)

    def normalize(j):
        def body(r):
            at = pl.ds(pl.multiple_of(j * rows + r, 32), 32)
            x = x_buf[at, :].astype(F32)
            n_buf[at, :] = (x * rms_rows(x) * gain[...]).astype(BF16)

        by_rows(rows, 32, body)

    load_x.wait()
    normalize(tp)
    outs = (normed_out, cot_out)
    bufs = (n_buf, c_buf)
    first = [
        remote(bufs[i].at[block(tp)], outs[i].at[2 - core], send.at[i], recv.at[i], across) for i in range(2)
    ]
    first[0].start()
    load_c.wait()
    first[1].start()
    for j in range(1, 4):
        normalize((tp + j) % 4)
    kept = []
    for k, (dy, dc) in enumerate(((0, 0), (1, 0), (0, 1), (1, 1))):
        there = line + dy * (1 - 2 * line)
        which = core + dc * (1 - 2 * core)
        effect = which
        spot = 4 * dc + dy * (1 + effect)
        for i in range(2):
            copy = pltpu.make_async_copy(bufs[i].at[block(there * 2 + which)], outs[i].at[spot], store.at[2 * k + i])
            copy.start()
            kept.append(copy)
    later = []
    for i in range(2):
        first[i].wait_recv()
        second = remote(outs[i].at[2 - core], outs[i].at[3], send.at[2 + i], recv.at[2 + i], along)
        second.start()
        third = remote(outs[i].at[2 - core], outs[i].at[6 - core], send.at[4 + i], recv.at[4 + i], same)
        third.start()
        later.append((second, third))
    last = []
    for i in range(2):
        later[i][0].wait_recv()
        fourth = remote(outs[i].at[3], outs[i].at[7], send.at[6 + i], recv.at[6 + i], same)
        fourth.start()
        last.append(fourth)
    for i in range(2):
        later[i][1].wait_recv()
        last[i].wait_recv()
        first[i].wait_send()
        later[i][0].wait_send()
        later[i][1].wait_send()
        last[i].wait_send()
    for copy in kept:
        copy.wait()


def head(tokens, cot, gain, collective_id):
    count, width = tokens.shape
    rows = count // 4
    out = jax.ShapeDtypeStruct((8, rows, width), BF16)
    anywhere = pl.BlockSpec(memory_space=pl.ANY)
    return pl.pallas_call(
        head_kernel,
        in_specs=[anywhere, anywhere, pl.BlockSpec(memory_space=pltpu.VMEM)],
        out_specs=[anywhere, anywhere],
        out_shape=[out, out],
        scratch_shapes=[pltpu.VMEM((count, width), BF16)] * 3
        + [
            pltpu.SemaphoreType.DMA((2,)),
            pltpu.SemaphoreType.DMA((8,)),
            pltpu.SemaphoreType.DMA((8,)),
            pltpu.SemaphoreType.DMA((8,)),
        ],
        compiler_params=pltpu.CompilerParams(
            collective_id=collective_id, has_side_effects=True, vmem_limit_bytes=60 << 20
        ),
        cost_estimate=pl.CostEstimate(flops=5 << 33, bytes_accessed=64 << 20, transcendentals=0),
        name="head",
    )(tokens, cot, gain)


def plane_sum_kernel(
    epilogue, wide, left, right, base, source, gain, *refs
):
    if epilogue == "norm":
        out, kept_out, refs = refs[0], refs[1], refs[2:]
    elif wide:
        out, kept_out, gain_out, refs = refs[0], refs[1], refs[2], refs[3:]
    else:
        rows_in, pair, single, out, gain_out, rows_out, pair_a, pair_b, single_out = refs[:9]
        refs = refs[9:]
    to_core, from_core, acc, to_far, from_far, to_near, from_near, own, store, send, recv, gsend, grecv = refs
    rows, width = own.shape
    core, line, tp, across, along, same, near, far = partners()
    meet(same, near, far)
    tile = width // 4

    def products(row, ref, at):
        def turn(i, _):
            cols = pl.ds(pl.multiple_of(i * tile, tile), tile)
            part = right_inner(left[pl.ds(row, 2 * rows), :], right[cols, :])
            ref[pl.ds(at, 2 * rows), cols] = part.astype(ref.dtype)
            return 0

        lax.fori_loop(0, 4, turn, 0)

    def both(a):
        return pl.ds(a * rows, 2 * rows)

    core_copy = [
        remote(to_core.at[both(2 * h)], from_core.at[both(2 * h)], send.at[h], recv.at[h], same) for h in range(2)
    ]
    far_copy = [remote(to_far.at[h], from_far.at[h], send.at[2 + h], recv.at[2 + h], far) for h in range(2)]
    near_copy = remote(to_near, from_near, send.at[4], recv.at[4], near)

    local = []
    if not wide:
        came = (1 - line) * 2 + core
        local.append(pltpu.make_async_copy(rows_in, rows_out.at[tp], store.at[1]))
        rows_copy = [
            remote(rows_in, rows_out.at[tp], gsend.at[3], grecv.at[3], along),
            remote(rows_in, rows_out.at[tp], gsend.at[4], grecv.at[4], same),
            remote(rows_out.at[came], rows_out.at[came], gsend.at[5], grecv.at[5], same),
        ]
        half_at = lax.axis_index("ctx")
        units, deep = pair.shape[1] // 2, single.shape[0]
        cols = pl.ds(pl.multiple_of(half_at * units, 128), units)
        lines = pl.ds(pl.multiple_of(half_at * deep, 16), deep)
        swap = (
            (pair.at[:, pl.ds(0, units)], pair_a.at[:, cols]),
            (pair.at[:, pl.ds(units, units)], pair_b.at[:, cols]),
            (single, single_out.at[lines, :]),
        )
        half_copy = [
            remote(src, dst, gsend.at[6 + i], grecv.at[6 + i], across) for i, (src, dst) in enumerate(swap)
        ]
        local += [pltpu.make_async_copy(src, dst, store.at[2 + i]) for i, (src, dst) in enumerate(swap)]
        rows_copy[0].start()
        rows_copy[1].start()
        for copy in local:
            copy.start()

    products(6 * rows, to_core, 2 * rows)
    core_copy[1].start()
    products(2 * rows, acc, 2 * rows)
    core_copy[1].wait_recv()
    for h in (1, 0):
        def body(r, h=h):
            at = pl.ds(pl.multiple_of((2 + h) * rows + r, 32), 32)
            to_far[h, pl.ds(r, 32), :] = (acc[at, :] + from_core[at, :].astype(F32)).astype(BF16)

        by_rows(rows, 32, body)
        far_copy[h].start()
    products(4 * rows, to_core, 0)
    core_copy[0].start()
    products(0, acc, 0)
    core_copy[0].wait_recv()
    far_copy[1].wait_recv()

    def send_near(r):
        at = pl.ds(pl.multiple_of(rows + r, 32), 32)
        total = acc[at, :] + from_core[at, :].astype(F32) + from_far[1, pl.ds(r, 32), :].astype(F32)
        to_near[pl.ds(r, 32), :] = total.astype(BF16)

    by_rows(rows, 32, send_near)
    near_copy.start()
    far_copy[0].wait_recv()
    if not wide:
        for copy in half_copy:
            copy.start()
        rows_copy[0].wait_recv()
        rows_copy[2].start()

    def settle(r):
        at = pl.ds(r, 32)
        acc[at, :] = acc[at, :] + from_core[at, :].astype(F32) + from_far[0, at, :].astype(F32)

    by_rows(rows, 32, settle)
    if epilogue != "norm":
        gain_out[...] = jnp.zeros_like(gain_out)
    near_copy.wait_recv()

    def finish(r):
        at = pl.ds(r, 32)
        total = acc[at, :] + from_near[at, :].astype(F32)
        if epilogue == "norm":
            resid = base[at, :].astype(F32) + total
            kept_out[at, :] = resid
            own[at, :] = (resid * rms_rows(resid) * gain[...]).astype(BF16)
        else:
            x = source[at, :].astype(F32)
            scale = rms_rows(x)
            scaled = x * scale
            grad = base[at, :].astype(F32) + norm_back(total, scaled, scale, gain[...])
            gain_out[...] += jnp.sum((total * scaled).reshape(4, 8, width), axis=0)
            if wide:
                kept_out[at, :] = grad
            own[at, :] = grad.astype(BF16)

    by_rows(rows, 32, finish)
    if wide:
        mine = pltpu.make_async_copy(own, out.at[0], store.at[0])
        mine.start()
        copies = [
            remote(own, out.at[1], gsend.at[1], grecv.at[1], near),
            remote(own, out.at[2], gsend.at[2], grecv.at[2], far),
            remote(own, out.at[4], gsend.at[4], grecv.at[4], same),
            remote(out.at[1], out.at[3], gsend.at[3], grecv.at[3], far),
            remote(out.at[1], out.at[5], gsend.at[5], grecv.at[5], same),
            remote(out.at[2], out.at[6], gsend.at[6], grecv.at[6], same),
            remote(out.at[3], out.at[7], gsend.at[7], grecv.at[7], same),
        ]
        for k in range(3):
            copies[k].start()
        copies[0].wait_recv()
        copies[3].start()
        copies[4].start()
        copies[1].wait_recv()
        copies[5].start()
        copies[3].wait_recv()
        copies[6].start()
        for k in (2, 4, 5, 6):
            copies[k].wait_recv()
    else:
        mine = pltpu.make_async_copy(own, out.at[tp], store.at[0])
        mine.start()
        copies = [
            remote(own, out.at[tp], gsend.at[0], grecv.at[0], along),
            remote(own, out.at[tp], gsend.at[1], grecv.at[1], same),
        ]
        copies[0].start()
        copies[1].start()
        copies[0].wait_recv()
        copies.append(remote(out.at[came], out.at[came], gsend.at[2], grecv.at[2], same))
        copies[2].start()
        copies[1].wait_recv()
        copies[2].wait_recv()
        for copy in rows_copy[1:] + half_copy:
            copy.wait_recv()
        copies += rows_copy + half_copy
    for copy in copies + core_copy + far_copy + [near_copy]:
        copy.wait_send()
    for copy in local + [mine]:
        copy.wait()


def plane_sum(epilogue, wide, left, right, base, source, gain, collective_id, cost, extra_in=()):
    count, width = left.shape[0], right.shape[0]
    rows = count // 8
    vmem = pl.BlockSpec(memory_space=pltpu.VMEM)
    anywhere = pl.BlockSpec(memory_space=pl.ANY)
    whole = jax.ShapeDtypeStruct((rows, width), F32)
    gains = jax.ShapeDtypeStruct((8, width), F32)
    extra = [whole] if epilogue == "norm" else [whole, gains] if wide else [gains]
    carried = []
    if not wide:
        _, pair, single = extra_in
        carried = [(4, rows, width), pair.shape, pair.shape, (2 * single.shape[0], single.shape[1])]
        carried = [jax.ShapeDtypeStruct(shape, BF16) for shape in carried]
    return pl.pallas_call(
        functools.partial(plane_sum_kernel, epilogue, wide),
        in_specs=[vmem] * (5 + len(extra_in)),
        out_specs=[anywhere] + [vmem] * len(extra) + [anywhere] * len(carried),
        out_shape=[jax.ShapeDtypeStruct((8 if wide else 4, rows, width), BF16)] + extra + carried,
        scratch_shapes=[
            pltpu.VMEM((4 * rows, width), BF16),
            pltpu.VMEM((4 * rows, width), BF16),
            pltpu.VMEM((4 * rows, width), F32),
            pltpu.VMEM((2, rows, width), BF16),
            pltpu.VMEM((2, rows, width), BF16),
            pltpu.VMEM((rows, width), BF16),
            pltpu.VMEM((rows, width), BF16),
            pltpu.VMEM((rows, width), BF16),
            pltpu.SemaphoreType.DMA((5,)),
            pltpu.SemaphoreType.DMA((5,)),
            pltpu.SemaphoreType.DMA((5,)),
            pltpu.SemaphoreType.DMA((9,)),
            pltpu.SemaphoreType.DMA((9,)),
        ],
        compiler_params=pltpu.CompilerParams(
            collective_id=collective_id, has_side_effects=True, vmem_limit_bytes=62 << 20
        ),
        cost_estimate=pl.CostEstimate(flops=cost, bytes_accessed=count * width, transcendentals=0),
        name="plane_sum",
    )(left, right, base, source, gain, *extra_in)


def last_kernel(
    size, deep, own_in, gain_a, gain_b, smalls, gains, plane, mine, lines, store, small_send, small_recv, plane_send,
    plane_recv, line_send, line_recv,
):
    thin = smalls.shape[2]
    fsdp, ctx, tp = lax.axis_index("fsdp"), lax.axis_index("ctx"), lax.axis_index("tp")

    def away(dz, dc, dt):
        return (lax.rem(fsdp + dz, size), lax.rem(ctx + dc, 2), lax.rem(tp + dt, 4))

    in_plane = [(0, dc, dt) for dc in range(2) for dt in range(4)][1:]
    across_line = [(dz, dc, 0) for dz in range(size) for dc in range(2)][1:]
    along_line = [(dz, 0, 0) for dz in range(1, size)]
    meet(*[away(*d) for d in in_plane + [d for d in across_line if d not in in_plane]])
    copies = []
    at = lax.broadcasted_iota(jnp.int32, gains.shape, 0)
    sum_a = jnp.sum(gain_a[...], axis=0, keepdims=True)
    sum_b = jnp.sum(gain_b[...], axis=0, keepdims=True)
    place = ctx * 4 + tp
    plane[place] = jnp.where(at == 0, sum_a, jnp.where(at == 1, sum_b, 0.0))
    sent = [
        remote(plane.at[place], plane.at[place], plane_send.at[i], plane_recv.at[i], away(*d))
        for i, d in enumerate(in_plane)
    ]
    for copy in sent:
        copy.start()
    thin_rows = own_in.at[pl.ds(deep, thin), :]
    local = pltpu.make_async_copy(thin_rows, smalls.at[ctx, fsdp], store.at[0])
    local.start()
    for i, d in enumerate(across_line):
        copies.append(remote(thin_rows, smalls.at[ctx, fsdp], small_send.at[i], small_recv.at[i], away(*d)))
        copies[-1].start()
    for copy in sent:
        copy.wait_recv()
    total = plane[0]
    for i in range(1, 8):
        total = total + plane[i]
    mine[...] = total
    lines[fsdp] = total
    further = [
        remote(mine, lines.at[fsdp], line_send.at[i], line_recv.at[i], away(*d)) for i, d in enumerate(along_line)
    ]
    for copy in further:
        copy.start()
    for copy in further:
        copy.wait_recv()
    total = lines[0]
    for i in range(1, size):
        total = total + lines[i]
    gains[...] = total
    for copy in copies:
        copy.wait_recv()
    for copy in copies + sent + further:
        copy.wait_send()
    local.wait()


def last(own_in, gain_a, gain_b, deep, size, collective_id):
    width, thin = own_in.shape[1], own_in.shape[0] - deep
    vmem = pl.BlockSpec(memory_space=pltpu.VMEM)
    anywhere = pl.BlockSpec(memory_space=pl.ANY)
    sems = [pltpu.SemaphoreType.DMA((n,)) for n in (1, 2 * size, 2 * size, 8, 8, size, size)]
    return pl.pallas_call(
        functools.partial(last_kernel, size, deep),
        in_specs=[anywhere, vmem, vmem],
        out_specs=[anywhere, vmem],
        out_shape=[
            jax.ShapeDtypeStruct((2, size, thin, width), BF16),
            jax.ShapeDtypeStruct(gain_a.shape, F32),
        ],
        scratch_shapes=[
            pltpu.VMEM((8,) + gain_a.shape, F32),
            pltpu.VMEM(gain_a.shape, F32),
            pltpu.VMEM((size,) + gain_a.shape, F32),
        ]
        + sems,
        compiler_params=pltpu.CompilerParams(
            collective_id=collective_id, has_side_effects=True, vmem_limit_bytes=32 << 20
        ),
        cost_estimate=pl.CostEstimate(flops=1 << 33, bytes_accessed=4 << 20, transcendentals=0),
        name="last",
    )(own_in, gain_a, gain_b)


def scan_rows(a_ref, b_ref, carry, reverse):
    rows, width = b_ref.shape
    groups = rows // 8
    a = a_ref[...].reshape(groups, 8, width)
    b = b_ref[...].reshape(groups, 8, width)
    at = lax.broadcasted_iota(jnp.int32, (groups, 8, width), 1)
    for shift in (1, 2, 4):
        ok = (at < 8 - shift) if reverse else (at >= shift)
        turn = 8 - shift if reverse else shift
        b_before = jnp.where(ok, pltpu.roll(b, turn, 1), 0.0)
        a_before = jnp.where(ok, pltpu.roll(a, turn, 1), 1.0)
        b = a * b_before + b
        a = a * a_before
    a_ref[...] = a.reshape(rows, width)
    b_ref[...] = b.reshape(rows, width)
    for k in range(groups):
        k = groups - 1 - k if reverse else k
        part = pl.ds(8 * k, 8)
        now = b_ref[part, :] + a_ref[part, :] * carry
        b_ref[part, :] = now
        carry = now[0:1, :] if reverse else now[7:8, :]
    return carry


def mixer_kernel(
    place, pre, masks, params, gate_a, gate_x, mixed, states, recur_out, input_out, conv_out, ext, a_buf, b_buf, carry
):
    rows, width = states.shape

    @pl.when(pl.program_id(0) == 0)
    def _():
        ext[...] = jnp.zeros_like(ext)
        carry[...] = jnp.zeros_like(carry)

    ext[0:8, :] = ext[rows : rows + 8, :]
    ext[8:, :] = pre[:, width:].astype(BF16).astype(F32)
    conv = params[4:5, :] + params[0:1, :] * ext[8:, :]
    for k in range(1, 4):
        conv = conv + params[k : k + 1, :] * (masks[:, k - 1 : k] * ext[pl.ds(8 - k, rows), :])
    conv_low = conv.astype(BF16)
    conv_out[...] = conv_low
    conv = conv_low.astype(F32)
    recur = jax.nn.sigmoid(matmul(conv_low, gate_a[...]) + params[5:6, :])
    opened = jax.nn.sigmoid(matmul(conv_low, gate_x[...]) + params[6:7, :])
    recur_out[...] = recur
    input_out[...] = opened
    log_decay = params[7:8, :] * recur
    same = masks[:, 0:1]
    root = jnp.sqrt(one_minus_exp(-2.0 * log_decay))
    a_buf[...] = same * jnp.exp(log_decay)
    b_buf[...] = opened * conv * jnp.where(same > 0.5, root, 1.0)
    carry[0:1, :] = scan_rows(a_buf, b_buf, carry[0:1, :], False)
    state = b_buf[...]
    states[...] = state
    mixed[...] = (state * gelu(pre[:, :width])).astype(BF16)


def mixer_back_kernel(
    place, grad_mixed, pre, pre_tail, states, states_tail, recur_in, input_in, conv_in, masks, params, gate_a, gate_x,
    grads, sums, sum_a, sum_x, ext, grad_ext, a_buf, b_buf, carry,
):
    rows, width = states.shape
    step = pl.program_id(0)
    first = step == pl.num_programs(0) - 1

    @pl.when(step == 0)
    def _():
        grad_ext[...] = jnp.zeros_like(grad_ext)
        carry[...] = jnp.zeros_like(carry)
        sums[...] = jnp.zeros_like(sums)
        sum_a[...] = jnp.zeros_like(sum_a)
        sum_x[...] = jnp.zeros_like(sum_x)

    inside = jnp.where(first, 0.0, 1.0)
    branch, slope = gelu_parts(pre[:, :width])
    above = grad_mixed[...]
    state = states[...]
    grads[:, :width] = (above * state * slope).astype(BF16)
    recur, opened = recur_in[...], input_in[...]
    conv_low = conv_in[...]
    conv = conv_low.astype(F32)
    same = masks[:, 0:1]
    rate = params[7:8, :]
    log_decay = rate * recur
    decay = jnp.exp(log_decay)
    root = jnp.sqrt(one_minus_exp(-2.0 * log_decay))
    mult = jnp.where(same > 0.5, root, 1.0)
    a_buf[0:rows, :] = same * decay
    head = a_buf[0:1, :]
    a_buf[rows : rows + 8, :] = jnp.broadcast_to(carry[1:2, :], (8, width))
    factor = a_buf[pl.ds(1, rows), :]
    a_buf[0:rows, :] = factor
    b_buf[...] = above * branch
    new_carry = scan_rows(a_buf.at[pl.ds(0, rows), :], b_buf, carry[0:1, :], True)
    carry[0:1, :] = new_carry
    carry[1:2, :] = head
    total = b_buf[...]
    ext[0:8, :] = inside * states_tail[...]
    ext[8:, :] = state
    before = ext[pl.ds(7, rows), :]
    grad_open = total * opened
    grad_log = jnp.where(
        same > 0.5, total * before * decay - grad_open * conv * decay * decay / root, 0.0
    )

    def fold(x):
        return jnp.sum(x.reshape(rows // 8, 8, width), axis=0)

    sums[0:8, :] += fold(grad_log * recur)
    low_a = (grad_log * rate * recur * (1.0 - recur)).astype(BF16)
    low_x = (total * conv * mult * opened * (1.0 - opened)).astype(BF16)
    sums[8:16, :] += fold(low_a.astype(F32))
    sums[16:24, :] += fold(low_x.astype(F32))
    sum_a[...] += left_inner(conv_low, low_a)
    sum_x[...] += left_inner(conv_low, low_x)
    grad_conv = grad_open * mult + (
        right_inner(low_a, gate_a[...]) + right_inner(low_x, gate_x[...])
    )
    sums[24:32, :] += fold(grad_conv)
    ext[0:8, :] = inside * pre_tail[:, width:].astype(BF16).astype(F32)
    ext[8:, :] = pre[:, width:].astype(BF16).astype(F32)
    grad_ext[rows : rows + 8, :] = grad_ext[0:8, :]
    grad_ext[0:rows, :] = grad_conv
    grad_in = params[0:1, :] * grad_conv
    sums[32:40, :] += fold(grad_conv * ext[8:, :])
    for k in range(1, 4):
        earlier = masks[:, k - 1 : k] * ext[pl.ds(8 - k, rows), :]
        sums[32 + 8 * k : 40 + 8 * k, :] += fold(grad_conv * earlier)
        grad_in = grad_in + params[k : k + 1, :] * (
            masks[:, k + 2 : k + 3] * grad_ext[pl.ds(k, rows), :]
        )
    grads[:, width:] = grad_in.astype(BF16)


def mixer(pre, masks, params, gate_a, gate_x, place, rows):
    count, width = pre.shape[0], pre.shape[1] // 2
    steps = count // rows
    spot = lambda i, place: (place[i], 0)
    inorder = lambda i, place: (i, 0)
    fixed = lambda i, place: (0, 0)
    wide = pl.BlockSpec((rows, 2 * width), spot)
    one = pl.BlockSpec((rows, width), spot)
    gate = pl.BlockSpec((width, width), fixed)
    return pl.pallas_call(
        mixer_kernel,
        grid_spec=pltpu.PrefetchScalarGridSpec(
            num_scalar_prefetch=1,
            grid=(steps,),
            in_specs=[wide, pl.BlockSpec((rows, 8), inorder), pl.BlockSpec((8, width), fixed), gate, gate],
            out_specs=[one] * 5,
            scratch_shapes=[
                pltpu.VMEM((rows + 8, width), F32),
                pltpu.VMEM((rows, width), F32),
                pltpu.VMEM((rows, width), F32),
                pltpu.VMEM((8, width), F32),
            ],
        ),
        out_shape=[
            jax.ShapeDtypeStruct((count, width), kind) for kind in (BF16, F32, F32, F32, BF16)
        ],
        cost_estimate=pl.CostEstimate(
            flops=count * width * (4 * width + 120), bytes_accessed=count * width * 24, transcendentals=count * width * 6
        ),
        name="mixer",
    )(place, pre, masks, params, gate_a, gate_x)


def mixer_back(grad_mixed, pre, states, recur, opened, conv, masks, params, gate_a, gate_x, place, rows):
    count, width = states.shape
    steps = count // rows
    last = steps - 1
    spot = lambda i, place: (place[last - i], 0)
    inorder = lambda i, place: (last - i, 0)
    fixed = lambda i, place: (0, 0)

    def tail(i, place):
        return (place[jnp.maximum(last - i - 1, 0)] * (rows // 8) + rows // 8 - 1, 0)

    wide = pl.BlockSpec((rows, 2 * width), spot)
    one = pl.BlockSpec((rows, width), spot)
    gate = pl.BlockSpec((width, width), fixed)
    return pl.pallas_call(
        mixer_back_kernel,
        grid_spec=pltpu.PrefetchScalarGridSpec(
            num_scalar_prefetch=1,
            grid=(steps,),
            in_specs=[
                one, wide, pl.BlockSpec((8, 2 * width), tail), one, pl.BlockSpec((8, width), tail), one, one, one,
                pl.BlockSpec((rows, 8), inorder), pl.BlockSpec((8, width), fixed), gate, gate,
            ],
            out_specs=[wide, pl.BlockSpec((64, width), fixed), gate, gate],
            scratch_shapes=[
                pltpu.VMEM((rows + 8, width), F32),
                pltpu.VMEM((rows + 8, width), F32),
                pltpu.VMEM((rows + 8, width), F32),
                pltpu.VMEM((rows, width), F32),
                pltpu.VMEM((8, width), F32),
            ],
        ),
        out_shape=[
            jax.ShapeDtypeStruct((count, 2 * width), BF16),
            jax.ShapeDtypeStruct((64, width), F32),
            jax.ShapeDtypeStruct((width, width), F32),
            jax.ShapeDtypeStruct((width, width), F32),
        ],
        cost_estimate=pl.CostEstimate(
            flops=count * width * (8 * width + 200), bytes_accessed=count * width * 34, transcendentals=count * width * 4
        ),
        name="mixer_back",
    )(place, grad_mixed, pre, pre, states, states, recur, opened, conv, masks, params, gate_a, gate_x)


def on_diagonal(blocks):
    heads, size = blocks.shape[0], blocks.shape[1]
    out = jnp.zeros((heads * size, heads * size), blocks.dtype)
    for h in range(heads):
        out = lax.dynamic_update_slice(out, blocks[h], (h * size, h * size))
    return out


def shards(
    tokens, segments, cotangent, gain_mix, w_branch, w_input, conv_weight, conv_bias, gate_a, bias_a, gate_x, bias_x,
    decay_param, w_out, gain_mlp, w_gate, w_up, w_down,
):
    half_at = lax.axis_index("ctx")
    place_tp = lax.axis_index("tp")

    def mine(x, axis):
        size = x.shape[axis] // 2
        return lax.dynamic_slice_in_dim(x, half_at * size, size, axis)

    def owned(x, axis):
        return lax.psum_scatter(x, "fsdp", scatter_dimension=axis, tiled=True)

    _, tok_count, model_width = tokens.shape
    rows = tok_count // 4
    length = 2 * tok_count
    own_in = jnp.concatenate([mine(w_branch, 1), mine(w_input, 1), mine(w_out, 0).T], axis=1)
    full_mix = lax.all_gather(own_in, "fsdp", axis=0, tiled=True)
    own_gu = jnp.concatenate([mine(w_gate, 1), mine(w_up, 1)], axis=1)
    full_gu = lax.all_gather(own_gu, "fsdp", axis=0, tiled=True)
    full_down = lax.all_gather(mine(w_down, 0), "fsdp", axis=1, tiled=True)

    width = own_in.shape[1] // 3
    full_in, full_out = full_mix[:, : 2 * width], full_mix[:, 2 * width :]
    units = own_gu.shape[1] // 2
    place = jnp.asarray(place_table())[half_at * 4 + place_tp]

    rate = -RATE_SCALE * jax.nn.softplus(-decay_param)
    params = jnp.concatenate(
        [
            mine(conv_weight, 1),
            jnp.stack([mine(v, 0) for v in (conv_bias, bias_a, bias_x, rate)]),
        ],
        axis=0,
    )
    heads_a, heads_x = mine(gate_a, 0), mine(gate_x, 0)
    head_count, head_width = heads_a.shape[0], heads_a.shape[1]
    diag_a, diag_x = on_diagonal(heads_a), on_diagonal(heads_x)
    seg = segments[0]
    around = jnp.pad(seg, (3, 3), constant_values=-1)
    marks = [around[3 - k : 3 - k + length] == seg for k in (1, 2, 3)]
    marks += [around[3 + k : 3 + k + length] == seg for k in (1, 2, 3)]
    marks += [jnp.zeros_like(marks[0])] * 2
    masks = jnp.stack(marks, axis=1).astype(F32)

    own = lax.dynamic_slice_in_dim(tokens[0], place_tp * rows, rows, 0)
    own_cot = lax.dynamic_slice_in_dim(cotangent[0], place_tp * rows, rows, 0)
    gain_mix, gain_mlp = gain_mix[None], gain_mlp[None]
    normed, cot = head(tokens[0], cotangent[0], gain_mix, 1)
    normed, cot = normed.reshape(length, model_width), cot.reshape(length, model_width)

    pre = matmul(normed, full_in)
    mixed, states, recur, opened, conv = mixer(pre, masks, params, diag_a, diag_x, place, rows)
    normed_mlp, resid = plane_sum("norm", True, mixed, full_out, own, own, gain_mlp, 2, 9 << 33)
    normed_mlp = normed_mlp.reshape(length, model_width)

    both = matmul(normed_mlp, full_gu)
    gate_pre, up_pre = both[:, :units], both[:, units:]
    gate_act, gate_slope = gelu_parts(gate_pre)
    hidden = (gate_act * up_pre).astype(BF16)
    grad_w_down = left_inner(hidden, cot).astype(BF16)
    full_down, grad_w_down, hidden, full_in, own_cot = tied((full_down, grad_w_down, hidden, full_in, own_cot))
    own_down = owned(grad_w_down, 1)

    grad_hidden = right_inner(cot, full_down)
    grad_both = jnp.concatenate(
        [
            (grad_hidden * up_pre * gate_slope).astype(BF16),
            (grad_hidden * gate_act).astype(BF16),
        ],
        axis=1,
    )
    grad_w_gu = left_inner(normed_mlp, grad_both).astype(BF16)
    half = length // 2
    sent = matmul(hidden[half:], full_down).astype(BF16)
    grad_w_gu, sent = tied((grad_w_gu, sent))
    own_gu = owned(grad_w_gu, 0)
    got = exchange(sent, "core")
    grad_both, got, grad_w_gu = tied((grad_both, got, grad_w_gu))
    far_sent = (matmul(hidden[half // 2 : half], full_down) + got[half // 2 :].astype(F32)).astype(BF16)
    got_far = exchange(far_sent, "far")
    low = matmul(hidden[: half // 2], full_down) + got[: half // 2].astype(F32)
    grad_both, low, far_sent = tied((grad_both, low, far_sent))
    grad_proj, grad_resid, gain_mlp_part = plane_sum(
        "back", True, grad_both, full_gu, own_cot, resid, gain_mlp, 3, 9 << 33
    )
    grad_proj = grad_proj.reshape(length, model_width)
    grad_proj, got_far, low = tied((grad_proj, got_far, low))
    near_sent = (low[rows:] + got_far[rows:].astype(F32)).astype(BF16)
    got_near = exchange(near_sent, "near")

    grad_w_out = left_inner(mixed, grad_proj).astype(BF16)
    grad_proj, own_down, grad_w_out = tied((grad_proj, own_down, grad_w_out))
    own_out = owned(grad_w_out, 1)
    grad_mixed = matmul(grad_proj, full_out)
    other_down = flip(own_down, 4)
    grads_in, sums, sum_a, sum_x = mixer_back(
        grad_mixed, pre, states, recur, opened, conv, masks, params, diag_a, diag_x, place, rows
    )
    grads_in, got_near, other_down, own_gu = tied((grads_in, got_near, other_down, own_gu))
    output = (resid + low[:rows] + got_far[:rows].astype(F32) + got_near.astype(F32)).astype(BF16)
    lines = jnp.sum(sums.reshape(8, 8, width), axis=1)
    head_at = lax.broadcasted_iota(jnp.int32, (head_width, width), 1) // head_width
    squares = [
        sum(
            jnp.where(head_at == h, part[h * head_width : (h + 1) * head_width], 0.0) for h in range(head_count)
        )
        for part in (sum_a, sum_x)
    ]
    fsdp_size = lax.axis_size("fsdp")
    part_rows = 16 * -(-(8 + 2 * head_width) // (16 * fsdp_size))
    spare = fsdp_size * part_rows - 8 - 2 * head_width
    small = jnp.concatenate([lines] + squares + [jnp.zeros((spare, width), F32)], axis=0).astype(BF16)
    small = small.reshape(fsdp_size, 2, part_rows // 2, width)
    small = jnp.concatenate([small[:, 0], small[:, 1]], axis=2)
    grad_w_in = left_inner(normed, grads_in).astype(BF16).reshape(fsdp_size, -1, 2 * width)
    grad_w_in = jnp.concatenate([grad_w_in, small], axis=1).reshape(-1, 2 * width)
    grads_in, grad_w_in, own_out = tied((grads_in, grad_w_in, own_out))
    own_in = owned(grad_w_in, 0)
    grad_tokens, gain_mix_part, output, own_gate, own_up, own_out = plane_sum(
        "back", False, grads_in, full_in, grad_resid, own, gain_mix, 4, 5 << 33, (output, own_gu, own_out)
    )
    own_in, own_gate, own_up, own_out, own_down = tied((own_in, own_gate, own_up, own_out, own_down))
    other_in = flip(own_in, 4)
    own_in, other_in = tied((own_in, other_in))
    smalls, gains = last(own_in, gain_mix_part, gain_mlp_part, model_width // fsdp_size, fsdp_size, 5)

    def both_halves(x, other, axis):
        low = jnp.where(half_at == 0, x, other)
        high = jnp.where(half_at == 0, other, x)
        return jnp.concatenate([low, high], axis=axis).astype(F32)

    own_in, other_in = [x[: model_width // fsdp_size] for x in (own_in, other_in)]
    own_down = both_halves(own_down, other_down, 0)
    smalls = jnp.stack([smalls[..., :width], smalls[..., width:]], axis=2).reshape(2, fsdp_size * part_rows, width)
    smalls = jnp.concatenate([smalls[0], smalls[1]], axis=1).astype(F32)
    lines = smalls[:8]
    squares = []
    for i in range(2):
        part = smalls[8 + i * head_width : 8 + (i + 1) * head_width]
        squares.append(
            jnp.stack([part[:, h * head_width : (h + 1) * head_width] for h in range(2 * head_count)])
        )
    own_branch = both_halves(own_in[:, :width], other_in[:, :width], 1)
    own_input = both_halves(own_in[:, width:], other_in[:, width:], 1)
    return (
        output.reshape(1, tok_count, model_width),
        grad_tokens.reshape(1, tok_count, model_width),
        gains[0],
        own_branch,
        own_input,
        lines[4:8],
        lines[3],
        squares[0],
        lines[1],
        squares[1],
        lines[2],
        RATE_SCALE * jax.nn.sigmoid(-decay_param) * lines[0],
        own_out.astype(F32),
        gains[1],
        own_gate.astype(F32),
        own_up.astype(F32),
        own_down,
    )


def solution(mesh):
    in_specs = (
        P("fsdp", "ctx", None),
        P("fsdp", None),
        P("fsdp", "ctx", None),
        P(),
        P("fsdp", "tp"),
        P("fsdp", "tp"),
        P(None, "tp"),
        P("tp"),
        P("tp", None, None),
        P("tp"),
        P("tp", None, None),
        P("tp"),
        P("tp"),
        P("tp", "fsdp"),
        P(),
        P("fsdp", "tp"),
        P("fsdp", "tp"),
        P("tp", "fsdp"),
    )
    out_specs = (
        P("fsdp", "ctx", None),
        P("fsdp", "ctx", None),
        P(),
        P("fsdp", "tp"),
        P("fsdp", "tp"),
        P(None, "tp"),
        P("tp"),
        P("tp", None, None),
        P("tp"),
        P("tp", None, None),
        P("tp"),
        P("tp"),
        P("tp", "fsdp"),
        P(),
        P("fsdp", "tp"),
        P("fsdp", "tp"),
        P("tp", "fsdp"),
    )
    return jax.shard_map(shards, mesh=mesh, in_specs=in_specs, out_specs=out_specs, check_vma=False)
```

```python
import functools

import jax
import jax.numpy as jnp
import numpy as np
from jax import lax
from jax.experimental import pallas as pl
from jax.experimental.pallas import tpu as pltpu
from jax.sharding import PartitionSpec as P

EPSILON = 1e-06
RATE_SCALE = 8.0
GELU_C = 0.7978845608028654
GELU_K = 0.044715
GROUP = ("ctx", "tp")
F32, BF16 = jnp.float32, jnp.bfloat16
tied = lax.optimization_barrier


def matmul(left, right):
    return jnp.dot(left, right, preferred_element_type=F32)


def left_inner(left, right):
    return lax.dot_general(left, right, (((0,), (0,)), ((), ())), preferred_element_type=F32)


def right_inner(left, right):
    return lax.dot_general(left, right, (((1,), (1,)), ((), ())), preferred_element_type=F32)


def gelu_parts(v):
    t = jnp.tanh(GELU_C * (v + GELU_K * (v * v * v)))
    half = 0.5 * (1.0 + t)
    slope = half + 0.5 * v * (1.0 - t * t) * (GELU_C * (1.0 + 3.0 * GELU_K * v * v))
    return v * half, slope


def gelu(v):
    return 0.5 * v * (1.0 + jnp.tanh(GELU_C * (v + GELU_K * (v * v * v))))


def one_minus_exp(u):
    series = 1.0 - u * (1.0 / 8.0)
    for n in (7.0, 6.0, 5.0, 4.0, 3.0, 2.0):
        series = 1.0 - u * (1.0 / n) * series
    return jnp.where(u < 0.5, u * series, 1.0 - jnp.exp(-u))


def rms_rows(values):
    return lax.rsqrt(jnp.mean(values * values, axis=-1, keepdims=True) + EPSILON)


def norm_back(grad_norm, scaled, scale_row, gain):
    grad_scaled = grad_norm * gain
    return scale_row * (
        grad_scaled - scaled * jnp.mean(grad_scaled * scaled, axis=-1, keepdims=True)
    )


def step_mask(kind, g):
    core = g % 2
    if kind == "core":
        return 1
    return 2 if (kind == "near") == (core == 0) else 4


def exchange(block, kind):
    pairs = [(g, g ^ step_mask(kind, g)) for g in range(8)]
    return lax.ppermute(block, GROUP, pairs)


def flip(block, mask):
    return lax.ppermute(block, GROUP, [(g, g ^ mask) for g in range(8)])


def place_table():
    table = np.zeros((8, 8), np.int32)
    for g in range(8):
        for spot in range(8):
            at = g ^ (spot >> 2)
            block = at
            if spot & 1:
                block ^= step_mask("near", at)
            if spot & 2:
                block ^= step_mask("far", at)
            table[g, block] = spot
    return table


def reduce_rows(left, right, product):
    half = left.shape[0] // 2
    sent = product(left[half:], right).astype(BF16)
    kept = product(left[:half], right)
    got = exchange(sent, "core")
    kept, got = lax.optimization_barrier((kept, got))
    total = kept + got.astype(F32)
    for kind in ("far", "near"):
        half = half // 2
        got = exchange(total[half:].astype(BF16), kind)
        total = total[:half] + got.astype(F32)
    return total


def partners():
    fsdp, ctx, tp = lax.axis_index("fsdp"), lax.axis_index("ctx"), lax.axis_index("tp")
    core, line = tp % 2, tp // 2
    across = (fsdp, 1 - ctx, tp)
    along = (fsdp, ctx, (1 - line) * 2 + core)
    same = (fsdp, ctx, line * 2 + 1 - core)
    near = (fsdp, ctx + core * (1 - 2 * ctx), (line + (1 - core) * (1 - 2 * line)) * 2 + core)
    far = (fsdp, ctx + (1 - core) * (1 - 2 * ctx), (line + core * (1 - 2 * line)) * 2 + core)
    return core, line, tp, across, along, same, near, far


def meet(*devices):
    barrier = pltpu.get_barrier_semaphore()
    for device in devices:
        pl.semaphore_signal(barrier, inc=1, device_id=device, device_id_type=pl.DeviceIdType.MESH)
    pl.semaphore_wait(barrier, len(devices))


def remote(src, dst, send_sem, recv_sem, device):
    return pltpu.make_async_remote_copy(
        src_ref=src, dst_ref=dst, send_sem=send_sem, recv_sem=recv_sem, device_id=device,
        device_id_type=pl.DeviceIdType.MESH,
    )


def by_rows(count, step, body):
    def turn(i, _):
        body(pl.multiple_of(i * step, step))
        return 0

    lax.fori_loop(0, count // step, turn, 0)


def head_kernel(tokens, cot, gain, normed_out, cot_out, x_buf, n_buf, c_buf, load, store, send, recv):
    rows = x_buf.shape[0] // 4
    core, line, tp, across, along, same, _, _ = partners()
    load_x = pltpu.make_async_copy(tokens, x_buf, load.at[0])
    load_c = pltpu.make_async_copy(cot, c_buf, load.at[1])
    load_x.start()
    load_c.start()
    meet(across, along, same)

    def block(j):
        return pl.ds(pl.multiple_of(j * rows, rows), rows)

    def normalize(j):
        def body(r):
            at = pl.ds(pl.multiple_of(j * rows + r, 32), 32)
            x = x_buf[at, :].astype(F32)
            n_buf[at, :] = (x * rms_rows(x) * gain[...]).astype(BF16)

        by_rows(rows, 32, body)

    load_x.wait()
    normalize(tp)
    outs = (normed_out, cot_out)
    bufs = (n_buf, c_buf)
    first = [
        remote(bufs[i].at[block(tp)], outs[i].at[2 - core], send.at[i], recv.at[i], across) for i in range(2)
    ]
    first[0].start()
    load_c.wait()
    first[1].start()
    for j in range(1, 4):
        normalize((tp + j) % 4)
    kept = []
    for k, (dy, dc) in enumerate(((0, 0), (1, 0), (0, 1), (1, 1))):
        there = line + dy * (1 - 2 * line)
        which = core + dc * (1 - 2 * core)
        effect = which
        spot = 4 * dc + dy * (1 + effect)
        for i in range(2):
            copy = pltpu.make_async_copy(bufs[i].at[block(there * 2 + which)], outs[i].at[spot], store.at[2 * k + i])
            copy.start()
            kept.append(copy)
    later = []
    for i in range(2):
        first[i].wait_recv()
        second = remote(outs[i].at[2 - core], outs[i].at[3], send.at[2 + i], recv.at[2 + i], along)
        second.start()
        third = remote(outs[i].at[2 - core], outs[i].at[6 - core], send.at[4 + i], recv.at[4 + i], same)
        third.start()
        later.append((second, third))
    last = []
    for i in range(2):
        later[i][0].wait_recv()
        fourth = remote(outs[i].at[3], outs[i].at[7], send.at[6 + i], recv.at[6 + i], same)
        fourth.start()
        last.append(fourth)
    for i in range(2):
        later[i][1].wait_recv()
        last[i].wait_recv()
        first[i].wait_send()
        later[i][0].wait_send()
        later[i][1].wait_send()
        last[i].wait_send()
    for copy in kept:
        copy.wait()


def head(tokens, cot, gain, collective_id):
    count, width = tokens.shape
    rows = count // 4
    out = jax.ShapeDtypeStruct((8, rows, width), BF16)
    anywhere = pl.BlockSpec(memory_space=pl.ANY)
    return pl.pallas_call(
        head_kernel,
        in_specs=[anywhere, anywhere, pl.BlockSpec(memory_space=pltpu.VMEM)],
        out_specs=[anywhere, anywhere],
        out_shape=[out, out],
        scratch_shapes=[pltpu.VMEM((count, width), BF16)] * 3
        + [
            pltpu.SemaphoreType.DMA((2,)),
            pltpu.SemaphoreType.DMA((8,)),
            pltpu.SemaphoreType.DMA((8,)),
            pltpu.SemaphoreType.DMA((8,)),
        ],
        compiler_params=pltpu.CompilerParams(
            collective_id=collective_id, has_side_effects=True, vmem_limit_bytes=60 << 20
        ),
        cost_estimate=pl.CostEstimate(flops=5 << 33, bytes_accessed=64 << 20, transcendentals=0),
        name="head",
    )(tokens, cot, gain)


def plane_sum_kernel(
    epilogue, wide, left, right, base, source, gain, *refs
):
    if epilogue == "norm":
        out, kept_out, refs = refs[0], refs[1], refs[2:]
    elif wide:
        out, kept_out, gain_out, refs = refs[0], refs[1], refs[2], refs[3:]
    else:
        rows_in, rows_along, pair, out, gain_out, rows_out, pair_a = refs[:7]
        refs = refs[7:]
    to_core, from_core, acc, to_far, from_far, to_near, from_near, own, store, send, recv, gsend, grecv = refs
    rows, width = own.shape
    if not wide:
        own = out
    core, line, tp, across, along, same, near, far = partners()
    meet(same, near, far)
    tile = width // 4

    def products(row, ref, at):
        def turn(i, _):
            cols = pl.ds(pl.multiple_of(i * tile, tile), tile)
            part = right_inner(left[pl.ds(row, 2 * rows), :], right[cols, :])
            ref[pl.ds(at, 2 * rows), cols] = part.astype(ref.dtype)
            return 0

        lax.fori_loop(0, 4, turn, 0)

    def both(a):
        return pl.ds(a * rows, 2 * rows)

    core_copy = [
        remote(to_core.at[both(2 * h)], from_core.at[both(2 * h)], send.at[h], recv.at[h], same) for h in range(2)
    ]
    far_copy = [remote(to_far.at[h], from_far.at[h], send.at[2 + h], recv.at[2 + h], far) for h in range(2)]
    near_copy = remote(to_near, from_near, send.at[4], recv.at[4], near)

    local, carried = [], []
    if not wide:
        came = (1 - line) * 2 + core
        units = pair.shape[1] // 2
        cols = pl.ds(pl.multiple_of(lax.axis_index("ctx") * units, 128), units)
        mine = pair.at[:, pl.ds(0, units)]
        carried = [
            remote(rows_in, rows_out.at[tp], gsend.at[0], grecv.at[0], same),
            remote(rows_along, rows_out.at[came], gsend.at[1], grecv.at[1], same),
            remote(mine, pair_a.at[:, cols], gsend.at[2], grecv.at[2], across),
        ]
        local = [
            pltpu.make_async_copy(rows_in, rows_out.at[tp], store.at[0]),
            pltpu.make_async_copy(rows_along, rows_out.at[came], store.at[1]),
            pltpu.make_async_copy(mine, pair_a.at[:, cols], store.at[2]),
        ]
        carried[2].start()
        for copy in local:
            copy.start()

    products(6 * rows, to_core, 2 * rows)
    core_copy[1].start()
    products(2 * rows, acc, 2 * rows)
    core_copy[1].wait_recv()
    for h in (1, 0):
        def body(r, h=h):
            at = pl.ds(pl.multiple_of((2 + h) * rows + r, 32), 32)
            to_far[h, pl.ds(r, 32), :] = (acc[at, :] + from_core[at, :].astype(F32)).astype(BF16)

        by_rows(rows, 32, body)
        far_copy[h].start()
    products(4 * rows, to_core, 0)
    core_copy[0].start()
    products(0, acc, 0)
    core_copy[0].wait_recv()
    far_copy[1].wait_recv()

    def send_near(r):
        at = pl.ds(pl.multiple_of(rows + r, 32), 32)
        total = acc[at, :] + from_core[at, :].astype(F32) + from_far[1, pl.ds(r, 32), :].astype(F32)
        to_near[pl.ds(r, 32), :] = total.astype(BF16)

    by_rows(rows, 32, send_near)
    near_copy.start()
    if not wide:
        carried[0].start()
        carried[1].start()
    far_copy[0].wait_recv()

    def settle(r):
        at = pl.ds(r, 32)
        acc[at, :] = acc[at, :] + from_core[at, :].astype(F32) + from_far[0, at, :].astype(F32)

    by_rows(rows, 32, settle)
    if epilogue != "norm":
        gain_out[...] = jnp.zeros_like(gain_out)
    near_copy.wait_recv()

    def finish(r):
        at = pl.ds(r, 32)
        total = acc[at, :] + from_near[at, :].astype(F32)
        if epilogue == "norm":
            resid = base[at, :].astype(F32) + total
            kept_out[at, :] = resid
            own[at, :] = (resid * rms_rows(resid) * gain[...]).astype(BF16)
        else:
            x = source[at, :].astype(F32)
            scale = rms_rows(x)
            scaled = x * scale
            grad = base[at, :].astype(F32) + norm_back(total, scaled, scale, gain[...])
            gain_out[...] += jnp.sum((total * scaled).reshape(4, 8, width), axis=0)
            if wide:
                kept_out[at, :] = grad
            own[at, :] = grad.astype(BF16)

    by_rows(rows, 32, finish)
    if wide:
        mine = pltpu.make_async_copy(own, out.at[0], store.at[0])
        mine.start()
        copies = [
            remote(own, out.at[1], gsend.at[1], grecv.at[1], near),
            remote(own, out.at[2], gsend.at[2], grecv.at[2], far),
            remote(own, out.at[4], gsend.at[4], grecv.at[4], same),
            remote(out.at[1], out.at[3], gsend.at[3], grecv.at[3], far),
            remote(out.at[1], out.at[5], gsend.at[5], grecv.at[5], same),
            remote(out.at[2], out.at[6], gsend.at[6], grecv.at[6], same),
            remote(out.at[3], out.at[7], gsend.at[7], grecv.at[7], same),
        ]
        for k in range(3):
            copies[k].start()
        copies[0].wait_recv()
        copies[3].start()
        copies[4].start()
        copies[1].wait_recv()
        copies[5].start()
        copies[3].wait_recv()
        copies[6].start()
        for k in (2, 4, 5, 6):
            copies[k].wait_recv()
        local.append(mine)
    else:
        for copy in carried:
            copy.wait_recv()
        copies = carried
    for copy in copies + core_copy + far_copy + [near_copy]:
        copy.wait_send()
    for copy in local:
        copy.wait()


def plane_sum(epilogue, wide, left, right, base, source, gain, collective_id, cost, extra_in=()):
    count, width = left.shape[0], right.shape[0]
    rows = count // 8
    vmem = pl.BlockSpec(memory_space=pltpu.VMEM)
    anywhere = pl.BlockSpec(memory_space=pl.ANY)
    whole = jax.ShapeDtypeStruct((rows, width), F32)
    gains = jax.ShapeDtypeStruct((8, width), F32)
    extra = [whole] if epilogue == "norm" else [whole, gains] if wide else [gains]
    carried = []
    result = jax.ShapeDtypeStruct((8, rows, width), BF16)
    if not wide:
        carried = [jax.ShapeDtypeStruct((4, rows, width), BF16), jax.ShapeDtypeStruct(extra_in[2].shape, BF16)]
        result = jax.ShapeDtypeStruct((rows, width), BF16)
    return pl.pallas_call(
        functools.partial(plane_sum_kernel, epilogue, wide),
        in_specs=[vmem] * (5 + len(extra_in)),
        out_specs=[anywhere if wide else vmem] + [vmem] * len(extra) + [anywhere] * len(carried),
        out_shape=[result] + extra + carried,
        scratch_shapes=[
            pltpu.VMEM((4 * rows, width), BF16),
            pltpu.VMEM((4 * rows, width), BF16),
            pltpu.VMEM((4 * rows, width), F32),
            pltpu.VMEM((2, rows, width), BF16),
            pltpu.VMEM((2, rows, width), BF16),
            pltpu.VMEM((rows, width), BF16),
            pltpu.VMEM((rows, width), BF16),
            pltpu.VMEM((rows, width), BF16),
            pltpu.SemaphoreType.DMA((5,)),
            pltpu.SemaphoreType.DMA((5,)),
            pltpu.SemaphoreType.DMA((5,)),
            pltpu.SemaphoreType.DMA((9,)),
            pltpu.SemaphoreType.DMA((9,)),
        ],
        compiler_params=pltpu.CompilerParams(
            collective_id=collective_id, has_side_effects=True, vmem_limit_bytes=62 << 20
        ),
        cost_estimate=pl.CostEstimate(flops=cost, bytes_accessed=count * width, transcendentals=0),
        name="plane_sum",
    )(left, right, base, source, gain, *extra_in)


def last_kernel(
    size, deep, own_in, gain_a, gain_b, rows_in, pair, single, other_in, smalls, gains, rows_out, pair_b, single_out,
    plane, mine, lines, store, send, recv, small_send, small_recv, plane_send, plane_recv, line_send, line_recv,
):
    thin = smalls.shape[2]
    fsdp, ctx, tp = lax.axis_index("fsdp"), lax.axis_index("ctx"), lax.axis_index("tp")

    def away(dz, dc, dt):
        return (lax.rem(fsdp + dz, size), lax.rem(ctx + dc, 2), lax.rem(tp + dt, 4))

    in_plane = [(0, dc, dt) for dc in range(2) for dt in range(4)][1:]
    across_line = [(dz, dc, 0) for dz in range(size) for dc in range(2)][1:]
    along_line = [(dz, 0, 0) for dz in range(1, size)]
    meet(*[away(*d) for d in in_plane + [d for d in across_line if d not in in_plane]])
    core, row, _, across, along, same, _, _ = partners()
    came = (1 - row) * 2 + core
    units, tall = pair.shape[1] // 2, single.shape[0]
    cols = pl.ds(pl.multiple_of(ctx * units, 128), units)
    tall_rows = pl.ds(pl.multiple_of(ctx * tall, 16), tall)
    high = pair.at[:, pl.ds(units, units)]
    copies = [
        remote(own_in.at[pl.ds(0, deep), :], other_in, send.at[0], recv.at[0], across),
        remote(rows_in, rows_out.at[tp], send.at[1], recv.at[1], along),
        remote(rows_in, rows_out.at[tp], send.at[2], recv.at[2], same),
        remote(rows_out.at[came], rows_out.at[came], send.at[3], recv.at[3], same),
        remote(high, pair_b.at[:, cols], send.at[4], recv.at[4], across),
        remote(single, single_out.at[tall_rows, :], send.at[5], recv.at[5], across),
    ]
    local = [
        pltpu.make_async_copy(rows_in, rows_out.at[tp], store.at[1]),
        pltpu.make_async_copy(high, pair_b.at[:, cols], store.at[2]),
        pltpu.make_async_copy(single, single_out.at[tall_rows, :], store.at[3]),
    ]
    for i in (1, 0, 2, 4, 5):
        copies[i].start()
    for copy in local:
        copy.start()
    at = lax.broadcasted_iota(jnp.int32, gains.shape, 0)
    sum_a = jnp.sum(gain_a[...], axis=0, keepdims=True)
    sum_b = jnp.sum(gain_b[...], axis=0, keepdims=True)
    place = ctx * 4 + tp
    plane[place] = jnp.where(at == 0, sum_a, jnp.where(at == 1, sum_b, 0.0))
    sent = [
        remote(plane.at[place], plane.at[place], plane_send.at[i], plane_recv.at[i], away(*d))
        for i, d in enumerate(in_plane)
    ]
    for copy in sent:
        copy.start()
    thin_rows = own_in.at[pl.ds(deep, thin), :]
    local.append(pltpu.make_async_copy(thin_rows, smalls.at[ctx, fsdp], store.at[0]))
    local[-1].start()
    for i, d in enumerate(across_line):
        copies.append(remote(thin_rows, smalls.at[ctx, fsdp], small_send.at[i], small_recv.at[i], away(*d)))
        copies[-1].start()
    for copy in sent:
        copy.wait_recv()
    total = plane[0]
    for i in range(1, 8):
        total = total + plane[i]
    mine[...] = total
    lines[fsdp] = total
    further = [
        remote(mine, lines.at[fsdp], line_send.at[i], line_recv.at[i], away(*d)) for i, d in enumerate(along_line)
    ]
    for copy in further:
        copy.start()
    for copy in further:
        copy.wait_recv()
    total = lines[0]
    for i in range(1, size):
        total = total + lines[i]
    gains[...] = total
    copies[1].wait_recv()
    copies[3].start()
    for copy in copies[:1] + copies[2:]:
        copy.wait_recv()
    for copy in copies + sent + further:
        copy.wait_send()
    for copy in local:
        copy.wait()


def last(own_in, gain_a, gain_b, rows, pair, single, deep, size, collective_id):
    width, thin = own_in.shape[1], own_in.shape[0] - deep
    vmem = pl.BlockSpec(memory_space=pltpu.VMEM)
    anywhere = pl.BlockSpec(memory_space=pl.ANY)
    sems = [pltpu.SemaphoreType.DMA((n,)) for n in (4, 6, 6, 2 * size, 2 * size, 8, 8, size, size)]
    return pl.pallas_call(
        functools.partial(last_kernel, size, deep),
        in_specs=[anywhere] + [vmem] * 5,
        out_specs=[anywhere, anywhere, vmem, anywhere, anywhere, anywhere],
        out_shape=[
            jax.ShapeDtypeStruct((deep, width), BF16),
            jax.ShapeDtypeStruct((2, size, thin, width), BF16),
            jax.ShapeDtypeStruct(gain_a.shape, F32),
            jax.ShapeDtypeStruct((4,) + rows.shape, BF16),
            jax.ShapeDtypeStruct(pair.shape, BF16),
            jax.ShapeDtypeStruct((2 * single.shape[0], single.shape[1]), BF16),
        ],
        scratch_shapes=[
            pltpu.VMEM((8,) + gain_a.shape, F32),
            pltpu.VMEM(gain_a.shape, F32),
            pltpu.VMEM((size,) + gain_a.shape, F32),
        ]
        + sems,
        compiler_params=pltpu.CompilerParams(
            collective_id=collective_id, has_side_effects=True, vmem_limit_bytes=32 << 20
        ),
        cost_estimate=pl.CostEstimate(flops=1 << 33, bytes_accessed=4 << 20, transcendentals=0),
        name="last",
    )(own_in, gain_a, gain_b, rows, pair, single)


def scan_rows(a_ref, b_ref, carry, reverse):
    rows, width = b_ref.shape
    groups = rows // 8
    a = a_ref[...].reshape(groups, 8, width)
    b = b_ref[...].reshape(groups, 8, width)
    at = lax.broadcasted_iota(jnp.int32, (groups, 8, width), 1)
    for shift in (1, 2, 4):
        ok = (at < 8 - shift) if reverse else (at >= shift)
        turn = 8 - shift if reverse else shift
        b_before = jnp.where(ok, pltpu.roll(b, turn, 1), 0.0)
        a_before = jnp.where(ok, pltpu.roll(a, turn, 1), 1.0)
        b = a * b_before + b
        a = a * a_before
    a_ref[...] = a.reshape(rows, width)
    b_ref[...] = b.reshape(rows, width)
    for k in range(groups):
        k = groups - 1 - k if reverse else k
        part = pl.ds(8 * k, 8)
        now = b_ref[part, :] + a_ref[part, :] * carry
        b_ref[part, :] = now
        carry = now[0:1, :] if reverse else now[7:8, :]
    return carry


def mixer_kernel(
    place, pre, masks, params, gate_a, gate_x, mixed, states, recur_out, input_out, conv_out, ext, a_buf, b_buf, carry
):
    rows, width = states.shape

    @pl.when(pl.program_id(0) == 0)
    def _():
        ext[...] = jnp.zeros_like(ext)
        carry[...] = jnp.zeros_like(carry)

    ext[0:8, :] = ext[rows : rows + 8, :]
    ext[8:, :] = pre[:, width:].astype(BF16).astype(F32)
    conv = params[4:5, :] + params[0:1, :] * ext[8:, :]
    for k in range(1, 4):
        conv = conv + params[k : k + 1, :] * (masks[:, k - 1 : k] * ext[pl.ds(8 - k, rows), :])
    conv_low = conv.astype(BF16)
    conv_out[...] = conv_low
    conv = conv_low.astype(F32)
    recur = jax.nn.sigmoid(matmul(conv_low, gate_a[...]) + params[5:6, :])
    opened = jax.nn.sigmoid(matmul(conv_low, gate_x[...]) + params[6:7, :])
    recur_out[...] = recur
    input_out[...] = opened
    log_decay = params[7:8, :] * recur
    same = masks[:, 0:1]
    root = jnp.sqrt(one_minus_exp(-2.0 * log_decay))
    a_buf[...] = same * jnp.exp(log_decay)
    b_buf[...] = opened * conv * jnp.where(same > 0.5, root, 1.0)
    carry[0:1, :] = scan_rows(a_buf, b_buf, carry[0:1, :], False)
    state = b_buf[...]
    states[...] = state
    mixed[...] = (state * gelu(pre[:, :width])).astype(BF16)


def mixer_back_kernel(
    place, grad_mixed, pre, pre_tail, states, states_tail, recur_in, input_in, conv_in, masks, params, gate_a, gate_x,
    grads, sums, sum_a, sum_x, ext, grad_ext, a_buf, b_buf, carry,
):
    rows, width = states.shape
    step = pl.program_id(0)
    first = step == pl.num_programs(0) - 1

    @pl.when(step == 0)
    def _():
        grad_ext[...] = jnp.zeros_like(grad_ext)
        carry[...] = jnp.zeros_like(carry)
        sums[...] = jnp.zeros_like(sums)
        sum_a[...] = jnp.zeros_like(sum_a)
        sum_x[...] = jnp.zeros_like(sum_x)

    inside = jnp.where(first, 0.0, 1.0)
    branch, slope = gelu_parts(pre[:, :width])
    above = grad_mixed[...]
    state = states[...]
    grads[:, :width] = (above * state * slope).astype(BF16)
    recur, opened = recur_in[...], input_in[...]
    conv_low = conv_in[...]
    conv = conv_low.astype(F32)
    same = masks[:, 0:1]
    rate = params[7:8, :]
    log_decay = rate * recur
    decay = jnp.exp(log_decay)
    root = jnp.sqrt(one_minus_exp(-2.0 * log_decay))
    mult = jnp.where(same > 0.5, root, 1.0)
    a_buf[0:rows, :] = same * decay
    head = a_buf[0:1, :]
    a_buf[rows : rows + 8, :] = jnp.broadcast_to(carry[1:2, :], (8, width))
    factor = a_buf[pl.ds(1, rows), :]
    a_buf[0:rows, :] = factor
    b_buf[...] = above * branch
    new_carry = scan_rows(a_buf.at[pl.ds(0, rows), :], b_buf, carry[0:1, :], True)
    carry[0:1, :] = new_carry
    carry[1:2, :] = head
    total = b_buf[...]
    ext[0:8, :] = inside * states_tail[...]
    ext[8:, :] = state
    before = ext[pl.ds(7, rows), :]
    grad_open = total * opened
    grad_log = jnp.where(
        same > 0.5, total * before * decay - grad_open * conv * decay * decay / root, 0.0
    )

    def fold(x):
        return jnp.sum(x.reshape(rows // 8, 8, width), axis=0)

    sums[0:8, :] += fold(grad_log * recur)
    low_a = (grad_log * rate * recur * (1.0 - recur)).astype(BF16)
    low_x = (total * conv * mult * opened * (1.0 - opened)).astype(BF16)
    sums[8:16, :] += fold(low_a.astype(F32))
    sums[16:24, :] += fold(low_x.astype(F32))
    sum_a[...] += left_inner(conv_low, low_a)
    sum_x[...] += left_inner(conv_low, low_x)
    grad_conv = grad_open * mult + (
        right_inner(low_a, gate_a[...]) + right_inner(low_x, gate_x[...])
    )
    sums[24:32, :] += fold(grad_conv)
    ext[0:8, :] = inside * pre_tail[:, width:].astype(BF16).astype(F32)
    ext[8:, :] = pre[:, width:].astype(BF16).astype(F32)
    grad_ext[rows : rows + 8, :] = grad_ext[0:8, :]
    grad_ext[0:rows, :] = grad_conv
    grad_in = params[0:1, :] * grad_conv
    sums[32:40, :] += fold(grad_conv * ext[8:, :])
    for k in range(1, 4):
        earlier = masks[:, k - 1 : k] * ext[pl.ds(8 - k, rows), :]
        sums[32 + 8 * k : 40 + 8 * k, :] += fold(grad_conv * earlier)
        grad_in = grad_in + params[k : k + 1, :] * (
            masks[:, k + 2 : k + 3] * grad_ext[pl.ds(k, rows), :]
        )
    grads[:, width:] = grad_in.astype(BF16)


def mixer(pre, masks, params, gate_a, gate_x, place, rows):
    count, width = pre.shape[0], pre.shape[1] // 2
    steps = count // rows
    spot = lambda i, place: (place[i], 0)
    inorder = lambda i, place: (i, 0)
    fixed = lambda i, place: (0, 0)
    wide = pl.BlockSpec((rows, 2 * width), spot)
    one = pl.BlockSpec((rows, width), spot)
    gate = pl.BlockSpec((width, width), fixed)
    return pl.pallas_call(
        mixer_kernel,
        grid_spec=pltpu.PrefetchScalarGridSpec(
            num_scalar_prefetch=1,
            grid=(steps,),
            in_specs=[wide, pl.BlockSpec((rows, 8), inorder), pl.BlockSpec((8, width), fixed), gate, gate],
            out_specs=[one] * 5,
            scratch_shapes=[
                pltpu.VMEM((rows + 8, width), F32),
                pltpu.VMEM((rows, width), F32),
                pltpu.VMEM((rows, width), F32),
                pltpu.VMEM((8, width), F32),
            ],
        ),
        out_shape=[
            jax.ShapeDtypeStruct((count, width), kind) for kind in (BF16, F32, F32, F32, BF16)
        ],
        cost_estimate=pl.CostEstimate(
            flops=count * width * (4 * width + 120), bytes_accessed=count * width * 24, transcendentals=count * width * 6
        ),
        name="mixer",
    )(place, pre, masks, params, gate_a, gate_x)


def mixer_back(grad_mixed, pre, states, recur, opened, conv, masks, params, gate_a, gate_x, place, rows):
    count, width = states.shape
    steps = count // rows
    last = steps - 1
    spot = lambda i, place: (place[last - i], 0)
    inorder = lambda i, place: (last - i, 0)
    fixed = lambda i, place: (0, 0)

    def tail(i, place):
        return (place[jnp.maximum(last - i - 1, 0)] * (rows // 8) + rows // 8 - 1, 0)

    wide = pl.BlockSpec((rows, 2 * width), spot)
    one = pl.BlockSpec((rows, width), spot)
    gate = pl.BlockSpec((width, width), fixed)
    return pl.pallas_call(
        mixer_back_kernel,
        grid_spec=pltpu.PrefetchScalarGridSpec(
            num_scalar_prefetch=1,
            grid=(steps,),
            in_specs=[
                one, wide, pl.BlockSpec((8, 2 * width), tail), one, pl.BlockSpec((8, width), tail), one, one, one,
                pl.BlockSpec((rows, 8), inorder), pl.BlockSpec((8, width), fixed), gate, gate,
            ],
            out_specs=[wide, pl.BlockSpec((64, width), fixed), gate, gate],
            scratch_shapes=[
                pltpu.VMEM((rows + 8, width), F32),
                pltpu.VMEM((rows + 8, width), F32),
                pltpu.VMEM((rows + 8, width), F32),
                pltpu.VMEM((rows, width), F32),
                pltpu.VMEM((8, width), F32),
            ],
        ),
        out_shape=[
            jax.ShapeDtypeStruct((count, 2 * width), BF16),
            jax.ShapeDtypeStruct((64, width), F32),
            jax.ShapeDtypeStruct((width, width), F32),
            jax.ShapeDtypeStruct((width, width), F32),
        ],
        cost_estimate=pl.CostEstimate(
            flops=count * width * (8 * width + 200), bytes_accessed=count * width * 34, transcendentals=count * width * 4
        ),
        name="mixer_back",
    )(place, grad_mixed, pre, pre, states, states, recur, opened, conv, masks, params, gate_a, gate_x)


def on_diagonal(blocks):
    heads, size = blocks.shape[0], blocks.shape[1]
    out = jnp.zeros((heads * size, heads * size), blocks.dtype)
    for h in range(heads):
        out = lax.dynamic_update_slice(out, blocks[h], (h * size, h * size))
    return out


def shards(
    tokens, segments, cotangent, gain_mix, w_branch, w_input, conv_weight, conv_bias, gate_a, bias_a, gate_x, bias_x,
    decay_param, w_out, gain_mlp, w_gate, w_up, w_down,
):
    half_at = lax.axis_index("ctx")
    place_tp = lax.axis_index("tp")

    def mine(x, axis):
        size = x.shape[axis] // 2
        return lax.dynamic_slice_in_dim(x, half_at * size, size, axis)

    def owned(x, axis):
        return lax.psum_scatter(x, "fsdp", scatter_dimension=axis, tiled=True)

    _, tok_count, model_width = tokens.shape
    rows = tok_count // 4
    length = 2 * tok_count
    own_in = jnp.concatenate([mine(w_branch, 1), mine(w_input, 1), mine(w_out, 0).T], axis=1)
    full_mix = lax.all_gather(own_in, "fsdp", axis=0, tiled=True)
    own_gu = jnp.concatenate([mine(w_gate, 1), mine(w_up, 1)], axis=1)
    full_gu = lax.all_gather(own_gu, "fsdp", axis=0, tiled=True)
    full_down = lax.all_gather(mine(w_down, 0), "fsdp", axis=1, tiled=True)

    width = own_in.shape[1] // 3
    full_in, full_out = full_mix[:, : 2 * width], full_mix[:, 2 * width :]
    units = own_gu.shape[1] // 2
    place = jnp.asarray(place_table())[half_at * 4 + place_tp]

    rate = -RATE_SCALE * jax.nn.softplus(-decay_param)
    params = jnp.concatenate(
        [
            mine(conv_weight, 1),
            jnp.stack([mine(v, 0) for v in (conv_bias, bias_a, bias_x, rate)]),
        ],
        axis=0,
    )
    heads_a, heads_x = mine(gate_a, 0), mine(gate_x, 0)
    head_count, head_width = heads_a.shape[0], heads_a.shape[1]
    diag_a, diag_x = on_diagonal(heads_a), on_diagonal(heads_x)
    seg = segments[0]
    around = jnp.pad(seg, (3, 3), constant_values=-1)
    marks = [around[3 - k : 3 - k + length] == seg for k in (1, 2, 3)]
    marks += [around[3 + k : 3 + k + length] == seg for k in (1, 2, 3)]
    marks += [jnp.zeros_like(marks[0])] * 2
    masks = jnp.stack(marks, axis=1).astype(F32)

    own = lax.dynamic_slice_in_dim(tokens[0], place_tp * rows, rows, 0)
    own_cot = lax.dynamic_slice_in_dim(cotangent[0], place_tp * rows, rows, 0)
    gain_mix, gain_mlp = gain_mix[None], gain_mlp[None]
    normed, cot = head(tokens[0], cotangent[0], gain_mix, 1)
    normed, cot = normed.reshape(length, model_width), cot.reshape(length, model_width)

    pre = matmul(normed, full_in)
    mixed, states, recur, opened, conv = mixer(pre, masks, params, diag_a, diag_x, place, rows)
    normed_mlp, resid = plane_sum("norm", True, mixed, full_out, own, own, gain_mlp, 2, 9 << 33)
    normed_mlp = normed_mlp.reshape(length, model_width)

    both = matmul(normed_mlp, full_gu)
    gate_pre, up_pre = both[:, :units], both[:, units:]
    gate_act, gate_slope = gelu_parts(gate_pre)
    hidden = (gate_act * up_pre).astype(BF16)
    grad_w_down = left_inner(hidden, cot).astype(BF16)
    full_down, grad_w_down, hidden, full_in, own_cot = tied((full_down, grad_w_down, hidden, full_in, own_cot))
    own_down = owned(grad_w_down, 1)

    grad_hidden = right_inner(cot, full_down)
    grad_both = jnp.concatenate(
        [
            (grad_hidden * up_pre * gate_slope).astype(BF16),
            (grad_hidden * gate_act).astype(BF16),
        ],
        axis=1,
    )
    grad_w_gu = left_inner(normed_mlp, grad_both).astype(BF16)
    half = length // 2
    sent = matmul(hidden[half:], full_down).astype(BF16)
    grad_w_gu, sent = tied((grad_w_gu, sent))
    own_gu = owned(grad_w_gu, 0)
    got = exchange(sent, "core")
    grad_both, got, grad_w_gu = tied((grad_both, got, grad_w_gu))
    far_sent = (matmul(hidden[half // 2 : half], full_down) + got[half // 2 :].astype(F32)).astype(BF16)
    got_far = exchange(far_sent, "far")
    low = matmul(hidden[: half // 2], full_down) + got[: half // 2].astype(F32)
    grad_both, low, far_sent = tied((grad_both, low, far_sent))
    grad_proj, grad_resid, gain_mlp_part = plane_sum(
        "back", True, grad_both, full_gu, own_cot, resid, gain_mlp, 3, 9 << 33
    )
    grad_proj = grad_proj.reshape(length, model_width)
    grad_proj, got_far, low = tied((grad_proj, got_far, low))
    near_sent = (low[rows:] + got_far[rows:].astype(F32)).astype(BF16)
    got_near = exchange(near_sent, "near")

    grad_w_out = left_inner(mixed, grad_proj).astype(BF16)
    grad_proj, own_down, grad_w_out = tied((grad_proj, own_down, grad_w_out))
    own_out = owned(grad_w_out, 1)
    grad_mixed = matmul(grad_proj, full_out)
    other_down = flip(own_down, 4)
    output = (resid + low[:rows] + got_far[:rows].astype(F32) + got_near.astype(F32)).astype(BF16)
    states, output = tied((states, output))
    output_along = flip(output, 2)
    grads_in, sums, sum_a, sum_x = mixer_back(
        grad_mixed, pre, states, recur, opened, conv, masks, params, diag_a, diag_x, place, rows
    )
    grads_in, output_along, other_down, own_gu = tied((grads_in, output_along, other_down, own_gu))
    lines = jnp.sum(sums.reshape(8, 8, width), axis=1)
    head_at = lax.broadcasted_iota(jnp.int32, (head_width, width), 1) // head_width
    squares = [
        sum(
            jnp.where(head_at == h, part[h * head_width : (h + 1) * head_width], 0.0) for h in range(head_count)
        )
        for part in (sum_a, sum_x)
    ]
    fsdp_size = lax.axis_size("fsdp")
    part_rows = 16 * -(-(8 + 2 * head_width) // (16 * fsdp_size))
    spare = fsdp_size * part_rows - 8 - 2 * head_width
    small = jnp.concatenate([lines] + squares + [jnp.zeros((spare, width), F32)], axis=0).astype(BF16)
    small = small.reshape(fsdp_size, 2, part_rows // 2, width)
    small = jnp.concatenate([small[:, 0], small[:, 1]], axis=2)
    grad_w_in = left_inner(normed, grads_in).astype(BF16).reshape(fsdp_size, -1, 2 * width)
    grad_w_in = jnp.concatenate([grad_w_in, small], axis=1).reshape(-1, 2 * width)
    grads_in, grad_w_in, own_out = tied((grads_in, grad_w_in, own_out))
    own_in = owned(grad_w_in, 0)
    grad_tokens, gain_mix_part, output, own_gate = plane_sum(
        "back", False, grads_in, full_in, grad_resid, own, gain_mix, 4, 5 << 33, (output, output_along, own_gu)
    )
    other_in, smalls, gains, grad_tokens, own_up, own_out = last(
        own_in, gain_mix_part, gain_mlp_part, grad_tokens, own_gu, own_out, model_width // fsdp_size, fsdp_size, 5
    )

    def both_halves(x, other, axis):
        low = jnp.where(half_at == 0, x, other)
        high = jnp.where(half_at == 0, other, x)
        return jnp.concatenate([low, high], axis=axis).astype(F32)

    own_in = own_in[: model_width // fsdp_size]
    own_down = both_halves(own_down, other_down, 0)
    smalls = jnp.stack([smalls[..., :width], smalls[..., width:]], axis=2).reshape(2, fsdp_size * part_rows, width)
    smalls = jnp.concatenate([smalls[0], smalls[1]], axis=1).astype(F32)
    lines = smalls[:8]
    squares = []
    for i in range(2):
        part = smalls[8 + i * head_width : 8 + (i + 1) * head_width]
        squares.append(
            jnp.stack([part[:, h * head_width : (h + 1) * head_width] for h in range(2 * head_count)])
        )
    own_branch = both_halves(own_in[:, :width], other_in[:, :width], 1)
    own_input = both_halves(own_in[:, width:], other_in[:, width:], 1)
    return (
        output.reshape(1, tok_count, model_width),
        grad_tokens.reshape(1, tok_count, model_width),
        gains[0],
        own_branch,
        own_input,
        lines[4:8],
        lines[3],
        squares[0],
        lines[1],
        squares[1],
        lines[2],
        RATE_SCALE * jax.nn.sigmoid(-decay_param) * lines[0],
        own_out.astype(F32),
        gains[1],
        own_gate.astype(F32),
        own_up.astype(F32),
        own_down,
    )


def solution(mesh):
    in_specs = (
        P("fsdp", "ctx", None),
        P("fsdp", None),
        P("fsdp", "ctx", None),
        P(),
        P("fsdp", "tp"),
        P("fsdp", "tp"),
        P(None, "tp"),
        P("tp"),
        P("tp", None, None),
        P("tp"),
        P("tp", None, None),
        P("tp"),
        P("tp"),
        P("tp", "fsdp"),
        P(),
        P("fsdp", "tp"),
        P("fsdp", "tp"),
        P("tp", "fsdp"),
    )
    out_specs = (
        P("fsdp", "ctx", None),
        P("fsdp", "ctx", None),
        P(),
        P("fsdp", "tp"),
        P("fsdp", "tp"),
        P(None, "tp"),
        P("tp"),
        P("tp", None, None),
        P("tp"),
        P("tp", None, None),
        P("tp"),
        P("tp"),
        P("tp", "fsdp"),
        P(),
        P("fsdp", "tp"),
        P("fsdp", "tp"),
        P("tp", "fsdp"),
    )
    return jax.shard_map(shards, mesh=mesh, in_specs=in_specs, out_specs=out_specs, check_vma=False)
```

```python
import functools

import jax
import jax.numpy as jnp
import numpy as np
from jax import lax
from jax.experimental import pallas as pl
from jax.experimental.pallas import tpu as pltpu
from jax.sharding import PartitionSpec as P

EPSILON = 1e-06
RATE_SCALE = 8.0
GELU_C = 0.7978845608028654
GELU_K = 0.044715
GROUP = ("ctx", "tp")
F32, BF16 = jnp.float32, jnp.bfloat16
tied = lax.optimization_barrier


def matmul(left, right):
    return jnp.dot(left, right, preferred_element_type=F32)


def left_inner(left, right):
    return lax.dot_general(left, right, (((0,), (0,)), ((), ())), preferred_element_type=F32)


def right_inner(left, right):
    return lax.dot_general(left, right, (((1,), (1,)), ((), ())), preferred_element_type=F32)


def gelu_parts(v):
    t = jnp.tanh(GELU_C * (v + GELU_K * (v * v * v)))
    half = 0.5 * (1.0 + t)
    slope = half + 0.5 * v * (1.0 - t * t) * (GELU_C * (1.0 + 3.0 * GELU_K * v * v))
    return v * half, slope


def gelu(v):
    return 0.5 * v * (1.0 + jnp.tanh(GELU_C * (v + GELU_K * (v * v * v))))


def one_minus_exp(u):
    series = 1.0 - u * (1.0 / 8.0)
    for n in (7.0, 6.0, 5.0, 4.0, 3.0, 2.0):
        series = 1.0 - u * (1.0 / n) * series
    return jnp.where(u < 0.5, u * series, 1.0 - jnp.exp(-u))


def rms_rows(values):
    return lax.rsqrt(jnp.mean(values * values, axis=-1, keepdims=True) + EPSILON)


def norm_back(grad_norm, scaled, scale_row, gain):
    grad_scaled = grad_norm * gain
    return scale_row * (
        grad_scaled - scaled * jnp.mean(grad_scaled * scaled, axis=-1, keepdims=True)
    )


def step_mask(kind, g):
    core = g % 2
    if kind == "core":
        return 1
    return 2 if (kind == "near") == (core == 0) else 4


def exchange(block, kind):
    pairs = [(g, g ^ step_mask(kind, g)) for g in range(8)]
    return lax.ppermute(block, GROUP, pairs)


def flip(block, mask):
    return lax.ppermute(block, GROUP, [(g, g ^ mask) for g in range(8)])


def place_table():
    table = np.zeros((8, 8), np.int32)
    for g in range(8):
        for spot in range(8):
            at = g ^ (spot >> 2)
            block = at
            if spot & 1:
                block ^= step_mask("near", at)
            if spot & 2:
                block ^= step_mask("far", at)
            table[g, block] = spot
    return table


def reduce_rows(left, right, product):
    half = left.shape[0] // 2
    sent = product(left[half:], right).astype(BF16)
    kept = product(left[:half], right)
    got = exchange(sent, "core")
    kept, got = lax.optimization_barrier((kept, got))
    total = kept + got.astype(F32)
    for kind in ("far", "near"):
        half = half // 2
        got = exchange(total[half:].astype(BF16), kind)
        total = total[:half] + got.astype(F32)
    return total


def partners():
    fsdp, ctx, tp = lax.axis_index("fsdp"), lax.axis_index("ctx"), lax.axis_index("tp")
    core, line = tp % 2, tp // 2
    across = (fsdp, 1 - ctx, tp)
    along = (fsdp, ctx, (1 - line) * 2 + core)
    same = (fsdp, ctx, line * 2 + 1 - core)
    near = (fsdp, ctx + core * (1 - 2 * ctx), (line + (1 - core) * (1 - 2 * line)) * 2 + core)
    far = (fsdp, ctx + (1 - core) * (1 - 2 * ctx), (line + core * (1 - 2 * line)) * 2 + core)
    return core, line, tp, across, along, same, near, far


def meet(*devices):
    barrier = pltpu.get_barrier_semaphore()
    for device in devices:
        pl.semaphore_signal(barrier, inc=1, device_id=device, device_id_type=pl.DeviceIdType.MESH)
    pl.semaphore_wait(barrier, len(devices))


def remote(src, dst, send_sem, recv_sem, device):
    return pltpu.make_async_remote_copy(
        src_ref=src, dst_ref=dst, send_sem=send_sem, recv_sem=recv_sem, device_id=device,
        device_id_type=pl.DeviceIdType.MESH,
    )


def by_rows(count, step, body):
    def turn(i, _):
        body(pl.multiple_of(i * step, step))
        return 0

    lax.fori_loop(0, count // step, turn, 0)


def head_kernel(tokens, cot, gain, normed_out, cot_out, x_buf, n_buf, c_buf, load, store, send, recv):
    rows = x_buf.shape[0] // 4
    core, line, tp, across, along, same, _, _ = partners()
    load_x = pltpu.make_async_copy(tokens, x_buf, load.at[0])
    load_c = pltpu.make_async_copy(cot, c_buf, load.at[1])
    load_x.start()
    load_c.start()
    meet(across, along, same)

    def block(j):
        return pl.ds(pl.multiple_of(j * rows, rows), rows)

    def normalize(j):
        def body(r):
            at = pl.ds(pl.multiple_of(j * rows + r, 32), 32)
            x = x_buf[at, :].astype(F32)
            n_buf[at, :] = (x * rms_rows(x) * gain[...]).astype(BF16)

        by_rows(rows, 32, body)

    load_x.wait()
    normalize(tp)
    outs = (normed_out, cot_out)
    bufs = (n_buf, c_buf)
    first = [
        remote(bufs[i].at[block(tp)], outs[i].at[2 - core], send.at[i], recv.at[i], across) for i in range(2)
    ]
    first[0].start()
    load_c.wait()
    first[1].start()
    for j in range(1, 4):
        normalize((tp + j) % 4)
    kept = []
    for k, (dy, dc) in enumerate(((0, 0), (1, 0), (0, 1), (1, 1))):
        there = line + dy * (1 - 2 * line)
        which = core + dc * (1 - 2 * core)
        effect = which
        spot = 4 * dc + dy * (1 + effect)
        for i in range(2):
            copy = pltpu.make_async_copy(bufs[i].at[block(there * 2 + which)], outs[i].at[spot], store.at[2 * k + i])
            copy.start()
            kept.append(copy)
    later = []
    for i in range(2):
        first[i].wait_recv()
        second = remote(outs[i].at[2 - core], outs[i].at[3], send.at[2 + i], recv.at[2 + i], along)
        second.start()
        third = remote(outs[i].at[2 - core], outs[i].at[6 - core], send.at[4 + i], recv.at[4 + i], same)
        third.start()
        later.append((second, third))
    last = []
    for i in range(2):
        later[i][0].wait_recv()
        fourth = remote(outs[i].at[3], outs[i].at[7], send.at[6 + i], recv.at[6 + i], same)
        fourth.start()
        last.append(fourth)
    for i in range(2):
        later[i][1].wait_recv()
        last[i].wait_recv()
        first[i].wait_send()
        later[i][0].wait_send()
        later[i][1].wait_send()
        last[i].wait_send()
    for copy in kept:
        copy.wait()


def head(tokens, cot, gain, collective_id):
    count, width = tokens.shape
    rows = count // 4
    out = jax.ShapeDtypeStruct((8, rows, width), BF16)
    anywhere = pl.BlockSpec(memory_space=pl.ANY)
    return pl.pallas_call(
        head_kernel,
        in_specs=[anywhere, anywhere, pl.BlockSpec(memory_space=pltpu.VMEM)],
        out_specs=[anywhere, anywhere],
        out_shape=[out, out],
        scratch_shapes=[pltpu.VMEM((count, width), BF16)] * 3
        + [
            pltpu.SemaphoreType.DMA((2,)),
            pltpu.SemaphoreType.DMA((8,)),
            pltpu.SemaphoreType.DMA((8,)),
            pltpu.SemaphoreType.DMA((8,)),
        ],
        compiler_params=pltpu.CompilerParams(
            collective_id=collective_id, has_side_effects=True, vmem_limit_bytes=60 << 20
        ),
        cost_estimate=pl.CostEstimate(flops=5 << 33, bytes_accessed=64 << 20, transcendentals=0),
        name="head",
    )(tokens, cot, gain)


def plane_sum_kernel(
    epilogue, wide, left, right, base, source, gain, *refs
):
    if epilogue == "norm":
        out, kept_out, refs = refs[0], refs[1], refs[2:]
    elif wide:
        out, kept_out, gain_out, refs = refs[0], refs[1], refs[2], refs[3:]
    else:
        rows_in, rows_along, pair, pair_far, stack, stack_far, out, gain_out, rows_out, pair_a, pair_b, stack_out = refs[:12]
        refs = refs[12:]
    to_core, from_core, acc, to_far, from_far, to_near, from_near, own, store, send, recv, gsend, grecv = refs
    rows, width = own.shape
    if not wide:
        own = out
    core, line, tp, across, along, same, near, far = partners()
    meet(same, near, far)
    tile = width // 4

    def products(row, ref, at):
        def turn(i, _):
            cols = pl.ds(pl.multiple_of(i * tile, tile), tile)
            part = right_inner(left[pl.ds(row, 2 * rows), :], right[cols, :])
            ref[pl.ds(at, 2 * rows), cols] = part.astype(ref.dtype)
            return 0

        lax.fori_loop(0, 4, turn, 0)

    def both(a):
        return pl.ds(a * rows, 2 * rows)

    core_copy = [
        remote(to_core.at[both(2 * h)], from_core.at[both(2 * h)], send.at[h], recv.at[h], same) for h in range(2)
    ]
    far_copy = [remote(to_far.at[h], from_far.at[h], send.at[2 + h], recv.at[2 + h], far) for h in range(2)]
    near_copy = remote(to_near, from_near, send.at[4], recv.at[4], near)

    local, carried = [], []
    if not wide:
        came = (1 - line) * 2 + core
        half_at = lax.axis_index("ctx")
        units, tall = pair.shape[1] // 2, stack.shape[0]
        carried = [
            remote(rows_in, rows_out.at[tp], gsend.at[0], grecv.at[0], same),
            remote(rows_along, rows_out.at[came], gsend.at[1], grecv.at[1], same),
        ]
        places = [(rows_in, rows_out.at[tp]), (rows_along, rows_out.at[came])]
        for at, halves, block in ((half_at, pair, stack), (1 - half_at, pair_far, stack_far)):
            cols = pl.ds(pl.multiple_of(at * units, 128), units)
            places.append((halves.at[:, pl.ds(0, units)], pair_a.at[:, cols]))
            places.append((halves.at[:, pl.ds(units, units)], pair_b.at[:, cols]))
            places.append((block, stack_out.at[pl.ds(pl.multiple_of(at * tall, 16), tall), :]))
        local = [pltpu.make_async_copy(src, dst, store.at[i]) for i, (src, dst) in enumerate(places)]
        for copy in local:
            copy.start()

    products(6 * rows, to_core, 2 * rows)
    core_copy[1].start()
    products(2 * rows, acc, 2 * rows)
    core_copy[1].wait_recv()
    for h in (1, 0):
        def body(r, h=h):
            at = pl.ds(pl.multiple_of((2 + h) * rows + r, 32), 32)
            to_far[h, pl.ds(r, 32), :] = (acc[at, :] + from_core[at, :].astype(F32)).astype(BF16)

        by_rows(rows, 32, body)
        far_copy[h].start()
    products(4 * rows, to_core, 0)
    core_copy[0].start()
    products(0, acc, 0)
    core_copy[0].wait_recv()
    far_copy[1].wait_recv()

    def send_near(r):
        at = pl.ds(pl.multiple_of(rows + r, 32), 32)
        total = acc[at, :] + from_core[at, :].astype(F32) + from_far[1, pl.ds(r, 32), :].astype(F32)
        to_near[pl.ds(r, 32), :] = total.astype(BF16)

    by_rows(rows, 32, send_near)
    near_copy.start()
    if not wide:
        carried[0].start()
        carried[1].start()
    far_copy[0].wait_recv()

    def settle(r):
        at = pl.ds(r, 32)
        acc[at, :] = acc[at, :] + from_core[at, :].astype(F32) + from_far[0, at, :].astype(F32)

    by_rows(rows, 32, settle)
    if epilogue != "norm":
        gain_out[...] = jnp.zeros_like(gain_out)
    near_copy.wait_recv()

    def finish(r):
        at = pl.ds(r, 32)
        total = acc[at, :] + from_near[at, :].astype(F32)
        if epilogue == "norm":
            resid = base[at, :].astype(F32) + total
            kept_out[at, :] = resid
            own[at, :] = (resid * rms_rows(resid) * gain[...]).astype(BF16)
        else:
            x = source[at, :].astype(F32)
            scale = rms_rows(x)
            scaled = x * scale
            grad = base[at, :].astype(F32) + norm_back(total, scaled, scale, gain[...])
            gain_out[...] += jnp.sum((total * scaled).reshape(4, 8, width), axis=0)
            if wide:
                kept_out[at, :] = grad
            own[at, :] = grad.astype(BF16)

    by_rows(rows, 32, finish)
    if wide:
        mine = pltpu.make_async_copy(own, out.at[0], store.at[0])
        mine.start()
        copies = [
            remote(own, out.at[1], gsend.at[1], grecv.at[1], near),
            remote(own, out.at[2], gsend.at[2], grecv.at[2], far),
            remote(own, out.at[4], gsend.at[4], grecv.at[4], same),
            remote(out.at[1], out.at[3], gsend.at[3], grecv.at[3], far),
            remote(out.at[1], out.at[5], gsend.at[5], grecv.at[5], same),
            remote(out.at[2], out.at[6], gsend.at[6], grecv.at[6], same),
            remote(out.at[3], out.at[7], gsend.at[7], grecv.at[7], same),
        ]
        for k in range(3):
            copies[k].start()
        copies[0].wait_recv()
        copies[3].start()
        copies[4].start()
        copies[1].wait_recv()
        copies[5].start()
        copies[3].wait_recv()
        copies[6].start()
        for k in (2, 4, 5, 6):
            copies[k].wait_recv()
        local.append(mine)
    else:
        for copy in carried:
            copy.wait_recv()
        copies = carried
    for copy in copies + core_copy + far_copy + [near_copy]:
        copy.wait_send()
    for copy in local:
        copy.wait()


def plane_sum(epilogue, wide, left, right, base, source, gain, collective_id, cost, extra_in=()):
    count, width = left.shape[0], right.shape[0]
    rows = count // 8
    vmem = pl.BlockSpec(memory_space=pltpu.VMEM)
    anywhere = pl.BlockSpec(memory_space=pl.ANY)
    whole = jax.ShapeDtypeStruct((rows, width), F32)
    gains = jax.ShapeDtypeStruct((8, width), F32)
    extra = [whole] if epilogue == "norm" else [whole, gains] if wide else [gains]
    carried = []
    result = jax.ShapeDtypeStruct((8, rows, width), BF16)
    if not wide:
        _, _, pair, _, stack, _ = extra_in
        carried = [(4, rows, width), pair.shape, pair.shape, (2 * stack.shape[0], stack.shape[1])]
        carried = [jax.ShapeDtypeStruct(shape, BF16) for shape in carried]
        result = jax.ShapeDtypeStruct((rows, width), BF16)
    return pl.pallas_call(
        functools.partial(plane_sum_kernel, epilogue, wide),
        in_specs=[vmem] * (5 + len(extra_in)),
        out_specs=[anywhere if wide else vmem] + [vmem] * len(extra) + [anywhere] * len(carried),
        out_shape=[result] + extra + carried,
        scratch_shapes=[
            pltpu.VMEM((4 * rows, width), BF16),
            pltpu.VMEM((4 * rows, width), BF16),
            pltpu.VMEM((4 * rows, width), F32),
            pltpu.VMEM((2, rows, width), BF16),
            pltpu.VMEM((2, rows, width), BF16),
            pltpu.VMEM((rows, width), BF16),
            pltpu.VMEM((rows, width), BF16),
            pltpu.VMEM((rows, width), BF16),
            pltpu.SemaphoreType.DMA((8,)),
            pltpu.SemaphoreType.DMA((5,)),
            pltpu.SemaphoreType.DMA((5,)),
            pltpu.SemaphoreType.DMA((8,)),
            pltpu.SemaphoreType.DMA((8,)),
        ],
        compiler_params=pltpu.CompilerParams(
            collective_id=collective_id, has_side_effects=True, vmem_limit_bytes=62 << 20
        ),
        cost_estimate=pl.CostEstimate(flops=cost, bytes_accessed=count * width, transcendentals=0),
        name="plane_sum",
    )(left, right, base, source, gain, *extra_in)


def last_kernel(
    size, deep, own_in, gain_a, gain_b, rows_in, single, other_in, smalls, gains, rows_out, single_out, plane,
    mine, lines, store, send, recv, small_send, small_recv, plane_send, plane_recv, line_send, line_recv,
):
    thin = smalls.shape[2]
    fsdp, ctx, tp = lax.axis_index("fsdp"), lax.axis_index("ctx"), lax.axis_index("tp")

    def away(dz, dc, dt):
        return (lax.rem(fsdp + dz, size), lax.rem(ctx + dc, 2), lax.rem(tp + dt, 4))

    in_plane = [(0, dc, dt) for dc in range(2) for dt in range(4)][1:]
    across_line = [(dz, dc, 0) for dz in range(size) for dc in range(2)][1:]
    along_line = [(dz, 0, 0) for dz in range(1, size)]
    meet(*[away(*d) for d in in_plane + [d for d in across_line if d not in in_plane]])
    core, row, _, across, along, same, _, _ = partners()
    came = (1 - row) * 2 + core
    tall = single.shape[0]
    tall_rows = pl.ds(pl.multiple_of(ctx * tall, 16), tall)
    copies = [
        remote(own_in.at[pl.ds(0, deep), :], other_in, send.at[0], recv.at[0], across),
        remote(rows_in, rows_out.at[tp], send.at[1], recv.at[1], along),
        remote(rows_in, rows_out.at[tp], send.at[2], recv.at[2], same),
        remote(rows_out.at[came], rows_out.at[came], send.at[3], recv.at[3], same),
        remote(single, single_out.at[tall_rows, :], send.at[4], recv.at[4], across),
    ]
    local = [
        pltpu.make_async_copy(rows_in, rows_out.at[tp], store.at[1]),
        pltpu.make_async_copy(single, single_out.at[tall_rows, :], store.at[2]),
    ]
    for i in (1, 0, 2, 4):
        copies[i].start()
    for copy in local:
        copy.start()
    at = lax.broadcasted_iota(jnp.int32, gains.shape, 0)
    part = jnp.zeros(gains.shape, F32)
    quarter = gains.shape[1]
    for k, gain in enumerate((gain_a, gain_b)):
        for i in range(4):
            line = jnp.sum(gain[:, i * quarter : (i + 1) * quarter], axis=0, keepdims=True)
            part = jnp.where(at == 4 * k + i, line, part)
    place = ctx * 4 + tp
    plane[place] = part
    sent = [
        remote(plane.at[place], plane.at[place], plane_send.at[i], plane_recv.at[i], away(*d))
        for i, d in enumerate(in_plane)
    ]
    for copy in sent:
        copy.start()
    thin_rows = own_in.at[pl.ds(deep, thin), :]
    local.append(pltpu.make_async_copy(thin_rows, smalls.at[ctx, fsdp], store.at[0]))
    local[-1].start()
    for i, d in enumerate(across_line):
        copies.append(remote(thin_rows, smalls.at[ctx, fsdp], small_send.at[i], small_recv.at[i], away(*d)))
        copies[-1].start()
    for copy in sent:
        copy.wait_recv()
    total = plane[0]
    for i in range(1, 8):
        total = total + plane[i]
    mine[...] = total
    lines[fsdp] = total
    further = [
        remote(mine, lines.at[fsdp], line_send.at[i], line_recv.at[i], away(*d)) for i, d in enumerate(along_line)
    ]
    for copy in further:
        copy.start()
    for copy in further:
        copy.wait_recv()
    total = lines[0]
    for i in range(1, size):
        total = total + lines[i]
    gains[...] = total
    copies[1].wait_recv()
    copies[3].start()
    for copy in copies[:1] + copies[2:]:
        copy.wait_recv()
    for copy in copies + sent + further:
        copy.wait_send()
    for copy in local:
        copy.wait()


def last(own_in, gain_a, gain_b, rows, single, deep, size, collective_id):
    width, thin = own_in.shape[1], own_in.shape[0] - deep
    gains = (8, gain_a.shape[1] // 4)
    vmem = pl.BlockSpec(memory_space=pltpu.VMEM)
    anywhere = pl.BlockSpec(memory_space=pl.ANY)
    sems = [pltpu.SemaphoreType.DMA((n,)) for n in (3, 5, 5, 2 * size, 2 * size, 8, 8, size, size)]
    return pl.pallas_call(
        functools.partial(last_kernel, size, deep),
        in_specs=[anywhere] + [vmem] * 4,
        out_specs=[anywhere, anywhere, vmem, anywhere, anywhere],
        out_shape=[
            jax.ShapeDtypeStruct((deep, width), BF16),
            jax.ShapeDtypeStruct((2, size, thin, width), BF16),
            jax.ShapeDtypeStruct(gains, F32),
            jax.ShapeDtypeStruct((4,) + rows.shape, BF16),
            jax.ShapeDtypeStruct((2 * single.shape[0], single.shape[1]), BF16),
        ],
        scratch_shapes=[
            pltpu.VMEM((8,) + gains, F32),
            pltpu.VMEM(gains, F32),
            pltpu.VMEM((size,) + gains, F32),
        ]
        + sems,
        compiler_params=pltpu.CompilerParams(
            collective_id=collective_id, has_side_effects=True, vmem_limit_bytes=32 << 20
        ),
        cost_estimate=pl.CostEstimate(flops=1 << 33, bytes_accessed=4 << 20, transcendentals=0),
        name="last",
    )(own_in, gain_a, gain_b, rows, single)


def scan_rows(a_ref, b_ref, carry, reverse):
    rows, width = b_ref.shape
    groups = rows // 8
    a = a_ref[...].reshape(groups, 8, width)
    b = b_ref[...].reshape(groups, 8, width)
    at = lax.broadcasted_iota(jnp.int32, (groups, 8, width), 1)
    for shift in (1, 2, 4):
        ok = (at < 8 - shift) if reverse else (at >= shift)
        turn = 8 - shift if reverse else shift
        b_before = jnp.where(ok, pltpu.roll(b, turn, 1), 0.0)
        a_before = jnp.where(ok, pltpu.roll(a, turn, 1), 1.0)
        b = a * b_before + b
        a = a * a_before
    a_ref[...] = a.reshape(rows, width)
    b_ref[...] = b.reshape(rows, width)
    for k in range(groups):
        k = groups - 1 - k if reverse else k
        part = pl.ds(8 * k, 8)
        now = b_ref[part, :] + a_ref[part, :] * carry
        b_ref[part, :] = now
        carry = now[0:1, :] if reverse else now[7:8, :]
    return carry


def mixer_kernel(
    place, pre, masks, params, gate_a, gate_x, mixed, states, recur_out, input_out, conv_out, ext, a_buf, b_buf, carry
):
    rows, width = states.shape

    @pl.when(pl.program_id(0) == 0)
    def _():
        ext[...] = jnp.zeros_like(ext)
        carry[...] = jnp.zeros_like(carry)

    ext[0:8, :] = ext[rows : rows + 8, :]
    ext[8:, :] = pre[:, width:].astype(BF16).astype(F32)
    conv = params[4:5, :] + params[0:1, :] * ext[8:, :]
    for k in range(1, 4):
        conv = conv + params[k : k + 1, :] * (masks[:, k - 1 : k] * ext[pl.ds(8 - k, rows), :])
    conv_low = conv.astype(BF16)
    conv_out[...] = conv_low
    conv = conv_low.astype(F32)
    recur = jax.nn.sigmoid(matmul(conv_low, gate_a[...]) + params[5:6, :])
    opened = jax.nn.sigmoid(matmul(conv_low, gate_x[...]) + params[6:7, :])
    recur_out[...] = recur
    input_out[...] = opened
    log_decay = params[7:8, :] * recur
    same = masks[:, 0:1]
    root = jnp.sqrt(one_minus_exp(-2.0 * log_decay))
    a_buf[...] = same * jnp.exp(log_decay)
    b_buf[...] = opened * conv * jnp.where(same > 0.5, root, 1.0)
    carry[0:1, :] = scan_rows(a_buf, b_buf, carry[0:1, :], False)
    state = b_buf[...]
    states[...] = state
    mixed[...] = (state * gelu(pre[:, :width])).astype(BF16)


def mixer_back_kernel(
    place, grad_proj, w_out, pre, pre_tail, states, states_tail, recur_in, input_in, conv_in, masks, params, gate_a, gate_x,
    grads, sums, sum_a, sum_x, ext, grad_ext, a_buf, b_buf, carry,
):
    rows, width = states.shape
    step = pl.program_id(0)
    first = step == pl.num_programs(0) - 1

    @pl.when(step == 0)
    def _():
        grad_ext[...] = jnp.zeros_like(grad_ext)
        carry[...] = jnp.zeros_like(carry)
        sums[...] = jnp.zeros_like(sums)
        sum_a[...] = jnp.zeros_like(sum_a)
        sum_x[...] = jnp.zeros_like(sum_x)

    inside = jnp.where(first, 0.0, 1.0)
    branch, slope = gelu_parts(pre[:, :width])
    above = matmul(grad_proj[...], w_out[...])
    state = states[...]
    grads[:, :width] = (above * state * slope).astype(BF16)
    recur, opened = recur_in[...], input_in[...]
    conv_low = conv_in[...]
    conv = conv_low.astype(F32)
    same = masks[:, 0:1]
    rate = params[7:8, :]
    log_decay = rate * recur
    decay = jnp.exp(log_decay)
    root = jnp.sqrt(one_minus_exp(-2.0 * log_decay))
    mult = jnp.where(same > 0.5, root, 1.0)
    a_buf[0:rows, :] = same * decay
    head = a_buf[0:1, :]
    a_buf[rows : rows + 8, :] = jnp.broadcast_to(carry[1:2, :], (8, width))
    factor = a_buf[pl.ds(1, rows), :]
    a_buf[0:rows, :] = factor
    b_buf[...] = above * branch
    new_carry = scan_rows(a_buf.at[pl.ds(0, rows), :], b_buf, carry[0:1, :], True)
    carry[0:1, :] = new_carry
    carry[1:2, :] = head
    total = b_buf[...]
    ext[0:8, :] = inside * states_tail[...]
    ext[8:, :] = state
    before = ext[pl.ds(7, rows), :]
    grad_open = total * opened
    grad_log = jnp.where(
        same > 0.5, total * before * decay - grad_open * conv * decay * decay / root, 0.0
    )

    def fold(x):
        return jnp.sum(x.reshape(rows // 8, 8, width), axis=0)

    sums[0:8, :] += fold(grad_log * recur)
    low_a = (grad_log * rate * recur * (1.0 - recur)).astype(BF16)
    low_x = (total * conv * mult * opened * (1.0 - opened)).astype(BF16)
    sums[8:16, :] += fold(low_a.astype(F32))
    sums[16:24, :] += fold(low_x.astype(F32))
    sum_a[...] += left_inner(conv_low, low_a)
    sum_x[...] += left_inner(conv_low, low_x)
    grad_conv = grad_open * mult + (
        right_inner(low_a, gate_a[...]) + right_inner(low_x, gate_x[...])
    )
    sums[24:32, :] += fold(grad_conv)
    ext[0:8, :] = inside * pre_tail[:, width:].astype(BF16).astype(F32)
    ext[8:, :] = pre[:, width:].astype(BF16).astype(F32)
    grad_ext[rows : rows + 8, :] = grad_ext[0:8, :]
    grad_ext[0:rows, :] = grad_conv
    grad_in = params[0:1, :] * grad_conv
    sums[32:40, :] += fold(grad_conv * ext[8:, :])
    for k in range(1, 4):
        earlier = masks[:, k - 1 : k] * ext[pl.ds(8 - k, rows), :]
        sums[32 + 8 * k : 40 + 8 * k, :] += fold(grad_conv * earlier)
        grad_in = grad_in + params[k : k + 1, :] * (
            masks[:, k + 2 : k + 3] * grad_ext[pl.ds(k, rows), :]
        )
    grads[:, width:] = grad_in.astype(BF16)


def mixer(pre, masks, params, gate_a, gate_x, place, rows):
    count, width = pre.shape[0], pre.shape[1] // 2
    steps = count // rows
    spot = lambda i, place: (place[i], 0)
    inorder = lambda i, place: (i, 0)
    fixed = lambda i, place: (0, 0)
    wide = pl.BlockSpec((rows, 2 * width), spot)
    one = pl.BlockSpec((rows, width), spot)
    gate = pl.BlockSpec((width, width), fixed)
    return pl.pallas_call(
        mixer_kernel,
        grid_spec=pltpu.PrefetchScalarGridSpec(
            num_scalar_prefetch=1,
            grid=(steps,),
            in_specs=[wide, pl.BlockSpec((rows, 8), inorder), pl.BlockSpec((8, width), fixed), gate, gate],
            out_specs=[one] * 5,
            scratch_shapes=[
                pltpu.VMEM((rows + 8, width), F32),
                pltpu.VMEM((rows, width), F32),
                pltpu.VMEM((rows, width), F32),
                pltpu.VMEM((8, width), F32),
            ],
        ),
        out_shape=[
            jax.ShapeDtypeStruct((count, width), kind) for kind in (BF16, F32, F32, F32, BF16)
        ],
        cost_estimate=pl.CostEstimate(
            flops=count * width * (4 * width + 120), bytes_accessed=count * width * 24, transcendentals=count * width * 6
        ),
        name="mixer",
    )(place, pre, masks, params, gate_a, gate_x)


def mixer_back(grad_proj, w_out, pre, states, recur, opened, conv, masks, params, gate_a, gate_x, place, rows):
    count, width = states.shape
    steps = count // rows
    last = steps - 1
    spot = lambda i, place: (place[last - i], 0)
    inorder = lambda i, place: (last - i, 0)
    fixed = lambda i, place: (0, 0)

    def tail(i, place):
        return (place[jnp.maximum(last - i - 1, 0)] * (rows // 8) + rows // 8 - 1, 0)

    wide = pl.BlockSpec((rows, 2 * width), spot)
    one = pl.BlockSpec((rows, width), spot)
    gate = pl.BlockSpec((width, width), fixed)
    return pl.pallas_call(
        mixer_back_kernel,
        grid_spec=pltpu.PrefetchScalarGridSpec(
            num_scalar_prefetch=1,
            grid=(steps,),
            in_specs=[
                pl.BlockSpec((rows, grad_proj.shape[1]), spot), pl.BlockSpec(w_out.shape, fixed),
                wide, pl.BlockSpec((8, 2 * width), tail), one, pl.BlockSpec((8, width), tail), one, one, one,
                pl.BlockSpec((rows, 8), inorder), pl.BlockSpec((8, width), fixed), gate, gate,
            ],
            out_specs=[wide, pl.BlockSpec((64, width), fixed), gate, gate],
            scratch_shapes=[
                pltpu.VMEM((rows + 8, width), F32),
                pltpu.VMEM((rows + 8, width), F32),
                pltpu.VMEM((rows + 8, width), F32),
                pltpu.VMEM((rows, width), F32),
                pltpu.VMEM((8, width), F32),
            ],
        ),
        out_shape=[
            jax.ShapeDtypeStruct((count, 2 * width), BF16),
            jax.ShapeDtypeStruct((64, width), F32),
            jax.ShapeDtypeStruct((width, width), F32),
            jax.ShapeDtypeStruct((width, width), F32),
        ],
        cost_estimate=pl.CostEstimate(
            flops=count * width * (8 * width + 2 * grad_proj.shape[1] + 200), bytes_accessed=count * width * 34, transcendentals=count * width * 4
        ),
        name="mixer_back",
    )(place, grad_proj, w_out, pre, pre, states, states, recur, opened, conv, masks, params, gate_a, gate_x)


def on_diagonal(blocks):
    heads, size = blocks.shape[0], blocks.shape[1]
    out = jnp.zeros((heads * size, heads * size), blocks.dtype)
    for h in range(heads):
        out = lax.dynamic_update_slice(out, blocks[h], (h * size, h * size))
    return out


def shards(
    tokens, segments, cotangent, gain_mix, w_branch, w_input, conv_weight, conv_bias, gate_a, bias_a, gate_x, bias_x,
    decay_param, w_out, gain_mlp, w_gate, w_up, w_down,
):
    half_at = lax.axis_index("ctx")
    place_tp = lax.axis_index("tp")

    def mine(x, axis):
        size = x.shape[axis] // 2
        return lax.dynamic_slice_in_dim(x, half_at * size, size, axis)

    def owned(x, axis):
        return lax.psum_scatter(x, "fsdp", scatter_dimension=axis, tiled=True)

    _, tok_count, model_width = tokens.shape
    rows = tok_count // 4
    length = 2 * tok_count
    own_in = jnp.concatenate([mine(w_branch, 1), mine(w_input, 1), mine(w_out, 0).T], axis=1)
    full_mix = lax.all_gather(own_in, "fsdp", axis=0, tiled=True)
    own_gu = jnp.concatenate([mine(w_gate, 1), mine(w_up, 1)], axis=1)
    full_gu = lax.all_gather(own_gu, "fsdp", axis=0, tiled=True)
    full_down = lax.all_gather(mine(w_down, 0), "fsdp", axis=1, tiled=True)

    width = own_in.shape[1] // 3
    full_in, full_out = full_mix[:, : 2 * width], full_mix[:, 2 * width :]
    units = own_gu.shape[1] // 2
    place = jnp.asarray(place_table())[half_at * 4 + place_tp]

    rate = -RATE_SCALE * jax.nn.softplus(-decay_param)
    params = jnp.concatenate(
        [
            mine(conv_weight, 1),
            jnp.stack([mine(v, 0) for v in (conv_bias, bias_a, bias_x, rate)]),
        ],
        axis=0,
    )
    heads_a, heads_x = mine(gate_a, 0), mine(gate_x, 0)
    head_count, head_width = heads_a.shape[0], heads_a.shape[1]
    diag_a, diag_x = on_diagonal(heads_a), on_diagonal(heads_x)
    seg = segments[0]
    around = jnp.pad(seg, (3, 3), constant_values=-1)
    marks = [around[3 - k : 3 - k + length] == seg for k in (1, 2, 3)]
    marks += [around[3 + k : 3 + k + length] == seg for k in (1, 2, 3)]
    marks += [jnp.zeros_like(marks[0])] * 2
    masks = jnp.stack(marks, axis=1).astype(F32)

    own = lax.dynamic_slice_in_dim(tokens[0], place_tp * rows, rows, 0)
    own_cot = lax.dynamic_slice_in_dim(cotangent[0], place_tp * rows, rows, 0)
    gain_mix, gain_mlp = gain_mix[None], gain_mlp[None]
    normed, cot = head(tokens[0], cotangent[0], gain_mix, 1)
    normed, cot = normed.reshape(length, model_width), cot.reshape(length, model_width)

    pre = matmul(normed, full_in)
    mixed, states, recur, opened, conv = mixer(pre, masks, params, diag_a, diag_x, place, rows)
    normed_mlp, resid = plane_sum("norm", True, mixed, full_out, own, own, gain_mlp, 2, 9 << 33)
    normed_mlp = normed_mlp.reshape(length, model_width)

    both = matmul(normed_mlp, full_gu)
    gate_pre, up_pre = both[:, :units], both[:, units:]
    gate_act, gate_slope = gelu_parts(gate_pre)
    hidden = (gate_act * up_pre).astype(BF16)
    grad_w_down = left_inner(hidden, cot).astype(BF16)
    full_down, grad_w_down, hidden, full_in, own_cot = tied((full_down, grad_w_down, hidden, full_in, own_cot))
    own_down = owned(grad_w_down, 1)

    grad_hidden = right_inner(cot, full_down)
    grad_both = jnp.concatenate(
        [
            (grad_hidden * up_pre * gate_slope).astype(BF16),
            (grad_hidden * gate_act).astype(BF16),
        ],
        axis=1,
    )
    grad_w_gu = left_inner(normed_mlp, grad_both).astype(BF16)
    half = length // 2
    sent = matmul(hidden[half:], full_down).astype(BF16)
    grad_w_gu, sent = tied((grad_w_gu, sent))
    own_gu = owned(grad_w_gu, 0)
    got = exchange(sent, "core")
    grad_both, got, grad_w_gu = tied((grad_both, got, grad_w_gu))
    far_sent = (matmul(hidden[half // 2 : half], full_down) + got[half // 2 :].astype(F32)).astype(BF16)
    got_far = exchange(far_sent, "far")
    low = matmul(hidden[: half // 2], full_down) + got[: half // 2].astype(F32)
    grad_both, low, far_sent = tied((grad_both, low, far_sent))
    grad_proj, grad_resid, gain_mlp_part = plane_sum(
        "back", True, grad_both, full_gu, own_cot, resid, gain_mlp, 3, 9 << 33
    )
    grad_proj = grad_proj.reshape(length, model_width)
    grad_proj, got_far, low = tied((grad_proj, got_far, low))
    near_sent = (low[rows:] + got_far[rows:].astype(F32)).astype(BF16)
    got_near = exchange(near_sent, "near")

    grad_w_out = left_inner(mixed, grad_proj).astype(BF16)
    grad_proj, own_down, grad_w_out = tied((grad_proj, own_down, grad_w_out))
    own_out = owned(grad_w_out, 1)
    other_down = flip(own_down, 4)
    low, own_gu, grad_w_out = tied((low, own_gu, grad_w_out))
    other_gu = flip(own_gu, 4)
    output = (resid + low[:rows] + got_far[:rows].astype(F32) + got_near.astype(F32)).astype(BF16)
    states, output = tied((states, output))
    output_along = flip(output, 2)
    grads_in, sums, sum_a, sum_x = mixer_back(
        grad_proj, full_out, pre, states, recur, opened, conv, masks, params, diag_a, diag_x, place, rows
    )
    grads_in, output_along, other_down = tied((grads_in, output_along, other_down))
    lines = jnp.sum(sums.reshape(8, 8, width), axis=1)
    head_at = lax.broadcasted_iota(jnp.int32, (head_width, width), 1) // head_width
    squares = [
        sum(
            jnp.where(head_at == h, part[h * head_width : (h + 1) * head_width], 0.0) for h in range(head_count)
        )
        for part in (sum_a, sum_x)
    ]
    fsdp_size = lax.axis_size("fsdp")
    part_rows = 16 * -(-(8 + 2 * head_width) // (16 * fsdp_size))
    spare = fsdp_size * part_rows - 8 - 2 * head_width
    small = jnp.concatenate([lines] + squares + [jnp.zeros((spare, width), F32)], axis=0).astype(BF16)
    small = small.reshape(fsdp_size, 2, part_rows // 2, width)
    small = jnp.concatenate([small[:, 0], small[:, 1]], axis=2)
    grad_w_in = left_inner(normed, grads_in).astype(BF16).reshape(fsdp_size, -1, 2 * width)
    grad_w_in = jnp.concatenate([grad_w_in, small], axis=1).reshape(-1, 2 * width)
    grads_in, grad_w_in, own_out, other_gu = tied((grads_in, grad_w_in, own_out, other_gu))
    own_in = owned(grad_w_in, 0)
    moved = (output, output_along, own_gu, other_gu, own_down, other_down)
    grad_tokens, gain_mix_part, output, own_gate, own_up, own_down = plane_sum(
        "back", False, grads_in, full_in, grad_resid, own, gain_mix, 4, 5 << 33, moved
    )
    other_in, smalls, gains, grad_tokens, own_out = last(
        own_in, gain_mix_part, gain_mlp_part, grad_tokens, own_out, model_width // fsdp_size, fsdp_size, 5
    )

    def both_halves(x, other, axis):
        low = jnp.where(half_at == 0, x, other)
        high = jnp.where(half_at == 0, other, x)
        return jnp.concatenate([low, high], axis=axis).astype(F32)

    own_in = own_in[: model_width // fsdp_size]
    smalls = jnp.stack([smalls[..., :width], smalls[..., width:]], axis=2).reshape(2, fsdp_size * part_rows, width)
    smalls = jnp.concatenate([smalls[0], smalls[1]], axis=1).astype(F32)
    lines = smalls[:8]
    squares = []
    for i in range(2):
        part = smalls[8 + i * head_width : 8 + (i + 1) * head_width]
        squares.append(
            jnp.stack([part[:, h * head_width : (h + 1) * head_width] for h in range(2 * head_count)])
        )
    own_branch = both_halves(own_in[:, :width], other_in[:, :width], 1)
    own_input = both_halves(own_in[:, width:], other_in[:, width:], 1)
    return (
        output.reshape(1, tok_count, model_width),
        grad_tokens.reshape(1, tok_count, model_width),
        gains[:4].reshape(model_width),
        own_branch,
        own_input,
        lines[4:8],
        lines[3],
        squares[0],
        lines[1],
        squares[1],
        lines[2],
        RATE_SCALE * jax.nn.sigmoid(-decay_param) * lines[0],
        own_out.astype(F32),
        gains[4:].reshape(model_width),
        own_gate.astype(F32),
        own_up.astype(F32),
        own_down.astype(F32),
    )


def solution(mesh):
    in_specs = (
        P("fsdp", "ctx", None),
        P("fsdp", None),
        P("fsdp", "ctx", None),
        P(),
        P("fsdp", "tp"),
        P("fsdp", "tp"),
        P(None, "tp"),
        P("tp"),
        P("tp", None, None),
        P("tp"),
        P("tp", None, None),
        P("tp"),
        P("tp"),
        P("tp", "fsdp"),
        P(),
        P("fsdp", "tp"),
        P("fsdp", "tp"),
        P("tp", "fsdp"),
    )
    out_specs = (
        P("fsdp", "ctx", None),
        P("fsdp", "ctx", None),
        P(),
        P("fsdp", "tp"),
        P("fsdp", "tp"),
        P(None, "tp"),
        P("tp"),
        P("tp", None, None),
        P("tp"),
        P("tp", None, None),
        P("tp"),
        P("tp"),
        P("tp", "fsdp"),
        P(),
        P("fsdp", "tp"),
        P("fsdp", "tp"),
        P("tp", "fsdp"),
    )
    return jax.shard_map(shards, mesh=mesh, in_specs=in_specs, out_specs=out_specs, check_vma=False)
```

```python
import functools

import jax
import jax.numpy as jnp
import numpy as np
from jax import lax
from jax.experimental import pallas as pl
from jax.experimental.pallas import tpu as pltpu
from jax.sharding import PartitionSpec as P

EPSILON = 1e-06
RATE_SCALE = 8.0
GELU_C = 0.7978845608028654
GELU_K = 0.044715
GROUP = ("ctx", "tp")
F32, BF16 = jnp.float32, jnp.bfloat16
tied = lax.optimization_barrier


def matmul(left, right):
    return jnp.dot(left, right, preferred_element_type=F32)


def left_inner(left, right):
    return lax.dot_general(left, right, (((0,), (0,)), ((), ())), preferred_element_type=F32)


def right_inner(left, right):
    return lax.dot_general(left, right, (((1,), (1,)), ((), ())), preferred_element_type=F32)


def gelu_parts(v):
    t = jnp.tanh(GELU_C * (v + GELU_K * (v * v * v)))
    half = 0.5 * (1.0 + t)
    slope = half + 0.5 * v * (1.0 - t * t) * (GELU_C * (1.0 + 3.0 * GELU_K * v * v))
    return v * half, slope


def gelu(v):
    return 0.5 * v * (1.0 + jnp.tanh(GELU_C * (v + GELU_K * (v * v * v))))


def one_minus_exp(u):
    series = 1.0 - u * (1.0 / 8.0)
    for n in (7.0, 6.0, 5.0, 4.0, 3.0, 2.0):
        series = 1.0 - u * (1.0 / n) * series
    return jnp.where(u < 0.5, u * series, 1.0 - jnp.exp(-u))


def rms_rows(values):
    return lax.rsqrt(jnp.mean(values * values, axis=-1, keepdims=True) + EPSILON)


def norm_back(grad_norm, scaled, scale_row, gain):
    grad_scaled = grad_norm * gain
    return scale_row * (
        grad_scaled - scaled * jnp.mean(grad_scaled * scaled, axis=-1, keepdims=True)
    )


def step_mask(kind, g):
    core = g % 2
    if kind == "core":
        return 1
    return 2 if (kind == "near") == (core == 0) else 4


def exchange(block, kind):
    pairs = [(g, g ^ step_mask(kind, g)) for g in range(8)]
    return lax.ppermute(block, GROUP, pairs)


def flip(block, mask):
    return lax.ppermute(block, GROUP, [(g, g ^ mask) for g in range(8)])


def place_table():
    table = np.zeros((8, 8), np.int32)
    for g in range(8):
        for spot in range(8):
            at = g ^ (spot >> 2)
            block = at
            if spot & 1:
                block ^= step_mask("near", at)
            if spot & 2:
                block ^= step_mask("far", at)
            table[g, block] = spot
    return table


def reduce_rows(left, right, product):
    half = left.shape[0] // 2
    sent = product(left[half:], right).astype(BF16)
    kept = product(left[:half], right)
    got = exchange(sent, "core")
    kept, got = lax.optimization_barrier((kept, got))
    total = kept + got.astype(F32)
    for kind in ("far", "near"):
        half = half // 2
        got = exchange(total[half:].astype(BF16), kind)
        total = total[:half] + got.astype(F32)
    return total


def partners():
    fsdp, ctx, tp = lax.axis_index("fsdp"), lax.axis_index("ctx"), lax.axis_index("tp")
    core, line = tp % 2, tp // 2
    across = (fsdp, 1 - ctx, tp)
    along = (fsdp, ctx, (1 - line) * 2 + core)
    same = (fsdp, ctx, line * 2 + 1 - core)
    near = (fsdp, ctx + core * (1 - 2 * ctx), (line + (1 - core) * (1 - 2 * line)) * 2 + core)
    far = (fsdp, ctx + (1 - core) * (1 - 2 * ctx), (line + core * (1 - 2 * line)) * 2 + core)
    return core, line, tp, across, along, same, near, far


def meet(*devices):
    barrier = pltpu.get_barrier_semaphore()
    for device in devices:
        pl.semaphore_signal(barrier, inc=1, device_id=device, device_id_type=pl.DeviceIdType.MESH)
    pl.semaphore_wait(barrier, len(devices))


def remote(src, dst, send_sem, recv_sem, device):
    return pltpu.make_async_remote_copy(
        src_ref=src, dst_ref=dst, send_sem=send_sem, recv_sem=recv_sem, device_id=device,
        device_id_type=pl.DeviceIdType.MESH,
    )


def by_rows(count, step, body):
    def turn(i, _):
        body(pl.multiple_of(i * step, step))
        return 0

    lax.fori_loop(0, count // step, turn, 0)


def head_kernel(tokens, cot, gain, normed_out, cot_out, x_buf, n_buf, c_buf, load, store, send, recv):
    rows = x_buf.shape[0] // 4
    core, line, tp, across, along, same, _, _ = partners()
    load_x = pltpu.make_async_copy(tokens, x_buf, load.at[0])
    load_c = pltpu.make_async_copy(cot, c_buf, load.at[1])
    load_x.start()
    load_c.start()
    meet(across, along, same)

    def block(j):
        return pl.ds(pl.multiple_of(j * rows, rows), rows)

    def normalize(j):
        def body(r):
            at = pl.ds(pl.multiple_of(j * rows + r, 32), 32)
            x = x_buf[at, :].astype(F32)
            n_buf[at, :] = (x * rms_rows(x) * gain[...]).astype(BF16)

        by_rows(rows, 32, body)

    load_x.wait()
    normalize(tp)
    outs = (normed_out, cot_out)
    bufs = (n_buf, c_buf)
    first = [
        remote(bufs[i].at[block(tp)], outs[i].at[2 - core], send.at[i], recv.at[i], across) for i in range(2)
    ]
    first[0].start()
    load_c.wait()
    first[1].start()
    for j in range(1, 4):
        normalize((tp + j) % 4)
    kept = []
    for k, (dy, dc) in enumerate(((0, 0), (1, 0), (0, 1), (1, 1))):
        there = line + dy * (1 - 2 * line)
        which = core + dc * (1 - 2 * core)
        effect = which
        spot = 4 * dc + dy * (1 + effect)
        for i in range(2):
            copy = pltpu.make_async_copy(bufs[i].at[block(there * 2 + which)], outs[i].at[spot], store.at[2 * k + i])
            copy.start()
            kept.append(copy)
    later = []
    for i in range(2):
        first[i].wait_recv()
        second = remote(outs[i].at[2 - core], outs[i].at[3], send.at[2 + i], recv.at[2 + i], along)
        second.start()
        third = remote(outs[i].at[2 - core], outs[i].at[6 - core], send.at[4 + i], recv.at[4 + i], same)
        third.start()
        later.append((second, third))
    last = []
    for i in range(2):
        later[i][0].wait_recv()
        fourth = remote(outs[i].at[3], outs[i].at[7], send.at[6 + i], recv.at[6 + i], same)
        fourth.start()
        last.append(fourth)
    for i in range(2):
        later[i][1].wait_recv()
        last[i].wait_recv()
        first[i].wait_send()
        later[i][0].wait_send()
        later[i][1].wait_send()
        last[i].wait_send()
    for copy in kept:
        copy.wait()


def head(tokens, cot, gain, collective_id):
    count, width = tokens.shape
    rows = count // 4
    out = jax.ShapeDtypeStruct((8, rows, width), BF16)
    anywhere = pl.BlockSpec(memory_space=pl.ANY)
    return pl.pallas_call(
        head_kernel,
        in_specs=[anywhere, anywhere, pl.BlockSpec(memory_space=pltpu.VMEM)],
        out_specs=[anywhere, anywhere],
        out_shape=[out, out],
        scratch_shapes=[pltpu.VMEM((count, width), BF16)] * 3
        + [
            pltpu.SemaphoreType.DMA((2,)),
            pltpu.SemaphoreType.DMA((8,)),
            pltpu.SemaphoreType.DMA((8,)),
            pltpu.SemaphoreType.DMA((8,)),
        ],
        compiler_params=pltpu.CompilerParams(
            collective_id=collective_id, has_side_effects=True, vmem_limit_bytes=60 << 20
        ),
        cost_estimate=pl.CostEstimate(flops=5 << 33, bytes_accessed=64 << 20, transcendentals=0),
        name="head",
    )(tokens, cot, gain)


def plane_sum_kernel(
    epilogue, wide, parts, *refs
):
    lefts, (right, base, source, gain), refs = refs[:parts], refs[parts : parts + 4], refs[parts + 4 :]
    if epilogue == "norm":
        out, kept_out, refs = refs[0], refs[1], refs[2:]
    elif wide:
        out, kept_out, gain_out, refs = refs[0], refs[1], refs[2], refs[3:]
    else:
        rows_in, rows_along, pair, pair_far, stack, stack_far, single = refs[:7]
        out, gain_out, rows_out, pair_a, pair_b, stack_out, single_out = refs[7:14]
        refs = refs[14:]
    to_core, from_core, acc, to_far, from_far, to_near, from_near, own, store, send, recv, gsend, grecv = refs
    rows, width = own.shape
    if not wide:
        own = out
    core, line, tp, across, along, same, near, far = partners()
    meet(same, near, far)
    tile = width // 4

    def products(row, ref, at):
        def turn(i, _):
            cols = pl.ds(pl.multiple_of(i * tile, tile), tile)
            part, start = 0.0, 0
            for left in lefts:
                part = part + right_inner(left[pl.ds(row, 2 * rows), :], right[cols, start : start + left.shape[1]])
                start += left.shape[1]
            ref[pl.ds(at, 2 * rows), cols] = part.astype(ref.dtype)
            return 0

        lax.fori_loop(0, 4, turn, 0)

    def both(a):
        return pl.ds(a * rows, 2 * rows)

    core_copy = [
        remote(to_core.at[both(2 * h)], from_core.at[both(2 * h)], send.at[h], recv.at[h], same) for h in range(2)
    ]
    far_copy = [remote(to_far.at[h], from_far.at[h], send.at[2 + h], recv.at[2 + h], far) for h in range(2)]
    near_copy = remote(to_near, from_near, send.at[4], recv.at[4], near)

    local, carried = [], []
    if not wide:
        came = (1 - line) * 2 + core
        half_at = lax.axis_index("ctx")
        units, tall = pair.shape[1] // 2, stack.shape[0]
        carried = [
            remote(rows_in, rows_out.at[tp], gsend.at[0], grecv.at[0], same),
            remote(rows_along, rows_out.at[came], gsend.at[1], grecv.at[1], same),
        ]
        single_rows = pl.ds(pl.multiple_of(half_at * single.shape[0], 16), single.shape[0])
        carried.append(remote(single, single_out.at[single_rows, :], gsend.at[2], grecv.at[2], across))
        carried[2].start()
        places = [(rows_in, rows_out.at[tp]), (rows_along, rows_out.at[came]), (single, single_out.at[single_rows, :])]
        for at, halves, block in ((half_at, pair, stack), (1 - half_at, pair_far, stack_far)):
            cols = pl.ds(pl.multiple_of(at * units, 128), units)
            places.append((halves.at[:, pl.ds(0, units)], pair_a.at[:, cols]))
            places.append((halves.at[:, pl.ds(units, units)], pair_b.at[:, cols]))
            places.append((block, stack_out.at[pl.ds(pl.multiple_of(at * tall, 16), tall), :]))
        local = [pltpu.make_async_copy(src, dst, store.at[i]) for i, (src, dst) in enumerate(places)]
        for copy in local:
            copy.start()

    products(6 * rows, to_core, 2 * rows)
    core_copy[1].start()
    products(2 * rows, acc, 2 * rows)
    core_copy[1].wait_recv()
    for h in (1, 0):
        def body(r, h=h):
            at = pl.ds(pl.multiple_of((2 + h) * rows + r, 32), 32)
            to_far[h, pl.ds(r, 32), :] = (acc[at, :] + from_core[at, :].astype(F32)).astype(BF16)

        by_rows(rows, 32, body)
        far_copy[h].start()
    products(4 * rows, to_core, 0)
    core_copy[0].start()
    products(0, acc, 0)
    core_copy[0].wait_recv()
    far_copy[1].wait_recv()

    def send_near(r):
        at = pl.ds(pl.multiple_of(rows + r, 32), 32)
        total = acc[at, :] + from_core[at, :].astype(F32) + from_far[1, pl.ds(r, 32), :].astype(F32)
        to_near[pl.ds(r, 32), :] = total.astype(BF16)

    by_rows(rows, 32, send_near)
    near_copy.start()
    if not wide:
        carried[0].start()
        carried[1].start()
    far_copy[0].wait_recv()

    def settle(r):
        at = pl.ds(r, 32)
        acc[at, :] = acc[at, :] + from_core[at, :].astype(F32) + from_far[0, at, :].astype(F32)

    by_rows(rows, 32, settle)
    if epilogue != "norm":
        gain_out[...] = jnp.zeros_like(gain_out)
    near_copy.wait_recv()

    def finish(r):
        at = pl.ds(r, 32)
        total = acc[at, :] + from_near[at, :].astype(F32)
        if epilogue == "norm":
            resid = base[at, :].astype(F32) + total
            kept_out[at, :] = resid
            own[at, :] = (resid * rms_rows(resid) * gain[...]).astype(BF16)
        else:
            x = source[at, :].astype(F32)
            scale = rms_rows(x)
            scaled = x * scale
            grad = base[at, :].astype(F32) + norm_back(total, scaled, scale, gain[...])
            gain_out[...] += jnp.sum((total * scaled).reshape(4, 8, width), axis=0)
            if wide:
                kept_out[at, :] = grad
            own[at, :] = grad.astype(BF16)

    by_rows(rows, 32, finish)
    if wide:
        mine = pltpu.make_async_copy(own, out.at[0], store.at[0])
        mine.start()
        copies = [
            remote(own, out.at[1], gsend.at[1], grecv.at[1], near),
            remote(own, out.at[2], gsend.at[2], grecv.at[2], far),
            remote(own, out.at[4], gsend.at[4], grecv.at[4], same),
            remote(out.at[1], out.at[3], gsend.at[3], grecv.at[3], far),
            remote(out.at[1], out.at[5], gsend.at[5], grecv.at[5], same),
            remote(out.at[2], out.at[6], gsend.at[6], grecv.at[6], same),
            remote(out.at[3], out.at[7], gsend.at[7], grecv.at[7], same),
        ]
        for k in range(3):
            copies[k].start()
        copies[0].wait_recv()
        copies[3].start()
        copies[4].start()
        copies[1].wait_recv()
        copies[5].start()
        copies[3].wait_recv()
        copies[6].start()
        for k in (2, 4, 5, 6):
            copies[k].wait_recv()
        local.append(mine)
    else:
        for copy in carried:
            copy.wait_recv()
        copies = carried
    for copy in copies + core_copy + far_copy + [near_copy]:
        copy.wait_send()
    for copy in local:
        copy.wait()


def plane_sum(epilogue, wide, lefts, right, base, source, gain, collective_id, cost, extra_in=()):
    count, width = lefts[0].shape[0], right.shape[0]
    rows = count // 8
    vmem = pl.BlockSpec(memory_space=pltpu.VMEM)
    anywhere = pl.BlockSpec(memory_space=pl.ANY)
    whole = jax.ShapeDtypeStruct((rows, width), F32)
    gains = jax.ShapeDtypeStruct((8, width), F32)
    extra = [whole] if epilogue == "norm" else [whole, gains] if wide else [gains]
    carried = []
    result = jax.ShapeDtypeStruct((8, rows, width), BF16)
    if not wide:
        _, _, pair, _, stack, _, single = extra_in
        carried = [(4, rows, width), pair.shape, pair.shape]
        carried += [(2 * block.shape[0], block.shape[1]) for block in (stack, single)]
        carried = [jax.ShapeDtypeStruct(shape, BF16) for shape in carried]
        result = jax.ShapeDtypeStruct((rows, width), BF16)
    return pl.pallas_call(
        functools.partial(plane_sum_kernel, epilogue, wide, len(lefts)),
        in_specs=[vmem] * (len(lefts) + 4 + len(extra_in)),
        out_specs=[anywhere if wide else vmem] + [vmem] * len(extra) + [anywhere] * len(carried),
        out_shape=[result] + extra + carried,
        scratch_shapes=[
            pltpu.VMEM((4 * rows, width), BF16),
            pltpu.VMEM((4 * rows, width), BF16),
            pltpu.VMEM((4 * rows, width), F32),
            pltpu.VMEM((2, rows, width), BF16),
            pltpu.VMEM((2, rows, width), BF16),
            pltpu.VMEM((rows, width), BF16),
            pltpu.VMEM((rows, width), BF16),
            pltpu.VMEM((rows, width), BF16),
            pltpu.SemaphoreType.DMA((9,)),
            pltpu.SemaphoreType.DMA((5,)),
            pltpu.SemaphoreType.DMA((5,)),
            pltpu.SemaphoreType.DMA((8,)),
            pltpu.SemaphoreType.DMA((8,)),
        ],
        compiler_params=pltpu.CompilerParams(
            collective_id=collective_id, has_side_effects=True, vmem_limit_bytes=62 << 20
        ),
        cost_estimate=pl.CostEstimate(flops=cost, bytes_accessed=count * width, transcendentals=0),
        name="plane_sum",
    )(*lefts, right, base, source, gain, *extra_in)


def last_kernel(
    size, deep, own_in, gain_a, gain_b, rows_in, other_in, smalls, gains, rows_out, plane,
    mine, lines, store, send, recv, small_send, small_recv, plane_send, plane_recv, line_send, line_recv,
):
    thin = smalls.shape[2]
    fsdp, ctx, tp = lax.axis_index("fsdp"), lax.axis_index("ctx"), lax.axis_index("tp")

    def away(dz, dc, dt):
        return (lax.rem(fsdp + dz, size), lax.rem(ctx + dc, 2), lax.rem(tp + dt, 4))

    in_plane = [(0, dc, dt) for dc in range(2) for dt in range(4)][1:]
    across_line = [(dz, dc, 0) for dz in range(size) for dc in range(2)][1:]
    along_line = [(dz, 0, 0) for dz in range(1, size)]
    meet(*[away(*d) for d in in_plane + [d for d in across_line if d not in in_plane]])
    core, row, _, across, along, same, _, _ = partners()
    came = (1 - row) * 2 + core
    copies = [
        remote(own_in.at[pl.ds(0, deep), :], other_in, send.at[0], recv.at[0], across),
        remote(rows_in, rows_out.at[tp], send.at[1], recv.at[1], along),
        remote(rows_in, rows_out.at[tp], send.at[2], recv.at[2], same),
        remote(rows_out.at[came], rows_out.at[came], send.at[3], recv.at[3], same),
    ]
    local = [
        pltpu.make_async_copy(rows_in, rows_out.at[tp], store.at[1]),
    ]
    for i in (1, 0, 2):
        copies[i].start()
    for copy in local:
        copy.start()
    at = lax.broadcasted_iota(jnp.int32, gains.shape, 0)
    part = jnp.zeros(gains.shape, F32)
    quarter = gains.shape[1]
    for k, gain in enumerate((gain_a, gain_b)):
        for i in range(4):
            line = jnp.sum(gain[:, i * quarter : (i + 1) * quarter], axis=0, keepdims=True)
            part = jnp.where(at == 4 * k + i, line, part)
    place = ctx * 4 + tp
    plane[place] = part
    sent = [
        remote(plane.at[place], plane.at[place], plane_send.at[i], plane_recv.at[i], away(*d))
        for i, d in enumerate(in_plane)
    ]
    for copy in sent:
        copy.start()
    thin_rows = own_in.at[pl.ds(deep, thin), :]
    local.append(pltpu.make_async_copy(thin_rows, smalls.at[ctx, fsdp], store.at[0]))
    local[-1].start()
    for i, d in enumerate(across_line):
        copies.append(remote(thin_rows, smalls.at[ctx, fsdp], small_send.at[i], small_recv.at[i], away(*d)))
        copies[-1].start()
    for copy in sent:
        copy.wait_recv()
    total = plane[0]
    for i in range(1, 8):
        total = total + plane[i]
    mine[...] = total
    lines[fsdp] = total
    further = [
        remote(mine, lines.at[fsdp], line_send.at[i], line_recv.at[i], away(*d)) for i, d in enumerate(along_line)
    ]
    for copy in further:
        copy.start()
    for copy in further:
        copy.wait_recv()
    total = lines[0]
    for i in range(1, size):
        total = total + lines[i]
    gains[...] = total
    copies[1].wait_recv()
    copies[3].start()
    for copy in copies[:1] + copies[2:]:
        copy.wait_recv()
    for copy in copies + sent + further:
        copy.wait_send()
    for copy in local:
        copy.wait()


def last(own_in, gain_a, gain_b, rows, deep, size, collective_id):
    width, thin = own_in.shape[1], own_in.shape[0] - deep
    gains = (8, gain_a.shape[1] // 4)
    vmem = pl.BlockSpec(memory_space=pltpu.VMEM)
    anywhere = pl.BlockSpec(memory_space=pl.ANY)
    sems = [pltpu.SemaphoreType.DMA((n,)) for n in (2, 4, 4, 2 * size, 2 * size, 8, 8, size, size)]
    return pl.pallas_call(
        functools.partial(last_kernel, size, deep),
        in_specs=[anywhere] + [vmem] * 3,
        out_specs=[anywhere, anywhere, vmem, anywhere],
        out_shape=[
            jax.ShapeDtypeStruct((deep, width), BF16),
            jax.ShapeDtypeStruct((2, size, thin, width), BF16),
            jax.ShapeDtypeStruct(gains, F32),
            jax.ShapeDtypeStruct((4,) + rows.shape, BF16),
        ],
        scratch_shapes=[
            pltpu.VMEM((8,) + gains, F32),
            pltpu.VMEM(gains, F32),
            pltpu.VMEM((size,) + gains, F32),
        ]
        + sems,
        compiler_params=pltpu.CompilerParams(
            collective_id=collective_id, has_side_effects=True, vmem_limit_bytes=32 << 20
        ),
        cost_estimate=pl.CostEstimate(flops=1 << 33, bytes_accessed=4 << 20, transcendentals=0),
        name="last",
    )(own_in, gain_a, gain_b, rows)


def scan_rows(a_ref, b_ref, carry, reverse):
    rows, width = b_ref.shape
    groups = rows // 8
    a = a_ref[...].reshape(groups, 8, width)
    b = b_ref[...].reshape(groups, 8, width)
    at = lax.broadcasted_iota(jnp.int32, (groups, 8, width), 1)
    for shift in (1, 2, 4):
        ok = (at < 8 - shift) if reverse else (at >= shift)
        turn = 8 - shift if reverse else shift
        b_before = jnp.where(ok, pltpu.roll(b, turn, 1), 0.0)
        a_before = jnp.where(ok, pltpu.roll(a, turn, 1), 1.0)
        b = a * b_before + b
        a = a * a_before
    a_ref[...] = a.reshape(rows, width)
    b_ref[...] = b.reshape(rows, width)
    for k in range(groups):
        k = groups - 1 - k if reverse else k
        part = pl.ds(8 * k, 8)
        now = b_ref[part, :] + a_ref[part, :] * carry
        b_ref[part, :] = now
        carry = now[0:1, :] if reverse else now[7:8, :]
    return carry


def mixer_kernel(
    place, pre, masks, params, gate_a, gate_x, mixed, states, recur_out, input_out, conv_out, ext, a_buf, b_buf, carry
):
    rows, width = states.shape

    @pl.when(pl.program_id(0) == 0)
    def _():
        ext[...] = jnp.zeros_like(ext)
        carry[...] = jnp.zeros_like(carry)

    ext[0:8, :] = ext[rows : rows + 8, :]
    ext[8:, :] = pre[:, width:].astype(BF16).astype(F32)
    conv = params[4:5, :] + params[0:1, :] * ext[8:, :]
    for k in range(1, 4):
        conv = conv + params[k : k + 1, :] * (masks[:, k - 1 : k] * ext[pl.ds(8 - k, rows), :])
    conv_low = conv.astype(BF16)
    conv_out[...] = conv_low
    conv = conv_low.astype(F32)
    recur = jax.nn.sigmoid(matmul(conv_low, gate_a[...]) + params[5:6, :])
    opened = jax.nn.sigmoid(matmul(conv_low, gate_x[...]) + params[6:7, :])
    recur_out[...] = recur
    input_out[...] = opened
    log_decay = params[7:8, :] * recur
    same = masks[:, 0:1]
    root = jnp.sqrt(one_minus_exp(-2.0 * log_decay))
    a_buf[...] = same * jnp.exp(log_decay)
    b_buf[...] = opened * conv * jnp.where(same > 0.5, root, 1.0)
    carry[0:1, :] = scan_rows(a_buf, b_buf, carry[0:1, :], False)
    state = b_buf[...]
    states[...] = state
    mixed[...] = (state * gelu(pre[:, :width])).astype(BF16)


def mixer_back_kernel(
    place, grad_proj, w_out, pre, pre_tail, states, states_tail, recur_in, input_in, conv_in, masks, params, gate_a, gate_x,
    grads, sums, sum_a, sum_x, ext, grad_ext, a_buf, b_buf, carry,
):
    rows, width = states.shape
    step = pl.program_id(0)
    first = step == pl.num_programs(0) - 1

    @pl.when(step == 0)
    def _():
        grad_ext[...] = jnp.zeros_like(grad_ext)
        carry[...] = jnp.zeros_like(carry)
        sums[...] = jnp.zeros_like(sums)
        sum_a[...] = jnp.zeros_like(sum_a)
        sum_x[...] = jnp.zeros_like(sum_x)

    inside = jnp.where(first, 0.0, 1.0)
    branch, slope = gelu_parts(pre[:, :width])
    above = matmul(grad_proj[...], w_out[...])
    state = states[...]
    grads[:, :width] = (above * state * slope).astype(BF16)
    recur, opened = recur_in[...], input_in[...]
    conv_low = conv_in[...]
    conv = conv_low.astype(F32)
    same = masks[:, 0:1]
    rate = params[7:8, :]
    log_decay = rate * recur
    decay = jnp.exp(log_decay)
    root = jnp.sqrt(one_minus_exp(-2.0 * log_decay))
    mult = jnp.where(same > 0.5, root, 1.0)
    a_buf[0:rows, :] = same * decay
    head = a_buf[0:1, :]
    a_buf[rows : rows + 8, :] = jnp.broadcast_to(carry[1:2, :], (8, width))
    factor = a_buf[pl.ds(1, rows), :]
    a_buf[0:rows, :] = factor
    b_buf[...] = above * branch
    new_carry = scan_rows(a_buf.at[pl.ds(0, rows), :], b_buf, carry[0:1, :], True)
    carry[0:1, :] = new_carry
    carry[1:2, :] = head
    total = b_buf[...]
    ext[0:8, :] = inside * states_tail[...]
    ext[8:, :] = state
    before = ext[pl.ds(7, rows), :]
    grad_open = total * opened
    grad_log = jnp.where(
        same > 0.5, total * before * decay - grad_open * conv * decay * decay / root, 0.0
    )

    def fold(x):
        return jnp.sum(x.reshape(rows // 8, 8, width), axis=0)

    sums[0:8, :] += fold(grad_log * recur)
    low_a = (grad_log * rate * recur * (1.0 - recur)).astype(BF16)
    low_x = (total * conv * mult * opened * (1.0 - opened)).astype(BF16)
    sums[8:16, :] += fold(low_a.astype(F32))
    sums[16:24, :] += fold(low_x.astype(F32))
    sum_a[...] += left_inner(conv_low, low_a)
    sum_x[...] += left_inner(conv_low, low_x)
    grad_conv = grad_open * mult + (
        right_inner(low_a, gate_a[...]) + right_inner(low_x, gate_x[...])
    )
    sums[24:32, :] += fold(grad_conv)
    ext[0:8, :] = inside * pre_tail[:, width:].astype(BF16).astype(F32)
    ext[8:, :] = pre[:, width:].astype(BF16).astype(F32)
    grad_ext[rows : rows + 8, :] = grad_ext[0:8, :]
    grad_ext[0:rows, :] = grad_conv
    grad_in = params[0:1, :] * grad_conv
    sums[32:40, :] += fold(grad_conv * ext[8:, :])
    for k in range(1, 4):
        earlier = masks[:, k - 1 : k] * ext[pl.ds(8 - k, rows), :]
        sums[32 + 8 * k : 40 + 8 * k, :] += fold(grad_conv * earlier)
        grad_in = grad_in + params[k : k + 1, :] * (
            masks[:, k + 2 : k + 3] * grad_ext[pl.ds(k, rows), :]
        )
    grads[:, width:] = grad_in.astype(BF16)


def mixer(pre, masks, params, gate_a, gate_x, place, rows):
    count, width = pre.shape[0], pre.shape[1] // 2
    steps = count // rows
    spot = lambda i, place: (place[i], 0)
    inorder = lambda i, place: (i, 0)
    fixed = lambda i, place: (0, 0)
    wide = pl.BlockSpec((rows, 2 * width), spot)
    one = pl.BlockSpec((rows, width), spot)
    gate = pl.BlockSpec((width, width), fixed)
    return pl.pallas_call(
        mixer_kernel,
        grid_spec=pltpu.PrefetchScalarGridSpec(
            num_scalar_prefetch=1,
            grid=(steps,),
            in_specs=[wide, pl.BlockSpec((rows, 8), inorder), pl.BlockSpec((8, width), fixed), gate, gate],
            out_specs=[one] * 5,
            scratch_shapes=[
                pltpu.VMEM((rows + 8, width), F32),
                pltpu.VMEM((rows, width), F32),
                pltpu.VMEM((rows, width), F32),
                pltpu.VMEM((8, width), F32),
            ],
        ),
        out_shape=[
            jax.ShapeDtypeStruct((count, width), kind) for kind in (BF16, F32, F32, F32, BF16)
        ],
        cost_estimate=pl.CostEstimate(
            flops=count * width * (4 * width + 120), bytes_accessed=count * width * 24, transcendentals=count * width * 6
        ),
        name="mixer",
    )(place, pre, masks, params, gate_a, gate_x)


def mixer_back(grad_proj, w_out, pre, states, recur, opened, conv, masks, params, gate_a, gate_x, place, rows):
    count, width = states.shape
    steps = count // rows
    last = steps - 1
    spot = lambda i, place: (place[last - i], 0)
    inorder = lambda i, place: (last - i, 0)
    fixed = lambda i, place: (0, 0)

    def tail(i, place):
        return (place[jnp.maximum(last - i - 1, 0)] * (rows // 8) + rows // 8 - 1, 0)

    wide = pl.BlockSpec((rows, 2 * width), spot)
    one = pl.BlockSpec((rows, width), spot)
    gate = pl.BlockSpec((width, width), fixed)
    return pl.pallas_call(
        mixer_back_kernel,
        grid_spec=pltpu.PrefetchScalarGridSpec(
            num_scalar_prefetch=1,
            grid=(steps,),
            in_specs=[
                pl.BlockSpec((rows, grad_proj.shape[1]), spot), pl.BlockSpec(w_out.shape, fixed),
                wide, pl.BlockSpec((8, 2 * width), tail), one, pl.BlockSpec((8, width), tail), one, one, one,
                pl.BlockSpec((rows, 8), inorder), pl.BlockSpec((8, width), fixed), gate, gate,
            ],
            out_specs=[wide, pl.BlockSpec((64, width), fixed), gate, gate],
            scratch_shapes=[
                pltpu.VMEM((rows + 8, width), F32),
                pltpu.VMEM((rows + 8, width), F32),
                pltpu.VMEM((rows + 8, width), F32),
                pltpu.VMEM((rows, width), F32),
                pltpu.VMEM((8, width), F32),
            ],
        ),
        out_shape=[
            jax.ShapeDtypeStruct((count, 2 * width), BF16),
            jax.ShapeDtypeStruct((64, width), F32),
            jax.ShapeDtypeStruct((width, width), F32),
            jax.ShapeDtypeStruct((width, width), F32),
        ],
        cost_estimate=pl.CostEstimate(
            flops=count * width * (8 * width + 2 * grad_proj.shape[1] + 200), bytes_accessed=count * width * 34, transcendentals=count * width * 4
        ),
        name="mixer_back",
    )(place, grad_proj, w_out, pre, pre, states, states, recur, opened, conv, masks, params, gate_a, gate_x)


def on_diagonal(blocks):
    heads, size = blocks.shape[0], blocks.shape[1]
    out = jnp.zeros((heads * size, heads * size), blocks.dtype)
    for h in range(heads):
        out = lax.dynamic_update_slice(out, blocks[h], (h * size, h * size))
    return out


def shards(
    tokens, segments, cotangent, gain_mix, w_branch, w_input, conv_weight, conv_bias, gate_a, bias_a, gate_x, bias_x,
    decay_param, w_out, gain_mlp, w_gate, w_up, w_down,
):
    half_at = lax.axis_index("ctx")
    place_tp = lax.axis_index("tp")

    def mine(x, axis):
        size = x.shape[axis] // 2
        return lax.dynamic_slice_in_dim(x, half_at * size, size, axis)

    def owned(x, axis):
        return lax.psum_scatter(x, "fsdp", scatter_dimension=axis, tiled=True)

    _, tok_count, model_width = tokens.shape
    rows = tok_count // 4
    length = 2 * tok_count
    own_in = jnp.concatenate([mine(w_branch, 1), mine(w_input, 1), mine(w_out, 0).T], axis=1)
    full_mix = lax.all_gather(own_in, "fsdp", axis=0, tiled=True)
    own_gu = jnp.concatenate([mine(w_gate, 1), mine(w_up, 1)], axis=1)
    full_gu = lax.all_gather(own_gu, "fsdp", axis=0, tiled=True)
    full_down = lax.all_gather(mine(w_down, 0), "fsdp", axis=1, tiled=True)

    width = own_in.shape[1] // 3
    full_in, full_out = full_mix[:, : 2 * width], full_mix[:, 2 * width :]
    units = own_gu.shape[1] // 2
    place = jnp.asarray(place_table())[half_at * 4 + place_tp]

    rate = -RATE_SCALE * jax.nn.softplus(-decay_param)
    params = jnp.concatenate(
        [
            mine(conv_weight, 1),
            jnp.stack([mine(v, 0) for v in (conv_bias, bias_a, bias_x, rate)]),
        ],
        axis=0,
    )
    heads_a, heads_x = mine(gate_a, 0), mine(gate_x, 0)
    head_count, head_width = heads_a.shape[0], heads_a.shape[1]
    diag_a, diag_x = on_diagonal(heads_a), on_diagonal(heads_x)
    seg = segments[0]
    around = jnp.pad(seg, (3, 3), constant_values=-1)
    marks = [around[3 - k : 3 - k + length] == seg for k in (1, 2, 3)]
    marks += [around[3 + k : 3 + k + length] == seg for k in (1, 2, 3)]
    marks += [jnp.zeros_like(marks[0])] * 2
    masks = jnp.stack(marks, axis=1).astype(F32)

    own = lax.dynamic_slice_in_dim(tokens[0], place_tp * rows, rows, 0)
    own_cot = lax.dynamic_slice_in_dim(cotangent[0], place_tp * rows, rows, 0)
    gain_mix, gain_mlp = gain_mix[None], gain_mlp[None]
    normed, cot = head(tokens[0], cotangent[0], gain_mix, 1)
    normed, cot = normed.reshape(length, model_width), cot.reshape(length, model_width)

    pre = matmul(normed, full_in)
    mixed, states, recur, opened, conv = mixer(pre, masks, params, diag_a, diag_x, place, rows)
    normed_mlp, resid = plane_sum("norm", True, [mixed], full_out, own, own, gain_mlp, 2, 9 << 33)
    normed_mlp = normed_mlp.reshape(length, model_width)

    both = matmul(normed_mlp, full_gu)
    gate_pre, up_pre = both[:, :units], both[:, units:]
    gate_act, gate_slope = gelu_parts(gate_pre)
    hidden = (gate_act * up_pre).astype(BF16)
    grad_w_down = left_inner(hidden, cot).astype(BF16)
    full_down, grad_w_down, hidden, full_in, own_cot = tied((full_down, grad_w_down, hidden, full_in, own_cot))
    own_down = owned(grad_w_down, 1)

    grad_hidden = right_inner(cot, full_down)
    grad_both = [(grad_hidden * up_pre * gate_slope).astype(BF16), (grad_hidden * gate_act).astype(BF16)]
    grad_both, hidden = tied((grad_both, hidden))
    half = length // 2
    sent = matmul(hidden[half:], full_down).astype(BF16)
    grad_both, sent = tied((grad_both, sent))
    grad_w_gu = left_inner(normed_mlp, jnp.concatenate(grad_both, axis=1)).astype(BF16)
    own_gu = owned(grad_w_gu, 0)
    got = exchange(sent, "core")
    grad_both, got, grad_w_gu = tied((grad_both, got, grad_w_gu))
    far_sent = (matmul(hidden[half // 2 : half], full_down) + got[half // 2 :].astype(F32)).astype(BF16)
    got_far = exchange(far_sent, "far")
    low = matmul(hidden[: half // 2], full_down) + got[: half // 2].astype(F32)
    grad_both, low, far_sent = tied((grad_both, low, far_sent))
    grad_proj, grad_resid, gain_mlp_part = plane_sum(
        "back", True, grad_both, full_gu, own_cot, resid, gain_mlp, 3, 9 << 33
    )
    grad_proj = grad_proj.reshape(length, model_width)
    grad_proj, got_far, low = tied((grad_proj, got_far, low))
    near_sent = (low[rows:] + got_far[rows:].astype(F32)).astype(BF16)
    got_near = exchange(near_sent, "near")

    grad_w_out = left_inner(mixed, grad_proj).astype(BF16)
    grad_proj, own_down, grad_w_out = tied((grad_proj, own_down, grad_w_out))
    own_out = owned(grad_w_out, 1)
    other_down = flip(own_down, 4)
    low, own_gu, grad_w_out = tied((low, own_gu, grad_w_out))
    other_gu = flip(own_gu, 4)
    output = (resid + low[:rows] + got_far[:rows].astype(F32) + got_near.astype(F32)).astype(BF16)
    states, output = tied((states, output))
    output_along = flip(output, 2)
    grads_in, sums, sum_a, sum_x = mixer_back(
        grad_proj, full_out, pre, states, recur, opened, conv, masks, params, diag_a, diag_x, place, rows
    )
    grads_in, output_along, other_down = tied((grads_in, output_along, other_down))
    lines = jnp.sum(sums.reshape(8, 8, width), axis=1)
    head_at = lax.broadcasted_iota(jnp.int32, (head_width, width), 1) // head_width
    squares = [
        sum(
            jnp.where(head_at == h, part[h * head_width : (h + 1) * head_width], 0.0) for h in range(head_count)
        )
        for part in (sum_a, sum_x)
    ]
    fsdp_size = lax.axis_size("fsdp")
    part_rows = 16 * -(-(8 + 2 * head_width) // (16 * fsdp_size))
    spare = fsdp_size * part_rows - 8 - 2 * head_width
    small = jnp.concatenate([lines] + squares + [jnp.zeros((spare, width), F32)], axis=0).astype(BF16)
    small = small.reshape(fsdp_size, 2, part_rows // 2, width)
    small = jnp.concatenate([small[:, 0], small[:, 1]], axis=2)
    grad_w_in = left_inner(normed, grads_in).astype(BF16).reshape(fsdp_size, -1, 2 * width)
    grad_w_in = jnp.concatenate([grad_w_in, small], axis=1).reshape(-1, 2 * width)
    grads_in, grad_w_in, own_out, other_gu = tied((grads_in, grad_w_in, own_out, other_gu))
    own_in = owned(grad_w_in, 0)
    moved = (output, output_along, own_gu, other_gu, own_down, other_down, own_out)
    grad_tokens, gain_mix_part, output, own_gate, own_up, own_down, own_out = plane_sum(
        "back", False, [grads_in], full_in, grad_resid, own, gain_mix, 4, 5 << 33, moved
    )
    other_in, smalls, gains, grad_tokens = last(
        own_in, gain_mix_part, gain_mlp_part, grad_tokens, model_width // fsdp_size, fsdp_size, 5
    )

    def both_halves(x, other, axis):
        low = jnp.where(half_at == 0, x, other)
        high = jnp.where(half_at == 0, other, x)
        return jnp.concatenate([low, high], axis=axis).astype(F32)

    own_in = own_in[: model_width // fsdp_size]
    smalls = jnp.stack([smalls[..., :width], smalls[..., width:]], axis=2).reshape(2, fsdp_size * part_rows, width)
    smalls = jnp.concatenate([smalls[0], smalls[1]], axis=1).astype(F32)
    lines = smalls[:8]
    squares = []
    for i in range(2):
        part = smalls[8 + i * head_width : 8 + (i + 1) * head_width]
        squares.append(
            jnp.stack([part[:, h * head_width : (h + 1) * head_width] for h in range(2 * head_count)])
        )
    own_branch = both_halves(own_in[:, :width], other_in[:, :width], 1)
    own_input = both_halves(own_in[:, width:], other_in[:, width:], 1)
    return (
        output.reshape(1, tok_count, model_width),
        grad_tokens.reshape(1, tok_count, model_width),
        gains[:4].reshape(model_width),
        own_branch,
        own_input,
        lines[4:8],
        lines[3],
        squares[0],
        lines[1],
        squares[1],
        lines[2],
        RATE_SCALE * jax.nn.sigmoid(-decay_param) * lines[0],
        own_out.astype(F32),
        gains[4:].reshape(model_width),
        own_gate.astype(F32),
        own_up.astype(F32),
        own_down.astype(F32),
    )


def solution(mesh):
    in_specs = (
        P("fsdp", "ctx", None),
        P("fsdp", None),
        P("fsdp", "ctx", None),
        P(),
        P("fsdp", "tp"),
        P("fsdp", "tp"),
        P(None, "tp"),
        P("tp"),
        P("tp", None, None),
        P("tp"),
        P("tp", None, None),
        P("tp"),
        P("tp"),
        P("tp", "fsdp"),
        P(),
        P("fsdp", "tp"),
        P("fsdp", "tp"),
        P("tp", "fsdp"),
    )
    out_specs = (
        P("fsdp", "ctx", None),
        P("fsdp", "ctx", None),
        P(),
        P("fsdp", "tp"),
        P("fsdp", "tp"),
        P(None, "tp"),
        P("tp"),
        P("tp", None, None),
        P("tp"),
        P("tp", None, None),
        P("tp"),
        P("tp"),
        P("tp", "fsdp"),
        P(),
        P("fsdp", "tp"),
        P("fsdp", "tp"),
        P("tp", "fsdp"),
    )
    return jax.shard_map(shards, mesh=mesh, in_specs=in_specs, out_specs=out_specs, check_vma=False)
```

```python
import functools

import jax
import jax.numpy as jnp
import numpy as np
from jax import lax
from jax.experimental import pallas as pl
from jax.experimental.pallas import tpu as pltpu
from jax.sharding import PartitionSpec as P

EPSILON = 1e-06
RATE_SCALE = 8.0
GELU_C = 0.7978845608028654
GELU_K = 0.044715
GROUP = ("ctx", "tp")
F32, BF16 = jnp.float32, jnp.bfloat16
tied = lax.optimization_barrier


def matmul(left, right):
    return jnp.dot(left, right, preferred_element_type=F32)


def left_inner(left, right):
    return lax.dot_general(left, right, (((0,), (0,)), ((), ())), preferred_element_type=F32)


def right_inner(left, right):
    return lax.dot_general(left, right, (((1,), (1,)), ((), ())), preferred_element_type=F32)


def gelu_parts(v):
    t = jnp.tanh(GELU_C * (v + GELU_K * (v * v * v)))
    half = 0.5 * (1.0 + t)
    slope = half + 0.5 * v * (1.0 - t * t) * (GELU_C * (1.0 + 3.0 * GELU_K * v * v))
    return v * half, slope


def gelu(v):
    return 0.5 * v * (1.0 + jnp.tanh(GELU_C * (v + GELU_K * (v * v * v))))


def one_minus_exp(u):
    series = 1.0 - u * (1.0 / 8.0)
    for n in (7.0, 6.0, 5.0, 4.0, 3.0, 2.0):
        series = 1.0 - u * (1.0 / n) * series
    return jnp.where(u < 0.5, u * series, 1.0 - jnp.exp(-u))


def rms_rows(values):
    return lax.rsqrt(jnp.mean(values * values, axis=-1, keepdims=True) + EPSILON)


def norm_back(grad_norm, scaled, scale_row, gain):
    grad_scaled = grad_norm * gain
    return scale_row * (
        grad_scaled - scaled * jnp.mean(grad_scaled * scaled, axis=-1, keepdims=True)
    )


def step_mask(kind, g):
    core = g % 2
    if kind == "core":
        return 1
    return 2 if (kind == "near") == (core == 0) else 4


def exchange(block, kind):
    pairs = [(g, g ^ step_mask(kind, g)) for g in range(8)]
    return lax.ppermute(block, GROUP, pairs)


def flip(block, mask):
    return lax.ppermute(block, GROUP, [(g, g ^ mask) for g in range(8)])


def place_table():
    table = np.zeros((8, 8), np.int32)
    for g in range(8):
        for spot in range(8):
            at = g ^ (spot >> 2)
            block = at
            if spot & 1:
                block ^= step_mask("near", at)
            if spot & 2:
                block ^= step_mask("far", at)
            table[g, block] = spot
    return table


def reduce_rows(left, right, product):
    half = left.shape[0] // 2
    sent = product(left[half:], right).astype(BF16)
    kept = product(left[:half], right)
    got = exchange(sent, "core")
    kept, got = lax.optimization_barrier((kept, got))
    total = kept + got.astype(F32)
    for kind in ("far", "near"):
        half = half // 2
        got = exchange(total[half:].astype(BF16), kind)
        total = total[:half] + got.astype(F32)
    return total


def partners():
    fsdp, ctx, tp = lax.axis_index("fsdp"), lax.axis_index("ctx"), lax.axis_index("tp")
    core, line = tp % 2, tp // 2
    across = (fsdp, 1 - ctx, tp)
    along = (fsdp, ctx, (1 - line) * 2 + core)
    same = (fsdp, ctx, line * 2 + 1 - core)
    near = (fsdp, ctx + core * (1 - 2 * ctx), (line + (1 - core) * (1 - 2 * line)) * 2 + core)
    far = (fsdp, ctx + (1 - core) * (1 - 2 * ctx), (line + core * (1 - 2 * line)) * 2 + core)
    return core, line, tp, across, along, same, near, far


def meet(*devices):
    barrier = pltpu.get_barrier_semaphore()
    for device in devices:
        pl.semaphore_signal(barrier, inc=1, device_id=device, device_id_type=pl.DeviceIdType.MESH)
    pl.semaphore_wait(barrier, len(devices))


def remote(src, dst, send_sem, recv_sem, device):
    return pltpu.make_async_remote_copy(
        src_ref=src, dst_ref=dst, send_sem=send_sem, recv_sem=recv_sem, device_id=device,
        device_id_type=pl.DeviceIdType.MESH,
    )


def by_rows(count, step, body):
    def turn(i, _):
        body(pl.multiple_of(i * step, step))
        return 0

    lax.fori_loop(0, count // step, turn, 0)


def head_kernel(tokens, cot, gain, normed_out, cot_out, x_buf, n_buf, c_buf, load, store, send, recv):
    rows = x_buf.shape[0] // 4
    core, line, tp, across, along, same, _, _ = partners()
    load_x = pltpu.make_async_copy(tokens, x_buf, load.at[0])
    load_c = pltpu.make_async_copy(cot, c_buf, load.at[1])
    load_x.start()
    load_c.start()
    meet(across, along, same)

    def block(j):
        return pl.ds(pl.multiple_of(j * rows, rows), rows)

    def normalize(j):
        def body(r):
            at = pl.ds(pl.multiple_of(j * rows + r, 32), 32)
            x = x_buf[at, :].astype(F32)
            n_buf[at, :] = (x * rms_rows(x) * gain[...]).astype(BF16)

        by_rows(rows, 32, body)

    load_x.wait()
    normalize(tp)
    outs = (normed_out, cot_out)
    bufs = (n_buf, c_buf)
    first = [
        remote(bufs[i].at[block(tp)], outs[i].at[2 - core], send.at[i], recv.at[i], across) for i in range(2)
    ]
    first[0].start()
    load_c.wait()
    first[1].start()
    for j in range(1, 4):
        normalize((tp + j) % 4)
    kept = []
    for k, (dy, dc) in enumerate(((0, 0), (1, 0), (0, 1), (1, 1))):
        there = line + dy * (1 - 2 * line)
        which = core + dc * (1 - 2 * core)
        effect = which
        spot = 4 * dc + dy * (1 + effect)
        for i in range(2):
            copy = pltpu.make_async_copy(bufs[i].at[block(there * 2 + which)], outs[i].at[spot], store.at[2 * k + i])
            copy.start()
            kept.append(copy)
    later = []
    for i in range(2):
        first[i].wait_recv()
        second = remote(outs[i].at[2 - core], outs[i].at[3], send.at[2 + i], recv.at[2 + i], along)
        second.start()
        third = remote(outs[i].at[2 - core], outs[i].at[6 - core], send.at[4 + i], recv.at[4 + i], same)
        third.start()
        later.append((second, third))
    last = []
    for i in range(2):
        later[i][0].wait_recv()
        fourth = remote(outs[i].at[3], outs[i].at[7], send.at[6 + i], recv.at[6 + i], same)
        fourth.start()
        last.append(fourth)
    for i in range(2):
        later[i][1].wait_recv()
        last[i].wait_recv()
        first[i].wait_send()
        later[i][0].wait_send()
        later[i][1].wait_send()
        last[i].wait_send()
    for copy in kept:
        copy.wait()


def head(tokens, cot, gain, collective_id):
    count, width = tokens.shape
    rows = count // 4
    out = jax.ShapeDtypeStruct((8, rows, width), BF16)
    anywhere = pl.BlockSpec(memory_space=pl.ANY)
    return pl.pallas_call(
        head_kernel,
        in_specs=[anywhere, anywhere, pl.BlockSpec(memory_space=pltpu.VMEM)],
        out_specs=[anywhere, anywhere],
        out_shape=[out, out],
        scratch_shapes=[pltpu.VMEM((count, width), BF16)] * 3
        + [
            pltpu.SemaphoreType.DMA((2,)),
            pltpu.SemaphoreType.DMA((8,)),
            pltpu.SemaphoreType.DMA((8,)),
            pltpu.SemaphoreType.DMA((8,)),
        ],
        compiler_params=pltpu.CompilerParams(
            collective_id=collective_id, has_side_effects=True, vmem_limit_bytes=60 << 20
        ),
        cost_estimate=pl.CostEstimate(flops=5 << 33, bytes_accessed=64 << 20, transcendentals=0),
        name="head",
    )(tokens, cot, gain)


def plane_sum_kernel(
    epilogue, wide, parts, *refs
):
    lefts, (right, base, source, gain), refs = refs[:parts], refs[parts : parts + 4], refs[parts + 4 :]
    if epilogue == "norm":
        out, kept_out, refs = refs[0], refs[1], refs[2:]
    elif wide:
        out, kept_out, gain_out, refs = refs[0], refs[1], refs[2], refs[3:]
    else:
        rows_in, rows_along, pair, pair_far, stack, stack_far, single = refs[:7]
        out, gain_out, rows_out, pair_a, pair_b, stack_out, single_out = refs[7:14]
        refs = refs[14:]
    to_core, from_core, acc, to_far, from_far, to_near, from_near, own, store, send, recv, gsend, grecv = refs
    rows, width = own.shape
    if not wide:
        own = out
    core, line, tp, across, along, same, near, far = partners()
    meet(same, near, far)
    tile = width // 4

    def products(row, ref, at):
        def turn(i, _):
            cols = pl.ds(pl.multiple_of(i * tile, tile), tile)
            part, start = 0.0, 0
            for left in lefts:
                part = part + right_inner(left[pl.ds(row, 2 * rows), :], right[cols, start : start + left.shape[1]])
                start += left.shape[1]
            ref[pl.ds(at, 2 * rows), cols] = part.astype(ref.dtype)
            return 0

        lax.fori_loop(0, 4, turn, 0)

    def both(a):
        return pl.ds(a * rows, 2 * rows)

    core_copy = [
        remote(to_core.at[both(2 * h)], from_core.at[both(2 * h)], send.at[h], recv.at[h], same) for h in range(2)
    ]
    far_copy = [remote(to_far.at[h], from_far.at[h], send.at[2 + h], recv.at[2 + h], far) for h in range(2)]
    near_copy = remote(to_near, from_near, send.at[4], recv.at[4], near)

    local, carried = [], []
    if not wide:
        came = (1 - line) * 2 + core
        half_at = lax.axis_index("ctx")
        units, tall = pair.shape[1] // 2, stack.shape[0]
        carried = [
            remote(rows_in, rows_out.at[tp], gsend.at[0], grecv.at[0], same),
            remote(rows_along, rows_out.at[came], gsend.at[1], grecv.at[1], same),
        ]
        single_rows = pl.ds(pl.multiple_of(half_at * single.shape[0], 16), single.shape[0])
        carried.append(remote(single, single_out.at[single_rows, :], gsend.at[2], grecv.at[2], across))
        carried[2].start()
        places = [(rows_in, rows_out.at[tp]), (rows_along, rows_out.at[came]), (single, single_out.at[single_rows, :])]
        for at, halves, block in ((half_at, pair, stack), (1 - half_at, pair_far, stack_far)):
            cols = pl.ds(pl.multiple_of(at * units, 128), units)
            places.append((halves.at[:, pl.ds(0, units)], pair_a.at[:, cols]))
            places.append((halves.at[:, pl.ds(units, units)], pair_b.at[:, cols]))
            places.append((block, stack_out.at[pl.ds(pl.multiple_of(at * tall, 16), tall), :]))
        local = [pltpu.make_async_copy(src, dst, store.at[i]) for i, (src, dst) in enumerate(places)]
        for copy in local:
            copy.start()

    products(6 * rows, to_core, 2 * rows)
    core_copy[1].start()
    products(2 * rows, acc, 2 * rows)
    core_copy[1].wait_recv()
    for h in (1, 0):
        def body(r, h=h):
            at = pl.ds(pl.multiple_of((2 + h) * rows + r, 32), 32)
            to_far[h, pl.ds(r, 32), :] = (acc[at, :] + from_core[at, :].astype(F32)).astype(BF16)

        by_rows(rows, 32, body)
        far_copy[h].start()
    products(4 * rows, to_core, 0)
    core_copy[0].start()
    products(0, acc, 0)
    core_copy[0].wait_recv()
    far_copy[1].wait_recv()

    def send_near(r):
        at = pl.ds(pl.multiple_of(rows + r, 32), 32)
        total = acc[at, :] + from_core[at, :].astype(F32) + from_far[1, pl.ds(r, 32), :].astype(F32)
        to_near[pl.ds(r, 32), :] = total.astype(BF16)

    by_rows(rows, 32, send_near)
    near_copy.start()
    if not wide:
        carried[0].start()
        carried[1].start()
    far_copy[0].wait_recv()

    def settle(r):
        at = pl.ds(r, 32)
        acc[at, :] = acc[at, :] + from_core[at, :].astype(F32) + from_far[0, at, :].astype(F32)

    by_rows(rows, 32, settle)
    if epilogue != "norm":
        gain_out[...] = jnp.zeros_like(gain_out)
    near_copy.wait_recv()

    def finish(r):
        at = pl.ds(r, 32)
        total = acc[at, :] + from_near[at, :].astype(F32)
        if epilogue == "norm":
            resid = base[at, :].astype(F32) + total
            kept_out[at, :] = resid
            own[at, :] = (resid * rms_rows(resid) * gain[...]).astype(BF16)
        else:
            x = source[at, :].astype(F32)
            scale = rms_rows(x)
            scaled = x * scale
            grad = base[at, :].astype(F32) + norm_back(total, scaled, scale, gain[...])
            gain_out[...] += jnp.sum((total * scaled).reshape(4, 8, width), axis=0)
            if wide:
                kept_out[at, :] = grad
            own[at, :] = grad.astype(BF16)

    by_rows(rows, 32, finish)
    if wide:
        mine = pltpu.make_async_copy(own, out.at[0], store.at[0])
        mine.start()
        copies = [
            remote(own, out.at[1], gsend.at[1], grecv.at[1], near),
            remote(own, out.at[2], gsend.at[2], grecv.at[2], far),
            remote(own, out.at[4], gsend.at[4], grecv.at[4], same),
            remote(out.at[1], out.at[3], gsend.at[3], grecv.at[3], far),
            remote(out.at[1], out.at[5], gsend.at[5], grecv.at[5], same),
            remote(out.at[2], out.at[6], gsend.at[6], grecv.at[6], same),
            remote(out.at[3], out.at[7], gsend.at[7], grecv.at[7], same),
        ]
        for k in range(3):
            copies[k].start()
        copies[0].wait_recv()
        copies[3].start()
        copies[4].start()
        copies[1].wait_recv()
        copies[5].start()
        copies[3].wait_recv()
        copies[6].start()
        for k in (2, 4, 5, 6):
            copies[k].wait_recv()
        local.append(mine)
    else:
        for copy in carried:
            copy.wait_recv()
        copies = carried
    for copy in copies + core_copy + far_copy + [near_copy]:
        copy.wait_send()
    for copy in local:
        copy.wait()


def plane_sum(epilogue, wide, lefts, right, base, source, gain, collective_id, cost, extra_in=()):
    count, width = lefts[0].shape[0], right.shape[0]
    rows = count // 8
    vmem = pl.BlockSpec(memory_space=pltpu.VMEM)
    anywhere = pl.BlockSpec(memory_space=pl.ANY)
    whole = jax.ShapeDtypeStruct((rows, width), F32)
    gains = jax.ShapeDtypeStruct((8, width), F32)
    extra = [whole] if epilogue == "norm" else [whole, gains] if wide else [gains]
    carried = []
    result = jax.ShapeDtypeStruct((8, rows, width), BF16)
    if not wide:
        _, _, pair, _, stack, _, single = extra_in
        carried = [(4, rows, width), pair.shape, pair.shape]
        carried += [(2 * block.shape[0], block.shape[1]) for block in (stack, single)]
        carried = [jax.ShapeDtypeStruct(shape, BF16) for shape in carried]
        result = jax.ShapeDtypeStruct((rows, width), BF16)
    return pl.pallas_call(
        functools.partial(plane_sum_kernel, epilogue, wide, len(lefts)),
        in_specs=[vmem] * (len(lefts) + 4 + len(extra_in)),
        out_specs=[anywhere if wide else vmem] + [vmem] * len(extra) + [anywhere] * len(carried),
        out_shape=[result] + extra + carried,
        scratch_shapes=[
            pltpu.VMEM((4 * rows, width), BF16),
            pltpu.VMEM((4 * rows, width), BF16),
            pltpu.VMEM((4 * rows, width), F32),
            pltpu.VMEM((2, rows, width), BF16),
            pltpu.VMEM((2, rows, width), BF16),
            pltpu.VMEM((rows, width), BF16),
            pltpu.VMEM((rows, width), BF16),
            pltpu.VMEM((rows, width), BF16),
            pltpu.SemaphoreType.DMA((9,)),
            pltpu.SemaphoreType.DMA((5,)),
            pltpu.SemaphoreType.DMA((5,)),
            pltpu.SemaphoreType.DMA((8,)),
            pltpu.SemaphoreType.DMA((8,)),
        ],
        compiler_params=pltpu.CompilerParams(
            collective_id=collective_id, has_side_effects=True, vmem_limit_bytes=62 << 20
        ),
        cost_estimate=pl.CostEstimate(flops=cost, bytes_accessed=count * width, transcendentals=0),
        name="plane_sum",
    )(*lefts, right, base, source, gain, *extra_in)


def last_kernel(
    size, deep, own_in, gain_a, gain_b, rows_in, other_in, smalls, gains, rows_out, plane,
    mine, lines, store, send, recv, small_send, small_recv, plane_send, plane_recv, line_send, line_recv,
):
    thin = smalls.shape[2]
    fsdp, ctx, tp = lax.axis_index("fsdp"), lax.axis_index("ctx"), lax.axis_index("tp")

    def away(dz, dc, dt):
        return (lax.rem(fsdp + dz, size), lax.rem(ctx + dc, 2), lax.rem(tp + dt, 4))

    in_plane = [(0, dc, dt) for dc in range(2) for dt in range(4)][1:]
    across_line = [(dz, dc, 0) for dz in range(size) for dc in range(2)][1:]
    along_line = [(dz, 0, 0) for dz in range(1, size)]
    meet(*[away(*d) for d in in_plane + [d for d in across_line if d not in in_plane]])
    core, row, _, across, along, same, _, _ = partners()
    came = (1 - row) * 2 + core
    copies = [
        remote(own_in.at[pl.ds(0, deep), :], other_in, send.at[0], recv.at[0], across),
        remote(rows_in, rows_out.at[tp], send.at[1], recv.at[1], along),
        remote(rows_in, rows_out.at[tp], send.at[2], recv.at[2], same),
        remote(rows_out.at[came], rows_out.at[came], send.at[3], recv.at[3], same),
    ]
    local = [
        pltpu.make_async_copy(rows_in, rows_out.at[tp], store.at[1]),
    ]
    for i in (1, 0, 2):
        copies[i].start()
    for copy in local:
        copy.start()
    at = lax.broadcasted_iota(jnp.int32, gains.shape, 0)
    part = jnp.zeros(gains.shape, F32)
    quarter = gains.shape[1]
    for k, gain in enumerate((gain_a, gain_b)):
        for i in range(4):
            line = jnp.sum(gain[:, i * quarter : (i + 1) * quarter], axis=0, keepdims=True)
            part = jnp.where(at == 4 * k + i, line, part)
    place = ctx * 4 + tp
    plane[place] = part
    sent = [
        remote(plane.at[place], plane.at[place], plane_send.at[i], plane_recv.at[i], away(*d))
        for i, d in enumerate(in_plane)
    ]
    for copy in sent:
        copy.start()
    thin_rows = own_in.at[pl.ds(deep, thin), :]
    local.append(pltpu.make_async_copy(thin_rows, smalls.at[ctx, fsdp], store.at[0]))
    local[-1].start()
    for i, d in enumerate(across_line):
        copies.append(remote(thin_rows, smalls.at[ctx, fsdp], small_send.at[i], small_recv.at[i], away(*d)))
        copies[-1].start()
    for copy in sent:
        copy.wait_recv()
    total = plane[0]
    for i in range(1, 8):
        total = total + plane[i]
    mine[...] = total
    lines[fsdp] = total
    further = [
        remote(mine, lines.at[fsdp], line_send.at[i], line_recv.at[i], away(*d)) for i, d in enumerate(along_line)
    ]
    for copy in further:
        copy.start()
    for copy in further:
        copy.wait_recv()
    total = lines[0]
    for i in range(1, size):
        total = total + lines[i]
    gains[...] = total
    copies[1].wait_recv()
    copies[3].start()
    for copy in copies[:1] + copies[2:]:
        copy.wait_recv()
    for copy in copies + sent + further:
        copy.wait_send()
    for copy in local:
        copy.wait()


def last(own_in, gain_a, gain_b, rows, deep, size, collective_id):
    width, thin = own_in.shape[1], own_in.shape[0] - deep
    gains = (8, gain_a.shape[1] // 4)
    vmem = pl.BlockSpec(memory_space=pltpu.VMEM)
    anywhere = pl.BlockSpec(memory_space=pl.ANY)
    sems = [pltpu.SemaphoreType.DMA((n,)) for n in (2, 4, 4, 2 * size, 2 * size, 8, 8, size, size)]
    return pl.pallas_call(
        functools.partial(last_kernel, size, deep),
        in_specs=[anywhere] + [vmem] * 3,
        out_specs=[anywhere, anywhere, vmem, anywhere],
        out_shape=[
            jax.ShapeDtypeStruct((deep, width), BF16),
            jax.ShapeDtypeStruct((2, size, thin, width), BF16),
            jax.ShapeDtypeStruct(gains, F32),
            jax.ShapeDtypeStruct((4,) + rows.shape, BF16),
        ],
        scratch_shapes=[
            pltpu.VMEM((8,) + gains, F32),
            pltpu.VMEM(gains, F32),
            pltpu.VMEM((size,) + gains, F32),
        ]
        + sems,
        compiler_params=pltpu.CompilerParams(
            collective_id=collective_id, has_side_effects=True, vmem_limit_bytes=32 << 20
        ),
        cost_estimate=pl.CostEstimate(flops=1 << 33, bytes_accessed=4 << 20, transcendentals=0),
        name="last",
    )(own_in, gain_a, gain_b, rows)


def scan_rows(a_ref, b_ref, carry, reverse):
    rows, width = b_ref.shape
    groups = rows // 8
    a = a_ref[...].reshape(groups, 8, width)
    b = b_ref[...].reshape(groups, 8, width)
    at = lax.broadcasted_iota(jnp.int32, (groups, 8, width), 1)
    for shift in (1, 2, 4):
        ok = (at < 8 - shift) if reverse else (at >= shift)
        turn = 8 - shift if reverse else shift
        b_before = jnp.where(ok, pltpu.roll(b, turn, 1), 0.0)
        a_before = jnp.where(ok, pltpu.roll(a, turn, 1), 1.0)
        b = a * b_before + b
        a = a * a_before
    a_ref[...] = a.reshape(rows, width)
    b_ref[...] = b.reshape(rows, width)
    for k in range(groups):
        k = groups - 1 - k if reverse else k
        part = pl.ds(8 * k, 8)
        now = b_ref[part, :] + a_ref[part, :] * carry
        b_ref[part, :] = now
        carry = now[0:1, :] if reverse else now[7:8, :]
    return carry


def mixer_kernel(
    place, pre, masks, params, gate_a, gate_x, mixed, states, recur_out, input_out, conv_out, ext, a_buf, b_buf, carry
):
    rows, width = states.shape

    @pl.when(pl.program_id(0) == 0)
    def _():
        ext[...] = jnp.zeros_like(ext)
        carry[...] = jnp.zeros_like(carry)

    ext[0:8, :] = ext[rows : rows + 8, :]
    ext[8:, :] = pre[:, width:].astype(BF16).astype(F32)
    conv = params[4:5, :] + params[0:1, :] * ext[8:, :]
    for k in range(1, 4):
        conv = conv + params[k : k + 1, :] * (masks[:, k - 1 : k] * ext[pl.ds(8 - k, rows), :])
    conv_low = conv.astype(BF16)
    conv_out[...] = conv_low
    conv = conv_low.astype(F32)
    recur = jax.nn.sigmoid(matmul(conv_low, gate_a[...]) + params[5:6, :])
    opened = jax.nn.sigmoid(matmul(conv_low, gate_x[...]) + params[6:7, :])
    recur_out[...] = recur
    input_out[...] = opened
    log_decay = params[7:8, :] * recur
    same = masks[:, 0:1]
    root = jnp.sqrt(one_minus_exp(-2.0 * log_decay))
    a_buf[...] = same * jnp.exp(log_decay)
    b_buf[...] = opened * conv * jnp.where(same > 0.5, root, 1.0)
    carry[0:1, :] = scan_rows(a_buf, b_buf, carry[0:1, :], False)
    state = b_buf[...]
    states[...] = state
    mixed[...] = (state * gelu(pre[:, :width])).astype(BF16)


def mixer_back_kernel(
    place, grad_proj, w_out, pre, pre_tail, states, states_tail, recur_in, input_in, conv_in, masks, params, gate_a, gate_x,
    grads, sums, sum_a, sum_x, ext, grad_ext, a_buf, b_buf, carry,
):
    rows, width = states.shape
    step = pl.program_id(0)
    first = step == pl.num_programs(0) - 1

    @pl.when(step == 0)
    def _():
        grad_ext[...] = jnp.zeros_like(grad_ext)
        carry[...] = jnp.zeros_like(carry)
        sums[...] = jnp.zeros_like(sums)
        sum_a[...] = jnp.zeros_like(sum_a)
        sum_x[...] = jnp.zeros_like(sum_x)

    inside = jnp.where(first, 0.0, 1.0)
    branch, slope = gelu_parts(pre[:, :width])
    above = matmul(grad_proj[...], w_out[...])
    state = states[...]
    grads[:, :width] = (above * state * slope).astype(BF16)
    recur, opened = recur_in[...], input_in[...]
    conv_low = conv_in[...]
    conv = conv_low.astype(F32)
    same = masks[:, 0:1]
    rate = params[7:8, :]
    log_decay = rate * recur
    decay = jnp.exp(log_decay)
    root = jnp.sqrt(one_minus_exp(-2.0 * log_decay))
    mult = jnp.where(same > 0.5, root, 1.0)
    a_buf[0:rows, :] = same * decay
    head = a_buf[0:1, :]
    a_buf[rows : rows + 8, :] = jnp.broadcast_to(carry[1:2, :], (8, width))
    factor = a_buf[pl.ds(1, rows), :]
    a_buf[0:rows, :] = factor
    b_buf[...] = above * branch
    new_carry = scan_rows(a_buf.at[pl.ds(0, rows), :], b_buf, carry[0:1, :], True)
    carry[0:1, :] = new_carry
    carry[1:2, :] = head
    total = b_buf[...]
    ext[0:8, :] = inside * states_tail[...]
    ext[8:, :] = state
    before = ext[pl.ds(7, rows), :]
    grad_open = total * opened
    grad_log = jnp.where(
        same > 0.5, total * before * decay - grad_open * conv * decay * decay / root, 0.0
    )

    def fold(x):
        return jnp.sum(x.reshape(rows // 8, 8, width), axis=0)

    sums[0:8, :] += fold(grad_log * recur)
    low_a = (grad_log * rate * recur * (1.0 - recur)).astype(BF16)
    low_x = (total * conv * mult * opened * (1.0 - opened)).astype(BF16)
    sums[8:16, :] += fold(low_a.astype(F32))
    sums[16:24, :] += fold(low_x.astype(F32))
    sum_a[...] += left_inner(conv_low, low_a)
    sum_x[...] += left_inner(conv_low, low_x)
    grad_conv = grad_open * mult + (
        right_inner(low_a, gate_a[...]) + right_inner(low_x, gate_x[...])
    )
    sums[24:32, :] += fold(grad_conv)
    ext[0:8, :] = inside * pre_tail[:, width:].astype(BF16).astype(F32)
    ext[8:, :] = pre[:, width:].astype(BF16).astype(F32)
    grad_ext[rows : rows + 8, :] = grad_ext[0:8, :]
    grad_ext[0:rows, :] = grad_conv
    grad_in = params[0:1, :] * grad_conv
    sums[32:40, :] += fold(grad_conv * ext[8:, :])
    for k in range(1, 4):
        earlier = masks[:, k - 1 : k] * ext[pl.ds(8 - k, rows), :]
        sums[32 + 8 * k : 40 + 8 * k, :] += fold(grad_conv * earlier)
        grad_in = grad_in + params[k : k + 1, :] * (
            masks[:, k + 2 : k + 3] * grad_ext[pl.ds(k, rows), :]
        )
    grads[:, width:] = grad_in.astype(BF16)


def mixer(pre, masks, params, gate_a, gate_x, place, rows):
    count, width = pre.shape[0], pre.shape[1] // 2
    steps = count // rows
    spot = lambda i, place: (place[i], 0)
    inorder = lambda i, place: (i, 0)
    fixed = lambda i, place: (0, 0)
    wide = pl.BlockSpec((rows, 2 * width), spot)
    one = pl.BlockSpec((rows, width), spot)
    gate = pl.BlockSpec((width, width), fixed)
    return pl.pallas_call(
        mixer_kernel,
        grid_spec=pltpu.PrefetchScalarGridSpec(
            num_scalar_prefetch=1,
            grid=(steps,),
            in_specs=[wide, pl.BlockSpec((rows, 8), inorder), pl.BlockSpec((8, width), fixed), gate, gate],
            out_specs=[one] * 5,
            scratch_shapes=[
                pltpu.VMEM((rows + 8, width), F32),
                pltpu.VMEM((rows, width), F32),
                pltpu.VMEM((rows, width), F32),
                pltpu.VMEM((8, width), F32),
            ],
        ),
        out_shape=[
            jax.ShapeDtypeStruct((count, width), kind) for kind in (BF16, F32, F32, F32, BF16)
        ],
        cost_estimate=pl.CostEstimate(
            flops=count * width * (4 * width + 120), bytes_accessed=count * width * 24, transcendentals=count * width * 6
        ),
        name="mixer",
    )(place, pre, masks, params, gate_a, gate_x)


def mixer_back(grad_proj, w_out, pre, states, recur, opened, conv, masks, params, gate_a, gate_x, place, rows):
    count, width = states.shape
    steps = count // rows
    last = steps - 1
    spot = lambda i, place: (place[last - i], 0)
    inorder = lambda i, place: (last - i, 0)
    fixed = lambda i, place: (0, 0)

    def tail(i, place):
        return (place[jnp.maximum(last - i - 1, 0)] * (rows // 8) + rows // 8 - 1, 0)

    wide = pl.BlockSpec((rows, 2 * width), spot)
    one = pl.BlockSpec((rows, width), spot)
    gate = pl.BlockSpec((width, width), fixed)
    return pl.pallas_call(
        mixer_back_kernel,
        grid_spec=pltpu.PrefetchScalarGridSpec(
            num_scalar_prefetch=1,
            grid=(steps,),
            in_specs=[
                pl.BlockSpec((rows, grad_proj.shape[1]), spot), pl.BlockSpec(w_out.shape, fixed),
                wide, pl.BlockSpec((8, 2 * width), tail), one, pl.BlockSpec((8, width), tail), one, one, one,
                pl.BlockSpec((rows, 8), inorder), pl.BlockSpec((8, width), fixed), gate, gate,
            ],
            out_specs=[wide, pl.BlockSpec((64, width), fixed), gate, gate],
            scratch_shapes=[
                pltpu.VMEM((rows + 8, width), F32),
                pltpu.VMEM((rows + 8, width), F32),
                pltpu.VMEM((rows + 8, width), F32),
                pltpu.VMEM((rows, width), F32),
                pltpu.VMEM((8, width), F32),
            ],
        ),
        out_shape=[
            jax.ShapeDtypeStruct((count, 2 * width), BF16),
            jax.ShapeDtypeStruct((64, width), F32),
            jax.ShapeDtypeStruct((width, width), F32),
            jax.ShapeDtypeStruct((width, width), F32),
        ],
        cost_estimate=pl.CostEstimate(
            flops=count * width * (8 * width + 2 * grad_proj.shape[1] + 200), bytes_accessed=count * width * 34, transcendentals=count * width * 4
        ),
        name="mixer_back",
    )(place, grad_proj, w_out, pre, pre, states, states, recur, opened, conv, masks, params, gate_a, gate_x)


def on_diagonal(blocks):
    heads, size = blocks.shape[0], blocks.shape[1]
    out = jnp.zeros((heads * size, heads * size), blocks.dtype)
    for h in range(heads):
        out = lax.dynamic_update_slice(out, blocks[h], (h * size, h * size))
    return out


def shards(
    tokens, segments, cotangent, gain_mix, w_branch, w_input, conv_weight, conv_bias, gate_a, bias_a, gate_x, bias_x,
    decay_param, w_out, gain_mlp, w_gate, w_up, w_down,
):
    half_at = lax.axis_index("ctx")
    place_tp = lax.axis_index("tp")

    def mine(x, axis):
        size = x.shape[axis] // 2
        return lax.dynamic_slice_in_dim(x, half_at * size, size, axis)

    def owned(x, axis):
        return lax.psum_scatter(x, "fsdp", scatter_dimension=axis, tiled=True)

    _, tok_count, model_width = tokens.shape
    rows = tok_count // 4
    length = 2 * tok_count
    own_in = jnp.concatenate([mine(w_branch, 1), mine(w_input, 1), mine(w_out, 0).T], axis=1)
    full_mix = lax.all_gather(own_in, "fsdp", axis=0, tiled=True)
    own_gu = jnp.concatenate([mine(w_gate, 1), mine(w_up, 1)], axis=1)
    full_gu = lax.all_gather(own_gu, "fsdp", axis=0, tiled=True)
    full_down = lax.all_gather(mine(w_down, 0), "fsdp", axis=1, tiled=True)

    width = own_in.shape[1] // 3
    full_in, full_out = full_mix[:, : 2 * width], full_mix[:, 2 * width :]
    units = own_gu.shape[1] // 2
    place = jnp.asarray(place_table())[half_at * 4 + place_tp]

    rate = -RATE_SCALE * jax.nn.softplus(-decay_param)
    params = jnp.concatenate(
        [
            mine(conv_weight, 1),
            jnp.stack([mine(v, 0) for v in (conv_bias, bias_a, bias_x, rate)]),
        ],
        axis=0,
    )
    heads_a, heads_x = mine(gate_a, 0), mine(gate_x, 0)
    head_count, head_width = heads_a.shape[0], heads_a.shape[1]
    diag_a, diag_x = on_diagonal(heads_a), on_diagonal(heads_x)
    seg = segments[0]
    around = jnp.pad(seg, (3, 3), constant_values=-1)
    marks = [around[3 - k : 3 - k + length] == seg for k in (1, 2, 3)]
    marks += [around[3 + k : 3 + k + length] == seg for k in (1, 2, 3)]
    marks += [jnp.zeros_like(marks[0])] * 2
    masks = jnp.stack(marks, axis=1).astype(F32)

    own = lax.dynamic_slice_in_dim(tokens[0], place_tp * rows, rows, 0)
    own_cot = lax.dynamic_slice_in_dim(cotangent[0], place_tp * rows, rows, 0)
    gain_mix, gain_mlp = gain_mix[None], gain_mlp[None]
    normed, cot = head(tokens[0], cotangent[0], gain_mix, 1)
    normed, cot = normed.reshape(length, model_width), cot.reshape(length, model_width)

    pre = matmul(normed, full_in)
    mixed, states, recur, opened, conv = mixer(pre, masks, params, diag_a, diag_x, place, rows)
    normed_mlp, resid = plane_sum("norm", True, [mixed], full_out, own, own, gain_mlp, 2, 9 << 33)
    normed_mlp = normed_mlp.reshape(length, model_width)

    both = matmul(normed_mlp, full_gu)
    gate_pre, up_pre = both[:, :units], both[:, units:]
    gate_act, gate_slope = gelu_parts(gate_pre)
    hidden = (gate_act * up_pre).astype(BF16)
    grad_w_down = left_inner(hidden, cot).astype(BF16)
    full_down, grad_w_down, hidden, full_in, own_cot = tied((full_down, grad_w_down, hidden, full_in, own_cot))
    own_down = owned(grad_w_down, 1)

    grad_hidden = right_inner(cot, full_down)
    grad_both = [(grad_hidden * up_pre * gate_slope).astype(BF16), (grad_hidden * gate_act).astype(BF16)]
    grad_both, hidden = tied((grad_both, hidden))
    half = length // 2
    sent = matmul(hidden[half:], full_down).astype(BF16)
    grad_both, sent = tied((grad_both, sent))
    grad_w_gu = left_inner(normed_mlp, jnp.concatenate(grad_both, axis=1)).astype(BF16)
    own_gu = owned(grad_w_gu, 0)
    got = exchange(sent, "core")
    grad_both, got, grad_w_gu = tied((grad_both, got, grad_w_gu))
    far_sent = (matmul(hidden[half // 2 : half], full_down) + got[half // 2 :].astype(F32)).astype(BF16)
    got_far = exchange(far_sent, "far")
    low = matmul(hidden[: half // 2], full_down) + got[: half // 2].astype(F32)
    grad_both, low, far_sent = tied((grad_both, low, far_sent))
    grad_proj, grad_resid, gain_mlp_part = plane_sum(
        "back", True, grad_both, full_gu, own_cot, resid, gain_mlp, 3, 9 << 33
    )
    grad_proj = grad_proj.reshape(length, model_width)
    grad_proj, got_far, low = tied((grad_proj, got_far, low))
    near_sent = (low[rows:] + got_far[rows:].astype(F32)).astype(BF16)
    got_near = exchange(near_sent, "near")

    grad_w_out = left_inner(mixed, grad_proj).astype(BF16)
    grad_proj, own_down, grad_w_out = tied((grad_proj, own_down, grad_w_out))
    own_out = owned(grad_w_out, 1)
    other_down = flip(own_down, 4)
    low, grad_w_out = tied((low, grad_w_out))
    output = (resid + low[:rows] + got_far[:rows].astype(F32) + got_near.astype(F32)).astype(BF16)
    output, own_gu = tied((output, own_gu))
    other_gu = flip(own_gu, 4)
    states, output = tied((states, output))
    output_along = flip(output, 2)
    grads_in, sums, sum_a, sum_x = mixer_back(
        grad_proj, full_out, pre, states, recur, opened, conv, masks, params, diag_a, diag_x, place, rows
    )
    grads_in, output_along, other_down = tied((grads_in, output_along, other_down))
    lines = jnp.sum(sums.reshape(8, 8, width), axis=1)
    head_at = lax.broadcasted_iota(jnp.int32, (head_width, width), 1) // head_width
    squares = [
        sum(
            jnp.where(head_at == h, part[h * head_width : (h + 1) * head_width], 0.0) for h in range(head_count)
        )
        for part in (sum_a, sum_x)
    ]
    fsdp_size = lax.axis_size("fsdp")
    part_rows = 16 * -(-(8 + 2 * head_width) // (16 * fsdp_size))
    spare = fsdp_size * part_rows - 8 - 2 * head_width
    small = jnp.concatenate([lines] + squares + [jnp.zeros((spare, width), F32)], axis=0).astype(BF16)
    small = small.reshape(fsdp_size, 2, part_rows // 2, width)
    small = jnp.concatenate([small[:, 0], small[:, 1]], axis=2)
    grad_w_in = left_inner(normed, grads_in).astype(BF16).reshape(fsdp_size, -1, 2 * width)
    grad_w_in = jnp.concatenate([grad_w_in, small], axis=1).reshape(-1, 2 * width)
    grads_in, grad_w_in, own_out, other_gu = tied((grads_in, grad_w_in, own_out, other_gu))
    own_in = owned(grad_w_in, 0)
    moved = (output, output_along, own_gu, other_gu, own_down, other_down, own_out)
    grad_tokens, gain_mix_part, output, own_gate, own_up, own_down, own_out = plane_sum(
        "back", False, [grads_in], full_in, grad_resid, own, gain_mix, 4, 5 << 33, moved
    )
    other_in, smalls, gains, grad_tokens = last(
        own_in, gain_mix_part, gain_mlp_part, grad_tokens, model_width // fsdp_size, fsdp_size, 5
    )

    def both_halves(x, other, axis):
        low = jnp.where(half_at == 0, x, other)
        high = jnp.where(half_at == 0, other, x)
        return jnp.concatenate([low, high], axis=axis).astype(F32)

    own_in = own_in[: model_width // fsdp_size]
    smalls = jnp.stack([smalls[..., :width], smalls[..., width:]], axis=2).reshape(2, fsdp_size * part_rows, width)
    smalls = jnp.concatenate([smalls[0], smalls[1]], axis=1).astype(F32)
    lines = smalls[:8]
    squares = []
    for i in range(2):
        part = smalls[8 + i * head_width : 8 + (i + 1) * head_width]
        squares.append(
            jnp.stack([part[:, h * head_width : (h + 1) * head_width] for h in range(2 * head_count)])
        )
    own_branch = both_halves(own_in[:, :width], other_in[:, :width], 1)
    own_input = both_halves(own_in[:, width:], other_in[:, width:], 1)
    return (
        output.reshape(1, tok_count, model_width),
        grad_tokens.reshape(1, tok_count, model_width),
        gains[:4].reshape(model_width),
        own_branch,
        own_input,
        lines[4:8],
        lines[3],
        squares[0],
        lines[1],
        squares[1],
        lines[2],
        RATE_SCALE * jax.nn.sigmoid(-decay_param) * lines[0],
        own_out.astype(F32),
        gains[4:].reshape(model_width),
        own_gate.astype(F32),
        own_up.astype(F32),
        own_down.astype(F32),
    )


def solution(mesh):
    in_specs = (
        P("fsdp", "ctx", None),
        P("fsdp", None),
        P("fsdp", "ctx", None),
        P(),
        P("fsdp", "tp"),
        P("fsdp", "tp"),
        P(None, "tp"),
        P("tp"),
        P("tp", None, None),
        P("tp"),
        P("tp", None, None),
        P("tp"),
        P("tp"),
        P("tp", "fsdp"),
        P(),
        P("fsdp", "tp"),
        P("fsdp", "tp"),
        P("tp", "fsdp"),
    )
    out_specs = (
        P("fsdp", "ctx", None),
        P("fsdp", "ctx", None),
        P(),
        P("fsdp", "tp"),
        P("fsdp", "tp"),
        P(None, "tp"),
        P("tp"),
        P("tp", None, None),
        P("tp"),
        P("tp", None, None),
        P("tp"),
        P("tp"),
        P("tp", "fsdp"),
        P(),
        P("fsdp", "tp"),
        P("fsdp", "tp"),
        P("tp", "fsdp"),
    )
    return jax.shard_map(shards, mesh=mesh, in_specs=in_specs, out_specs=out_specs, check_vma=False)
```
